32 devices in a mesh: rep: 2 (over x), ga: 16 (over z, y, core).
Axes of the slice: x: 2, y: 2, z: 4, core: 2. Of those that a mesh axis runs over, the one named last changes fastest.
Arguments:
- positions: float32 [64, 3, 768], P('rep', None, 'ga'), parts along dimension 0, may hold values from -3 to 23, as said below
- weights: int32 [1, 32], replicated, may hold values from 1 to 16
- psi: bfloat16 [2, 512, 2, 32768], P('rep', None, None, 'ga'), parts along dimension 0, may hold values from -5 to 5
- vloc: float32 [2, 32768], P('rep'), parts along dimension 0, may hold values from -8 to 8
Outputs:
- psi_new: bfloat16 [2, 512, 2, 32768], P('rep', None, None, 'ga'), parts along dimension 0
- bead_forces: float32 [64, 3, 768], P('rep', None, 'ga'), parts along dimension 0
The draws below stay inside these ranges and needn't reach their ends.
There are 2 independent parts, one for each index of `rep`. The reference program is written for one: setup_inputs(seed, part) draws one part's arguments, and reference() takes and returns one part's arrays. A program takes and returns all parts, laid end to end along the dimension named above; an argument that names none is the same for every part. Nothing has to cross between parts.
Inputs may be any that keep to these rules, and one draw needn't show every extreme that they name: `positions`: atom 3w is the oxygen of water w and atoms 3w+1 and 3w+2 are its hydrogens; in every bead each hydrogen lies between 1.0 and 2.6 from its oxygen.
All inputs are finite; a program needn't handle non-finite values.
Results may differ from the reference program's by a relative error of at most 0.0037.
The reference program's roundings to bfloat16 on the way (of `table`, `projections`, `trial` and `mixer`) count: a program that leaves them out, or rounds other values in their place, can miss the bound.
Values may be sent and summed in bfloat16 or wider, within the bound.
A program may use at most 192 MiB of HBM per device.

```python
import jax
import jax.numpy as jnp
from jax import lax

BEADS = 32
CBEADS = 1
WATERS = 256
ATOMS = 768
BANDS = 512
NGRID = 32
GVECS = 32768


def draw_positions(key, part):
    subkeys = jax.random.split(jax.random.fold_in(key, 7), 5)
    oxygen = jax.random.uniform(subkeys[0], (3, WATERS), jnp.float32, 0.0, 20.0)
    first_dir = jax.random.normal(subkeys[1], (3, WATERS), jnp.float32)
    second_dir = jax.random.normal(subkeys[2], (3, WATERS), jnp.float32)
    first_dir = first_dir / jnp.sqrt(jnp.sum(first_dir * first_dir, axis=0, keepdims=True) + 1e-06)
    second_dir = second_dir / jnp.sqrt(jnp.sum(second_dir * second_dir, axis=0, keepdims=True) + 1e-06)
    lengths = jax.random.uniform(subkeys[3], (2, WATERS), jnp.float32, 1.5, 2.1)
    centroid = jnp.stack([oxygen, oxygen + lengths[0] * first_dir, oxygen + lengths[1] * second_dir], axis=2).reshape(3, ATOMS)
    spread = jax.random.uniform(subkeys[4], (BEADS, 3, ATOMS), jnp.float32, -0.12, 0.12)
    return centroid[None] + spread


def with_ends(array, stream_key, least, top_value):
    spot = [jax.random.randint(jax.random.fold_in(stream_key, axis), (), 0, length) for axis, length in enumerate(array.shape)]
    longest = array.shape.index(max(array.shape))
    next_to = spot[:longest] + [(spot[longest] + 1) % array.shape[longest]] + spot[longest + 1:]
    return array.at[tuple(spot)].set(least).at[tuple(next_to)].set(top_value)


def block_scale(rng, dims, pieces, low, top_value):
    loudness, own = 1.0, jax.random.fold_in(rng, 6)
    for axis_at, parts in pieces:
        steps = jnp.exp(jax.random.uniform(jax.random.fold_in(own, axis_at), (parts,), jnp.float32, low / len(pieces), top_value / len(pieces)))
        loudness = loudness * jnp.repeat(steps, dims[axis_at] // parts).reshape([-1 if axis == axis_at else 1 for axis in range(len(dims))])
    return loudness


def bell_draw(stream_key, extent, scale, most, shards=(), kind=jnp.bfloat16):
    entries = jax.random.normal(stream_key, extent, jnp.float32) * scale
    if len(shards) > 0:
        entries = block_scale(stream_key, extent, shards, -0.22, 0.18) * entries
    return jnp.clip(entries, min=-most, max=most).astype(kind)


def setup_inputs(seed: int = 0, part: int = 0) -> dict:
    streams_of = jax.random.split(jax.random.key(seed), 5)
    part_splits = jax.random.split(jax.random.fold_in(streams_of[4], part), 5)
    positions = draw_positions(jax.random.fold_in(jax.random.fold_in(streams_of[4], part), 71), part)
    weights = with_ends(jax.random.randint(streams_of[1], (CBEADS, BEADS), 1, 17), jax.random.fold_in(streams_of[1], 1), 1, 16).astype(jnp.int32)
    psi = bell_draw(part_splits[2], (CBEADS, BANDS, 2, GVECS), 0.7071, 5.0, ((3, 16),))
    vloc = jnp.clip(jax.random.uniform(part_splits[3], (CBEADS, GVECS), jnp.float32, -8.0, 8.0), -8.0, 8.0)
    return {"positions": positions, "weights": weights, "psi": psi, "vloc": vloc}


box_length = 20.0
bond_stiff = 0.5
bond_rest = 1.8
spring_stiff = 2.0
width_square = 0.09
step_size = 0.02
nonlocal_strength = 250.0
occupation = 2.0
highest = lax.Precision.HIGHEST

def frequency(index, count):
    signed = jnp.where(index < count // 2, index, index - count)
    return signed.astype(jnp.float32) * (2.0 * jnp.pi / box_length)

def field_forces(positions):
    oxygen = positions[:, :, 0::3]
    toward_one = positions[:, :, 1::3] - oxygen
    toward_two = positions[:, :, 2::3] - oxygen

    def stretch(offset):
        length = jnp.sqrt(lax.optimization_barrier(jnp.sum(offset * offset, axis=1, keepdims=True)))
        return -bond_stiff * (length - bond_rest) * offset / length
    pull_one = stretch(toward_one)
    pull_two = stretch(toward_two)
    bonds = jnp.stack([-(pull_one + pull_two), pull_one, pull_two], axis=3).reshape(positions.shape)
    springs = 2.0 * positions - jnp.roll(positions, 1, axis=0) - jnp.roll(positions, -1, axis=0)
    return bonds - spring_stiff * springs

def inner(left_mat, right_mat):
    return lax.dot_general(left_mat, right_mat, (((1,), (1,)), ((), ())), preferred_element_type=jnp.float32)

def reference(positions, weights, psi, vloc):
    near_forces = field_forces(positions)
    weight_float = weights.astype(jnp.float32)
    mixing = weight_float / lax.optimization_barrier(jnp.sum(weight_float, axis=1, keepdims=True))
    centres = jnp.einsum('cj,jan->can', mixing, positions, precision=highest)
    flat_index = jnp.arange(GVECS, dtype=jnp.int32)
    gvectors = jnp.stack([frequency(flat_index // (NGRID * NGRID), NGRID), frequency(flat_index // NGRID % NGRID, NGRID), frequency(flat_index % NGRID, NGRID)])
    square = lax.optimization_barrier(jnp.sum(gvectors * gvectors, axis=0))
    profile = jnp.exp(-0.5 * width_square * square)
    kinetic = 0.5 * square
    new_waves = []
    dft_forces = []
    for contracted in range(CBEADS):
        oxygens = centres[contracted][:, 0::3]
        phases = jnp.einsum('ai,ag->ig', oxygens, gvectors, precision=highest)
        wave_cos = profile * jnp.cos(phases)
        wave_sin = profile * jnp.sin(phases)
        table = jnp.concatenate([jnp.concatenate([wave_cos, -wave_sin], 1), jnp.concatenate([wave_sin, wave_cos], 1)], 0).astype(jnp.bfloat16)
        wavefunc = psi[contracted].reshape(BANDS, 2 * GVECS)
        real_part = wavefunc[:, :GVECS]
        imag_part = wavefunc[:, GVECS:]
        projections = (inner(table, wavefunc) * (1.0 / GVECS)).astype(jnp.bfloat16)
        nonlocal_term = lax.dot_general(projections, table, (((0,), (0,)), ((), ())), preferred_element_type=jnp.float32)
        paired = jnp.concatenate([wavefunc, jnp.concatenate([imag_part, -real_part], 1)], 0)
        side_by_side = jnp.concatenate([projections[:WATERS], projections[WATERS:]], 1)
        weighted = jnp.dot(side_by_side, paired, preferred_element_type=jnp.float32)
        mixed_wave = wave_cos * weighted[:, GVECS:] + wave_sin * weighted[:, :GVECS]
        oxygen_force = 2.0 * occupation * nonlocal_strength / GVECS * jnp.einsum('ag,ig->ai', gvectors, mixed_wave, precision=highest)
        hydrogen_zero = jnp.zeros_like(oxygen_force)
        dft_forces.append(jnp.stack([oxygen_force, hydrogen_zero, hydrogen_zero], axis=2).reshape(3, ATOMS))
        grid_potential = vloc[contracted].reshape(NGRID, NGRID, NGRID)

        def apply_block(band_block):
            complex_wave = (band_block[:, 0].astype(jnp.float32) + 1j * band_block[:, 1].astype(jnp.float32)).reshape(-1, NGRID, NGRID, NGRID)
            spread = jnp.fft.fftn(grid_potential * jnp.fft.ifftn(complex_wave, axes=(1, 2, 3)), axes=(1, 2, 3)).reshape(-1, GVECS)
            return jnp.stack([jnp.real(spread), jnp.imag(spread)], axis=1).astype(jnp.float32)
        blocks = min(64, BANDS)
        potential_term = lax.map(apply_block, psi[contracted].reshape(BANDS // blocks, blocks, 2, GVECS)).reshape(BANDS, 2, GVECS)
        wave_float = psi[contracted].astype(jnp.float32)
        hamil_re = kinetic * wave_float[:, 0] + potential_term[:, 0] + nonlocal_strength * nonlocal_term[:, :GVECS]
        hamil_im = kinetic * wave_float[:, 1] + potential_term[:, 1] + nonlocal_strength * nonlocal_term[:, GVECS:]
        trial = jnp.concatenate([wave_float[:, 0] - step_size * hamil_re, wave_float[:, 1] - step_size * hamil_im], 1).astype(jnp.bfloat16)
        rotated = jnp.concatenate([trial, jnp.concatenate([-trial[:, GVECS:], trial[:, :GVECS]], 1)], 0)
        margin = inner(trial, rotated) * (1.0 / GVECS)
        identity_rows = jnp.concatenate([jnp.eye(BANDS, dtype=jnp.float32), jnp.zeros((BANDS, BANDS), jnp.float32)], 1)
        mixer = (1.5 * identity_rows - 0.5 * margin).astype(jnp.bfloat16)
        updated = jnp.dot(mixer, rotated, preferred_element_type=jnp.float32).astype(jnp.bfloat16)
        new_waves.append(updated.reshape(BANDS, 2, GVECS))
    contracted_force = jnp.einsum('cj,can->jan', mixing, jnp.stack(dft_forces), precision=highest)
    bead_forces = near_forces + BEADS / CBEADS * contracted_force
    return (jnp.stack(new_waves), bead_forces)
```

```python
import functools

import jax
import jax.numpy as jnp
import numpy as np
from jax import lax
from jax.experimental import pallas as pl
from jax.experimental.pallas import tpu as pltpu
from jax.sharding import PartitionSpec as P

BEADS = 32
CBEADS = 1
WATERS = 256
NGRID = 32
GVECS = 32768
CHUNKS = 2


box_length = 20.0
bond_stiff = 0.5
bond_rest = 1.8
spring_stiff = 2.0
width_square = 0.09
step_size = 0.02
nonlocal_strength = 250.0
occupation = 2.0
highest = lax.Precision.HIGHEST


def frequency(index, count):
    signed = jnp.where(index < count // 2, index, index - count)
    return signed.astype(jnp.float32) * (2.0 * jnp.pi / box_length)


def field_forces(positions):
    oxygen = positions[:, :, 0::3]
    toward_one = positions[:, :, 1::3] - oxygen
    toward_two = positions[:, :, 2::3] - oxygen

    def stretch(offset):
        length = jnp.sqrt(jnp.sum(offset * offset, axis=1, keepdims=True))
        return -bond_stiff * (length - bond_rest) * offset / length

    pull_one = stretch(toward_one)
    pull_two = stretch(toward_two)
    bonds = jnp.stack([-(pull_one + pull_two), pull_one, pull_two], axis=3).reshape(positions.shape)
    springs = 2.0 * positions - jnp.roll(positions, 1, axis=0) - jnp.roll(positions, -1, axis=0)
    return bonds - spring_stiff * springs


def inner(left_mat, right_mat):
    return lax.dot_general(
        left_mat, right_mat, (((1,), (1,)), ((), ())), preferred_element_type=jnp.float32
    )


def real_form(freq_index, group_index):
    product = freq_index[:, None] * freq_index[None, :] % NGRID
    angle = product.astype(jnp.float32) * (2.0 * jnp.pi / NGRID)
    same = (group_index[:, None] == group_index[None, :]).astype(jnp.float32)
    cosines = jnp.cos(angle) * same
    sines = jnp.sin(angle) * same
    return jnp.stack([jnp.stack([cosines, sines], 1), jnp.stack([-sines, cosines], 1)], 0)


def plane_table():
    index = jnp.arange(NGRID, dtype=jnp.int32)
    return real_form(index, jnp.zeros_like(index))


def block_table(length, within):
    index = jnp.arange(length, dtype=jnp.int32)
    if within:
        return real_form(index % NGRID, index // NGRID)
    return real_form(index // NGRID, index % NGRID)


def grid_sum(psi, vloc, parts):
    bands = psi.shape[1]
    local_g = psi.shape[3]
    x_table = plane_table()
    z_table = block_table(local_g, True)
    y_table = block_table(NGRID * NGRID, False)
    grid_potential = vloc[0].reshape(1, 1, NGRID, NGRID * NGRID)
    grouped_raw = psi[0].reshape(parts, bands // parts, 2, local_g)
    planes = lax.all_to_all(grouped_raw, "ga", split_axis=0, concat_axis=3, tiled=True)
    band_count = planes.shape[1]
    blocks_whole = planes.astype(jnp.float32).reshape(band_count, 2, NGRID**3 // local_g, local_g)
    along_z = jnp.einsum("mckp,cpdq->mdkq", blocks_whole, z_table, precision=highest) * (
        1.0 / NGRID
    )
    grid = along_z.reshape(band_count, 2, NGRID, NGRID * NGRID)
    grid = jnp.einsum("mcxr,cxdw->mdwr", grid, x_table, precision=highest) * (1.0 / NGRID)
    grid = jnp.einsum("mcxp,cpdq->mdxq", grid, y_table, precision=highest) * (1.0 / NGRID)
    grid = grid * grid_potential
    grid = jnp.einsum("mdxq,cpdq->mcxp", grid, y_table, precision=highest)
    grid = jnp.einsum("mdwr,cxdw->mcxr", grid, x_table, precision=highest)
    returning = grid.reshape(1, band_count, 2, NGRID**3)
    returned = lax.all_to_all(
        returning.astype(jnp.bfloat16), "ga", split_axis=3, concat_axis=0, tiled=True
    ).astype(returning.dtype)
    returned = returned.reshape(bands, 2, local_g)
    potential = jnp.einsum("bdq,cpdq->bcp", returned, z_table, precision=highest)
    return potential[:, 0], potential[:, 1]


def plane_rotation():
    small = np.arange(NGRID)
    angle = small[:, None] * small[None, :] % NGRID * (2.0 * np.pi / NGRID)
    side = NGRID * NGRID
    wave = np.kron(np.exp(1j * angle), np.exp(1j * angle))
    real, imag = np.real(wave), np.imag(wave)
    table = np.stack([np.stack([real, -imag], 1), np.stack([imag, real], 1)], 1)
    return jnp.asarray(table.reshape(2 * side, 2 * side).astype(np.float32), jnp.bfloat16)


def line_rotation(group):
    small = np.arange(NGRID)
    angle = small[:, None] * small[None, :] % NGRID * (2.0 * np.pi / NGRID)
    real, imag = np.cos(angle), np.sin(angle)
    form = np.stack([np.stack([real, -imag], 2), np.stack([imag, real], 2)], 1)
    same = np.eye(group)
    table = form[:, None, :, :, None, :] * same[None, :, None, None, :, None]
    size = 2 * NGRID * group
    return jnp.asarray(table.reshape(size, size).astype(np.float32), jnp.bfloat16)


def plane_out(psi, parts, plane_table, offset):
    bands = psi.shape[1]
    side = NGRID * NGRID
    planes = psi.shape[3] // side
    chunk = bands // CHUNKS
    pieces = []
    for first in range(0, bands, chunk):
        part = lax.dynamic_slice_in_dim(psi[0], first + offset, chunk, axis=0).reshape(chunk, 2, planes, side)
        part = part.transpose(2, 0, 1, 3).reshape(planes, chunk, 2 * side)
        pieces.append(
            jnp.stack(
                [
                    jnp.einsum(
                        "qk,bk->qb", plane_table, part[p], preferred_element_type=jnp.float32
                    )
                    .astype(jnp.bfloat16)
                    .reshape(parts, 2 * side // parts, chunk)
                    for p in range(planes)
                ],
                1,
            )
        )
    return pieces


def exchange(piece):
    return lax.all_to_all(piece, "ga", split_axis=0, concat_axis=0, tiled=True)


def line_action(vloc, parts):
    side = NGRID * NGRID
    points = side // parts
    group = min(8, points)
    groups = points // group
    line_table = line_rotation(group)
    start = lax.axis_index("ga") * points
    own = lax.dynamic_slice_in_dim(vloc[0].reshape(NGRID, side), start, points, axis=1)
    own = own.reshape(NGRID, groups, group).transpose(1, 0, 2) * (1.0 / (NGRID * side))
    own = jnp.broadcast_to(own[..., None], (groups, NGRID, group, 2)).reshape(groups, -1, 1)
    scaled = (own * line_table.astype(jnp.float32)).astype(jnp.bfloat16)
    return jnp.einsum(
        "ea,gec->gac", line_table, scaled, preferred_element_type=jnp.float32
    ).astype(jnp.bfloat16)


def line_step(action, lines):
    parts, planes, rows, chunk = lines.shape
    groups = action.shape[0]
    lines = lines.reshape(parts * planes, groups, rows // groups, chunk)
    lines = lines.transpose(1, 0, 2, 3).reshape(groups, -1, chunk)
    lines = jnp.einsum(
        "gac,gcb->gab", action, lines, preferred_element_type=jnp.float32
    ).astype(jnp.bfloat16)
    lines = lines.reshape(groups, parts * planes, rows // groups, chunk).transpose(1, 0, 2, 3)
    return lines.reshape(parts, planes, rows, chunk)


def plane_back(backs, plane_table):
    side = NGRID * NGRID
    reals, imags = [], []
    for back in backs:
        chunk = back.shape[3]
        whole = [
            jnp.einsum(
                "qb,qk->bk",
                back[:, p].reshape(2 * side, chunk),
                plane_table,
                preferred_element_type=jnp.float32,
            )
            for p in range(back.shape[1])
        ]
        reals.append(jnp.concatenate([w[:, :side] for w in whole], 1))
        imags.append(jnp.concatenate([w[:, side:] for w in whole], 1))
    return jnp.concatenate(reals, 0), jnp.concatenate(imags, 0)


def waves(oxygens, gvectors, profile):
    local_g = profile.shape[0]
    side = NGRID * NGRID
    if local_g % side:
        phases = jnp.einsum("ai,ag->ig", oxygens, gvectors, precision=highest)
        return profile * jnp.cos(phases), profile * jnp.sin(phases)
    spots = oxygens.T
    flat = spots[:, 1:2] * gvectors[1:2, :side] + spots[:, 2:3] * gvectors[2:3, :side]
    flat_cos, flat_sin = jnp.cos(flat), jnp.sin(flat)
    along = spots[:, 0:1] * gvectors[0:1, ::side]
    along_cos, along_sin = jnp.cos(along), jnp.sin(along)
    cosines, sines = [], []
    for p in range(local_g // side):
        c, s = along_cos[:, p : p + 1], along_sin[:, p : p + 1]
        cosines.append(c * flat_cos - s * flat_sin)
        sines.append(s * flat_cos + c * flat_sin)
    return profile * jnp.concatenate(cosines, 1), profile * jnp.concatenate(sines, 1)


def per_device(positions, weights, psi, vloc):
    near_forces = field_forces(positions)
    weight_float = weights.astype(jnp.float32)
    mixing = weight_float / jnp.sum(weight_float, axis=1, keepdims=True)
    centres = jnp.einsum("cj,jan->can", mixing, positions, precision=highest)
    parts = lax.axis_size("ga")
    near_oxygen = centres[0][:, 0::3]
    own_waters = near_oxygen.shape[1]
    everyone = lax.dynamic_update_slice(
        jnp.zeros((3, own_waters * parts), jnp.float32),
        near_oxygen,
        (0, lax.axis_index("ga") * own_waters),
    )
    oxygens = lax.psum(everyone, "ga")
    side = NGRID * NGRID
    whole_planes = psi.shape[3] % side == 0 and side % parts == 0
    if whole_planes:
        plane_table = plane_rotation()
        pieces = plane_out(psi, parts, plane_table, (oxygens[0, 0] * 0.0).astype(jnp.int32))
        lines = [exchange(piece) for piece in pieces]
        action = line_action(vloc, parts)
    bands = psi.shape[1]
    local_g = psi.shape[3]
    flat_index = lax.axis_index("ga") * local_g + jnp.arange(local_g, dtype=jnp.int32)
    gvectors = jnp.stack(
        [
            frequency(flat_index // (NGRID * NGRID), NGRID),
            frequency(flat_index // NGRID % NGRID, NGRID),
            frequency(flat_index % NGRID, NGRID),
        ]
    )
    square = jnp.sum(gvectors * gvectors, axis=0)
    profile = jnp.exp(-0.5 * width_square * square)
    kinetic = 0.5 * square
    wave_cos, wave_sin = waves(oxygens, gvectors, profile)
    table = jnp.concatenate(
        [jnp.concatenate([wave_cos, -wave_sin], 1), jnp.concatenate([wave_sin, wave_cos], 1)], 0
    ).astype(jnp.bfloat16)
    wavefunc = psi[0].reshape(bands, 2 * local_g)
    partial_proj = (inner(table, wavefunc) * (1.0 / GVECS)).reshape(2, WATERS, bands)
    share = lax.psum_scatter(partial_proj, "ga", scatter_dimension=1, tiled=True).astype(
        jnp.bfloat16
    )
    table_blocks = table.reshape(2 * WATERS, 2 * local_g)
    copies = jnp.broadcast_to(share[None], (parts,) + share.shape)
    if whole_planes:
        lines[-1], copies = lax.optimization_barrier((lines[-1], copies))
    all_proj = lax.all_to_all(copies, "ga", split_axis=0, concat_axis=0, tiled=True)
    if whole_planes:
        moved = [line_step(action, line) for line in lines]
        moved[0], all_proj = lax.optimization_barrier((moved[0], all_proj))
        backs = [exchange(piece) for piece in moved]
    all_proj = all_proj.transpose(1, 0, 2, 3).reshape(2 * WATERS, bands)
    nonlocal_term = jnp.einsum(
        "ib,ig->bg", all_proj, table_blocks, preferred_element_type=jnp.float32
    )
    crossed = jnp.dot(all_proj, wavefunc, preferred_element_type=jnp.float32)
    weighted_re = crossed[:WATERS, :local_g] + crossed[WATERS:, local_g:]
    weighted_im = crossed[:WATERS, local_g:] - crossed[WATERS:, :local_g]
    mixed_wave = wave_cos * weighted_im + wave_sin * weighted_re
    force_part = (
        2.0
        * occupation
        * nonlocal_strength
        / GVECS
        * jnp.einsum("ag,ig->ai", gvectors, mixed_wave, precision=highest)
    )
    force_rows = force_part.reshape(3, parts, own_waters).transpose(1, 0, 2)
    force_rows = force_rows.reshape(parts, 1, 3 * own_waters)
    force_rows = jnp.pad(force_rows, ((0, 0), (0, 0), (0, bands - 3 * own_waters)))
    wave_float = psi[0].astype(jnp.float32)
    if whole_planes:
        potential = plane_back(backs, plane_table)
    else:
        potential = grid_sum(psi, vloc, parts)
    hamil_re = (
        kinetic * wave_float[:, 0]
        + potential[0]
        + nonlocal_strength * nonlocal_term[:, :local_g]
    )
    hamil_im = (
        kinetic * wave_float[:, 1]
        + potential[1]
        + nonlocal_strength * nonlocal_term[:, local_g:]
    )
    trial_re = (wave_float[:, 0] - step_size * hamil_re).astype(jnp.bfloat16)
    trial_im = (wave_float[:, 1] - step_size * hamil_im).astype(jnp.bfloat16)
    row = lax.broadcasted_iota(jnp.int32, (bands, bands), 0)
    column = lax.broadcasted_iota(jnp.int32, (bands, bands), 1)
    even = inner(trial_re, trial_re) + inner(trial_im, trial_im)
    odd = inner(trial_im, trial_re) - inner(trial_re, trial_im)
    packed = jnp.where(row <= column, even, odd) * (1.0 / GVECS)
    shares = lax.all_to_all(
        jnp.concatenate([packed.reshape(parts, bands // parts, bands), force_rows], 1),
        "ga",
        split_axis=0,
        concat_axis=0,
        tiled=True,
    )
    sums = jnp.sum(shares, axis=0)
    oxygen_force = sums[-1, : 3 * own_waters].reshape(3, own_waters)
    hydrogen_zero = jnp.zeros_like(oxygen_force)
    dft_forces = [jnp.stack([oxygen_force, hydrogen_zero, hydrogen_zero], axis=2).reshape(3, -1)]
    own_rows = lax.broadcasted_iota(jnp.int32, (bands // parts, bands), 0) + lax.axis_index(
        "ga"
    ) * (bands // parts)
    own_columns = lax.broadcasted_iota(jnp.int32, (bands // parts, bands), 1)
    mixed_rows = jnp.where(own_rows == own_columns, 1.5, 0.0) - 0.5 * sums[:-1]
    mixed = lax.all_gather(mixed_rows.astype(jnp.bfloat16), "ga", axis=0, tiled=True)
    turned = mixed.T
    mix_re = jnp.where(row <= column, mixed, turned)
    mix_im = jnp.where(row > column, mixed, jnp.where(row < column, -turned, jnp.zeros_like(turned)))
    both = jnp.concatenate([trial_re, trial_im], 0)
    new_re = jnp.dot(
        jnp.concatenate([mix_re, -mix_im], 1), both, preferred_element_type=jnp.float32
    ).astype(jnp.bfloat16)
    new_im = jnp.dot(
        jnp.concatenate([mix_im, mix_re], 1), both, preferred_element_type=jnp.float32
    ).astype(jnp.bfloat16)
    new_waves = [jnp.stack([new_re, new_im], 1)]
    contracted_force = jnp.einsum("cj,can->jan", mixing, jnp.stack(dft_forces), precision=highest)
    bead_forces = near_forces + BEADS / CBEADS * contracted_force
    return (jnp.stack(new_waves), bead_forces)


def product(left_mat, right_mat):
    return jnp.dot(left_mat, right_mat, preferred_element_type=jnp.float32)


def trig_tables():
    small = np.arange(NGRID)
    angle = small[:, None] * small[None, :] % NGRID * (2.0 * np.pi / NGRID)
    cosines, sines = np.cos(angle), np.sin(angle)
    rows = [np.repeat(cosines, NGRID, 1), np.repeat(sines, NGRID, 1)]
    rows += [np.tile(cosines, (1, NGRID)), np.tile(sines, (1, NGRID))]
    return jnp.asarray(np.stack(rows), jnp.float32)


def cross_tables(parts, planes, share):
    spot = (np.arange(parts)[None, :] * planes + np.arange(planes)[:, None]).reshape(-1)
    angle = spot[:, None] * spot[None, :] % NGRID * (2.0 * np.pi / NGRID)
    same = np.eye(share)
    pair = np.stack([np.kron(np.cos(angle), same), np.kron(np.sin(angle), same)])
    return jnp.asarray(pair.astype(np.float32), jnp.bfloat16)


def step_kernel(
    sizes,
    psi_hbm,
    own_waves,
    grid,
    trig,
    cross,
    vloc,
    trial_hbm,
    mixed_out,
    force_out,
    psi,
    all_waves,
    table_cos,
    table_sin,
    wave_cos,
    wave_sin,
    plane_cos,
    plane_sin,
    potential,
    got,
    middle,
    giving,
    back,
    base,
    trial,
    partial,
    landing,
    gathered,
    turned,
    margin,
    landing_two,
    gathered_two,
    force_sum,
    force_land,
    grid_rows,
    local_sem,
    wave_sems,
    out_sems,
    back_sems,
    force_sems,
    sum_sems,
    share_sems,
):
    parts, bands, local_g = sizes
    side = NGRID * NGRID
    planes = local_g // side
    share = bands // (parts * CHUNKS)
    block = parts * share
    steps = parts.bit_length() - 1
    tile = 256
    me = lax.axis_index("ga")

    def other(turn):
        total = 0
        for bit in range(steps):
            size = 1 << bit
            total = total + (me // size + turn // size) % 2 * size
        return total

    def remote(source, target, sems, peer):
        return pltpu.make_async_remote_copy(
            src_ref=source,
            dst_ref=target,
            send_sem=sems[0],
            recv_sem=sems[1],
            device_id={"ga": peer},
            device_id_type=pl.DeviceIdType.MESH,
        )

    def each_peer(act):
        def body(turn, carry):
            act(turn)
            return carry

        lax.fori_loop(1, parts, body, 0)

    def pair(sems, *spot):
        return sems.at[(0,) + spot], sems.at[(1,) + spot]

    def wave_copy(turn):
        waters = own_waves.shape[0]
        spot = pl.ds(pl.multiple_of(me * waters, waters), waters)
        return remote(own_waves, all_waves.at[spot], pair(wave_sems, turn), other(turn))

    def out_copy(chunk, turn):
        peer = other(turn)
        source = pl.ds(pl.multiple_of(chunk * block + peer * share, share), share)
        target = pl.ds(pl.multiple_of(me * share, share), share)
        return remote(
            psi_hbm.at[source], got.at[chunk, target], pair(out_sems, chunk, turn), peer
        )

    def back_copy(chunk, turn):
        peer = other(turn)
        source = pl.ds(pl.multiple_of(peer * share, share), share)
        target = pl.ds(pl.multiple_of(chunk * block + me * share, share), share)
        return remote(
            giving.at[chunk, source], back.at[target], pair(back_sems, chunk, turn), peer
        )

    def force_copy(turn):
        peer = other(turn)
        waters = own_waves.shape[0]
        source = pl.ds(pl.multiple_of(peer * waters, waters), waters)
        return remote(
            force_sum.at[source], force_land.at[me], pair(force_sems, turn), peer
        )

    local_psi = pltpu.make_async_copy(psi_hbm, psi, local_sem.at[0])
    local_psi.start()
    barrier = pltpu.get_barrier_semaphore()

    def greet(turn):
        pl.semaphore_signal(
            barrier, inc=1, device_id={"ga": other(turn)}, device_id_type=pl.DeviceIdType.MESH
        )

    each_peer(greet)
    pl.semaphore_wait(barrier, parts - 1)

    units = [(chunk, far) for chunk in range(CHUNKS) for far in range(parts // 2)]
    queue = list(units)

    def issue(count):
        for _ in range(count):
            if queue:
                chunk, far = queue.pop(0)
                out_copy(chunk, parts // 2 + far).start()
                if far > 0:
                    out_copy(chunk, far).start()

    each_peer(lambda turn: wave_copy(turn).start())
    issue(2)

    waters = own_waves.shape[0]
    own_spot = pl.ds(pl.multiple_of(me * waters, waters), waters)
    all_waves[own_spot, :] = own_waves[...]
    grid_rows[...] = jnp.zeros_like(grid_rows)
    grid_rows[: grid.shape[0], :] = grid[...]

    def plane_rows(row, carry):
        spot = pl.ds(pl.multiple_of(row * NGRID, NGRID), NGRID)
        across_cos, across_sin = trig[0, pl.ds(row, 1), :], trig[1, pl.ds(row, 1), :]
        plane_cos[spot, :] = (across_cos * trig[2] - across_sin * trig[3]).astype(jnp.bfloat16)
        plane_sin[spot, :] = (across_sin * trig[2] + across_cos * trig[3]).astype(jnp.bfloat16)
        return carry

    lax.fori_loop(0, NGRID, plane_rows, 0)

    def potential_rows(spot, carry):
        plane = spot % planes * parts + spot // planes
        rows = pl.ds(pl.multiple_of(plane * share, share), share)
        value = vloc[pl.ds(spot, 1), :] * (1.0 / NGRID**3)
        potential[rows, :] = jnp.broadcast_to(value, (share, side))
        return carry

    lax.fori_loop(0, NGRID, potential_rows, 0)

    each_peer(lambda turn: wave_copy(turn).wait_recv())
    lane = lax.broadcasted_iota(jnp.int32, all_waves.shape, 1)
    line = lax.broadcasted_iota(jnp.int32, (all_waves.shape[1], tile), 0)
    place = lax.broadcasted_iota(jnp.int32, (all_waves.shape[1], tile), 1)

    def pick(first, spot):
        return jnp.where(line == first * NGRID + spot, 1.0, 0.0)

    def spread(first, spot):
        return lax.dot_general(
            all_waves[...],
            pick(first, spot),
            (((1,), (0,)), ((), ())),
            precision=highest,
            preferred_element_type=jnp.float32,
        )

    def table_tile(step, carry):
        first = step * tile
        flat = first + place
        rise, along = flat // NGRID, flat % NGRID
        rise_cos, rise_sin = spread(2, rise), spread(3, rise)
        long_cos, long_sin = spread(4, along), spread(5, along)
        flat_cos = rise_cos * long_cos - rise_sin * long_sin
        flat_sin = rise_sin * long_cos + rise_cos * long_sin
        for plane in range(planes):
            level = me * planes + plane
            c = jnp.sum(jnp.where(lane == level, all_waves[...], 0.0), axis=1, keepdims=True)
            s = jnp.sum(
                jnp.where(lane == level + NGRID, all_waves[...], 0.0), axis=1, keepdims=True
            )
            spot = pl.ds(pl.multiple_of(plane * side + first, tile), tile)
            profile = grid[0:1, spot]
            full_cos = profile * (c * flat_cos - s * flat_sin)
            full_sin = profile * (s * flat_cos + c * flat_sin)
            wave_cos[:, spot] = full_cos
            wave_sin[:, spot] = full_sin
            table_cos[:, spot] = full_cos.astype(jnp.bfloat16)
            table_sin[:, spot] = full_sin.astype(jnp.bfloat16)
        return carry

    lax.fori_loop(0, side // tile, table_tile, 0)
    local_psi.wait()
    partial[...] = jnp.zeros_like(partial)

    def project(step, carry):
        spot = pl.ds(pl.multiple_of(step * tile, tile), tile)
        far = pl.ds(pl.multiple_of(local_g + step * tile, tile), tile)
        real, imag = psi[:, spot], psi[:, far]
        cosines, sines = table_cos[:, spot], table_sin[:, spot]
        partial[:WATERS, :] += inner(cosines, real) - inner(sines, imag)
        partial[WATERS:, :] += inner(sines, real) + inner(cosines, imag)
        return carry

    lax.fori_loop(0, local_g // tile, project, 0)

    def own_start(upto, rows):
        start = 0
        for bit in range(upto):
            start = start + me // (1 << bit) % 2 * (rows >> (bit + 1))
        return start

    def sum_step(values, land, which, bit, between):
        rows = values.shape[0]
        half = rows >> (bit + 1)
        size = 1 << bit
        mine = me // size % 2
        start = own_start(bit, rows)
        away = pl.ds(pl.multiple_of(start + (1 - mine) * half, half), half)
        keep = pl.ds(pl.multiple_of(start + mine * half, half), half)
        spot = pl.ds(rows - 2 * half, half)
        copy = remote(
            values.at[away], land.at[spot], pair(sum_sems, which, bit), me + (1 - 2 * mine) * size
        )
        copy.start()
        between()
        copy.wait()
        values[keep, :] += land[spot, :]

    def share_step(values, which, bit, between):
        rows = values.shape[0]
        size = 1 << bit
        mine = me // size % 2
        count = rows >> (bit + 1)
        spot = pl.ds(pl.multiple_of(own_start(bit + 1, rows), count), count)
        copy = remote(
            values.at[spot],
            values.at[spot],
            pair(share_sems, which, bit),
            me + (1 - 2 * mine) * size,
        )
        copy.start()
        between()
        copy.wait()

    for bit in range(steps):
        sum_step(partial, landing, 0, bit, lambda: issue(1))
    own_rows = partial.shape[0] // parts
    own = pl.ds(pl.multiple_of(own_start(steps, partial.shape[0]), own_rows), own_rows)
    gathered[own, :] = (partial[own, :] * (1.0 / GVECS)).astype(jnp.bfloat16)
    for bit in reversed(range(steps)):
        share_step(gathered, 0, bit, lambda: issue(1))
    issue(len(units))

    for first in range(0, gathered.shape[0], tile):
        for second in range(0, bands, tile):
            part = gathered[first : first + tile, second : second + tile].astype(jnp.float32)
            turned[second : second + tile, first : first + tile] = part.T.astype(jnp.bfloat16)

    def transform(chunk):
        mine = pl.ds(pl.multiple_of(me * share, share), share)
        own_bands = pl.ds(pl.multiple_of(chunk * block + me * share, share), share)
        got[chunk, mine, :] = psi[own_bands, :]
        each_peer(lambda turn: out_copy(chunk, turn).wait_recv())
        columns = side // tile

        def forward(step, carry):
            plane, column = step // columns, step % columns
            spot = pl.ds(pl.multiple_of(column * tile, tile), tile)
            rows = pl.ds(pl.multiple_of(plane * block, block), block)
            real = got[chunk, :, pl.ds(pl.multiple_of(plane * side, side), side)]
            imag = got[chunk, :, pl.ds(pl.multiple_of(local_g + plane * side, side), side)]
            cosines, sines = plane_cos[:, spot], plane_sin[:, spot]
            middle[0, rows, spot] = (product(real, cosines) - product(imag, sines)).astype(
                jnp.bfloat16
            )
            middle[1, rows, spot] = (product(real, sines) + product(imag, cosines)).astype(
                jnp.bfloat16
            )
            return carry

        lax.fori_loop(0, planes * columns, forward, 0)

        def lines(column, carry):
            spot = pl.ds(pl.multiple_of(column * tile, tile), tile)
            real, imag = middle[0, :, spot], middle[1, :, spot]
            value = potential[:, spot]
            cosines, sines = cross[0], cross[1]
            upper = (product(cosines, real) - product(sines, imag)) * value
            lower = (product(sines, real) + product(cosines, imag)) * value
            upper, lower = upper.astype(jnp.bfloat16), lower.astype(jnp.bfloat16)
            middle[0, :, spot] = (product(cosines, upper) + product(sines, lower)).astype(
                jnp.bfloat16
            )
            middle[1, :, spot] = (product(cosines, lower) - product(sines, upper)).astype(
                jnp.bfloat16
            )
            return carry

        lax.fori_loop(0, columns, lines, 0)

        def backward(step, carry):
            plane, column = step // columns, step % columns
            spot = pl.ds(pl.multiple_of(column * tile, tile), tile)
            rows = pl.ds(pl.multiple_of(plane * block, block), block)
            real, imag = middle[0, rows, :], middle[1, rows, :]
            cosines, sines = plane_cos[:, spot], plane_sin[:, spot]
            upper = pl.ds(pl.multiple_of(plane * side + column * tile, tile), tile)
            lower = pl.ds(pl.multiple_of(local_g + plane * side + column * tile, tile), tile)
            giving[chunk, :, upper] = (product(real, cosines) + product(imag, sines)).astype(
                jnp.bfloat16
            )
            giving[chunk, :, lower] = (product(imag, cosines) - product(real, sines)).astype(
                jnp.bfloat16
            )
            return carry

        lax.fori_loop(0, planes * columns, backward, 0)
        back[own_bands, :] = giving[chunk, mine, :]
        for far in range(parts // 2):
            back_copy(chunk, parts // 2 + far).start()
            if far > 0:
                back_copy(chunk, far).start()

    transform(0)

    force_sum[...] = jnp.zeros_like(force_sum)

    def local_part(step, carry):
        spot = pl.ds(pl.multiple_of(step * tile, tile), tile)
        far = pl.ds(pl.multiple_of(local_g + step * tile, tile), tile)
        kinetic = 1.0 - step_size * grid[1:2, spot]
        real, imag = psi[:, spot], psi[:, far]
        cosines, sines = table_cos[:, spot], table_sin[:, spot]
        turned_re, turned_im = turned[:, :WATERS], turned[:, WATERS:]
        strength = step_size * nonlocal_strength
        base[:, spot] = kinetic * real.astype(jnp.float32) - strength * (
            product(turned_re, cosines) + product(turned_im, sines)
        )
        base[:, far] = kinetic * imag.astype(jnp.float32) - strength * (
            product(turned_im, cosines) - product(turned_re, sines)
        )
        proj_re, proj_im = gathered[:WATERS, :], gathered[WATERS:, :]
        weighted_re = product(proj_re, real) + product(proj_im, imag)
        weighted_im = product(proj_re, imag) - product(proj_im, real)
        mixed = wave_cos[:, spot] * weighted_im + wave_sin[:, spot] * weighted_re
        force_sum[...] += lax.dot_general(
            mixed,
            grid_rows[:, spot],
            (((1,), (1,)), ((), ())),
            precision=highest,
            preferred_element_type=jnp.float32,
        )
        return carry

    lax.fori_loop(0, local_g // tile, local_part, 0)
    force_land[me] = force_sum[own_spot, :]
    each_peer(lambda turn: force_copy(turn).start())

    transform(1)

    def finish(chunk):
        def rows_of(turn, carry):
            @pl.when(turn > 0)
            def _():
                back_copy(chunk, turn).wait_recv()

            rows = pl.ds(
                pl.multiple_of(chunk * block + other(turn) * share, share), share
            )
            value = base[rows, :] - step_size * back[rows, :].astype(jnp.float32)
            value = value.astype(jnp.bfloat16)
            trial[0, rows, :] = value[:, :local_g]
            trial[1, rows, :] = value[:, local_g:]
            return carry

        lax.fori_loop(0, parts, rows_of, 0)

    corner_row = lax.broadcasted_iota(jnp.int32, (block, block), 0)
    corner_column = lax.broadcasted_iota(jnp.int32, (block, block), 1)

    def overlap(first, second):
        rows = pl.ds(first * block, block)
        columns = pl.ds(second * block, block)

        def even(spot):
            return inner(trial[0, rows, spot], trial[0, columns, spot]) + inner(
                trial[1, rows, spot], trial[1, columns, spot]
            )

        def odd(spot):
            return inner(trial[1, rows, spot], trial[0, columns, spot]) - inner(
                trial[0, rows, spot], trial[1, columns, spot]
            )

        margin[rows, columns] = jnp.zeros((block, block), jnp.float32)

        def add(step, carry):
            spot = pl.ds(pl.multiple_of(step * tile, tile), tile)
            if first < second:
                value = even(spot)
            elif first > second:
                value = odd(spot)
            else:
                value = jnp.where(corner_row <= corner_column, even(spot), odd(spot))
            margin[rows, columns] += value
            return carry

        lax.fori_loop(0, local_g // tile, add, 0)

    for chunk in range(CHUNKS):
        finish(chunk)
        trial_copy = pltpu.make_async_copy(
            trial.at[:, pl.ds(chunk * block, block)],
            trial_hbm.at[:, pl.ds(chunk * block, block)],
            local_sem.at[1 + chunk],
        )
        trial_copy.start()
        for first in range(chunk + 1):
            overlap(first, chunk)
            if first != chunk:
                overlap(chunk, first)

    for bit in range(steps):
        sum_step(margin, landing_two, 1, bit, lambda: None)
    start = own_start(steps, bands)
    own_rows = bands // parts
    own = pl.ds(pl.multiple_of(start, own_rows), own_rows)
    row = start + lax.broadcasted_iota(jnp.int32, (own_rows, bands), 0)
    column = lax.broadcasted_iota(jnp.int32, (own_rows, bands), 1)
    mixed_rows = jnp.where(row == column, 1.5, 0.0) - (0.5 / GVECS) * margin[own, :]
    gathered_two[own, :] = mixed_rows.astype(jnp.bfloat16)
    for bit in reversed(range(steps)):
        share_step(gathered_two, 1, bit, lambda: None)

    for first in range(0, bands, tile):
        for second in range(0, bands, tile):
            there = gathered_two[first : first + tile, second : second + tile]
            flipped = gathered_two[second : second + tile, first : first + tile]
            there = there.astype(jnp.float32)
            flipped = flipped.astype(jnp.float32).T
            row = first + lax.broadcasted_iota(jnp.int32, (tile, tile), 0)
            column = second + lax.broadcasted_iota(jnp.int32, (tile, tile), 1)
            mix_re = jnp.where(row <= column, there, flipped)
            mix_im = jnp.where(
                row > column, there, jnp.where(row < column, -flipped, jnp.zeros_like(there))
            )
            mixed_out[0, first : first + tile, second : second + tile] = mix_re.astype(
                jnp.bfloat16
            )
            mixed_out[1, first : first + tile, second : second + tile] = mix_im.astype(
                jnp.bfloat16
            )

    each_peer(lambda turn: force_copy(turn).wait_recv())

    def add_force(source, carry):
        return carry + force_land[source]

    force_out[...] = lax.fori_loop(0, parts, add_force, jnp.zeros(force_out.shape, jnp.float32))
    for chunk in range(CHUNKS):
        pltpu.make_async_copy(
            trial.at[:, pl.ds(chunk * block, block)],
            trial_hbm.at[:, pl.ds(chunk * block, block)],
            local_sem.at[1 + chunk],
        ).wait()
        each_peer(lambda turn: out_copy(chunk, turn).wait_send())
        each_peer(lambda turn: back_copy(chunk, turn).wait_send())
    each_peer(lambda turn: wave_copy(turn).wait_send())
    each_peer(lambda turn: force_copy(turn).wait_send())


def fused_device(positions, weights, psi, vloc):
    near_forces = field_forces(positions)
    weight_float = weights.astype(jnp.float32)
    mixing = weight_float / jnp.sum(weight_float, axis=1, keepdims=True)
    parts = lax.axis_size("ga")
    bands, local_g = psi.shape[1], psi.shape[3]
    side = NGRID * NGRID
    planes = local_g // side
    share = bands // (parts * CHUNKS)
    block = parts * share
    waters = positions.shape[2] // 3
    near_oxygen = jnp.einsum("cj,jan->can", mixing, positions[:, :, 0::3], precision=highest)[0]
    spokes = frequency(jnp.arange(NGRID, dtype=jnp.int32), NGRID)
    angles = near_oxygen.T[:, :, None] * spokes
    own_waves = jnp.stack([jnp.cos(angles), jnp.sin(angles)], 2).reshape(waters, 6 * NGRID)
    own_waves = jnp.pad(own_waves, ((0, 0), (0, 2 * NGRID)))
    flat_index = lax.axis_index("ga") * local_g + jnp.arange(local_g, dtype=jnp.int32)
    gvectors = [
        frequency(flat_index // side, NGRID),
        frequency(flat_index // NGRID % NGRID, NGRID),
        frequency(flat_index % NGRID, NGRID),
    ]
    square = gvectors[0] * gvectors[0] + gvectors[1] * gvectors[1] + gvectors[2] * gvectors[2]
    profile = jnp.exp(-0.5 * width_square * square)
    nothing = jnp.zeros_like(square)
    grid = jnp.stack([profile, 0.5 * square] + gvectors + [nothing] * 3)
    vmem = pl.BlockSpec(memory_space=pltpu.VMEM)
    anywhere = pl.BlockSpec(memory_space=pl.ANY)
    steps = parts.bit_length() - 1
    f32, bf16 = jnp.float32, jnp.bfloat16
    dma = pltpu.SemaphoreType.DMA
    trial, mixed, force = pl.pallas_call(
        functools.partial(step_kernel, (parts, bands, local_g)),
        out_shape=(
            jax.ShapeDtypeStruct((2, bands, local_g), bf16),
            jax.ShapeDtypeStruct((2, bands, bands), bf16),
            jax.ShapeDtypeStruct((waters, 128), f32),
        ),
        in_specs=[anywhere, vmem, vmem, vmem, vmem, vmem],
        out_specs=(anywhere, vmem, vmem),
        scratch_shapes=[
            pltpu.VMEM((bands, 2 * local_g), bf16),
            pltpu.VMEM((WATERS, 8 * NGRID), f32),
            pltpu.VMEM((WATERS, local_g), bf16),
            pltpu.VMEM((WATERS, local_g), bf16),
            pltpu.VMEM((WATERS, local_g), f32),
            pltpu.VMEM((WATERS, local_g), f32),
            pltpu.VMEM((side, side), bf16),
            pltpu.VMEM((side, side), bf16),
            pltpu.VMEM((planes * block, side), f32),
            pltpu.VMEM((CHUNKS, block, 2 * local_g), bf16),
            pltpu.VMEM((2, planes * block, side), bf16),
            pltpu.VMEM((CHUNKS, block, 2 * local_g), bf16),
            pltpu.VMEM((bands, 2 * local_g), bf16),
            pltpu.VMEM((bands, 2 * local_g), f32),
            pltpu.VMEM((2, bands, local_g), bf16),
            pltpu.VMEM((2 * WATERS, bands), f32),
            pltpu.VMEM((2 * WATERS, bands), f32),
            pltpu.VMEM((2 * WATERS, bands), bf16),
            pltpu.VMEM((bands, 2 * WATERS), bf16),
            pltpu.VMEM((bands, bands), f32),
            pltpu.VMEM((bands, bands), f32),
            pltpu.VMEM((bands, bands), bf16),
            pltpu.VMEM((WATERS, 128), f32),
            pltpu.VMEM((parts, waters, 128), f32),
            pltpu.VMEM((128, local_g), f32),
            dma((1 + CHUNKS,)),
            dma((2, parts)),
            dma((2, CHUNKS, parts)),
            dma((2, CHUNKS, parts)),
            dma((2, parts)),
            dma((2, 2, steps)),
            dma((2, 2, steps)),
        ],
        compiler_params=pltpu.CompilerParams(
            collective_id=0, has_side_effects=True, vmem_limit_bytes=67043328
        ),
    )(
        psi[0].reshape(bands, 2 * local_g),
        own_waves,
        grid,
        trig_tables(),
        cross_tables(parts, planes, share),
        vloc[0].reshape(NGRID, side),
    )
    turn = jnp.concatenate(
        [
            jnp.concatenate([mixed[0], -mixed[1]], 1),
            jnp.concatenate([mixed[1], mixed[0]], 1),
        ],
        0,
    )
    updated = product(turn, trial.reshape(2 * bands, local_g)).astype(jnp.bfloat16)
    psi_new = updated.reshape(2, bands, local_g).transpose(1, 0, 2)[None]
    strength = 2.0 * occupation * nonlocal_strength / GVECS
    oxygen_force = strength * force[:, 2:5].T
    hydrogen_zero = jnp.zeros_like(oxygen_force)
    dft_force = jnp.stack([oxygen_force, hydrogen_zero, hydrogen_zero], axis=2).reshape(1, 3, -1)
    contracted_force = mixing[0][:, None, None] * dft_force
    return (psi_new, near_forces + BEADS / CBEADS * contracted_force)


def step_device(positions, weights, psi, vloc):
    parts = lax.axis_size("ga")
    bands, local_g = psi.shape[1], psi.shape[3]
    side = NGRID * NGRID
    fits = (
        local_g % side == 0
        and parts & (parts - 1) == 0
        and parts >= 4
        and bands % (parts * CHUNKS * 16) == 0
        and bands // CHUNKS % 256 == 0
        and bands * local_g <= 2**20
    )
    if fits:
        return fused_device(positions, weights, psi, vloc)
    return per_device(positions, weights, psi, vloc)


def solution(mesh):
    placed = (P("rep", None, "ga"), P(), P("rep", None, None, "ga"), P("rep", None))
    return jax.shard_map(
        step_device,
        mesh=mesh,
        in_specs=placed,
        out_specs=(P("rep", None, None, "ga"), P("rep", None, "ga")),
        check_vma=False,
    )
```

```python
import functools

import jax
import jax.numpy as jnp
import numpy as np
from jax import lax
from jax.experimental import pallas as pl
from jax.experimental.pallas import tpu as pltpu
from jax.sharding import PartitionSpec as P

BEADS = 32
CBEADS = 1
WATERS = 256
NGRID = 32
GVECS = 32768
CHUNKS = 2


box_length = 20.0
bond_stiff = 0.5
bond_rest = 1.8
spring_stiff = 2.0
width_square = 0.09
step_size = 0.02
nonlocal_strength = 250.0
occupation = 2.0
highest = lax.Precision.HIGHEST


def frequency(index, count):
    signed = jnp.where(index < count // 2, index, index - count)
    return signed.astype(jnp.float32) * (2.0 * jnp.pi / box_length)


def field_forces(positions):
    oxygen = positions[:, :, 0::3]
    toward_one = positions[:, :, 1::3] - oxygen
    toward_two = positions[:, :, 2::3] - oxygen

    def stretch(offset):
        length = jnp.sqrt(jnp.sum(offset * offset, axis=1, keepdims=True))
        return -bond_stiff * (length - bond_rest) * offset / length

    pull_one = stretch(toward_one)
    pull_two = stretch(toward_two)
    bonds = jnp.stack([-(pull_one + pull_two), pull_one, pull_two], axis=3).reshape(positions.shape)
    springs = 2.0 * positions - jnp.roll(positions, 1, axis=0) - jnp.roll(positions, -1, axis=0)
    return bonds - spring_stiff * springs


def inner(left_mat, right_mat):
    return lax.dot_general(
        left_mat, right_mat, (((1,), (1,)), ((), ())), preferred_element_type=jnp.float32
    )


def real_form(freq_index, group_index):
    product = freq_index[:, None] * freq_index[None, :] % NGRID
    angle = product.astype(jnp.float32) * (2.0 * jnp.pi / NGRID)
    same = (group_index[:, None] == group_index[None, :]).astype(jnp.float32)
    cosines = jnp.cos(angle) * same
    sines = jnp.sin(angle) * same
    return jnp.stack([jnp.stack([cosines, sines], 1), jnp.stack([-sines, cosines], 1)], 0)


def plane_table():
    index = jnp.arange(NGRID, dtype=jnp.int32)
    return real_form(index, jnp.zeros_like(index))


def block_table(length, within):
    index = jnp.arange(length, dtype=jnp.int32)
    if within:
        return real_form(index % NGRID, index // NGRID)
    return real_form(index // NGRID, index % NGRID)


def grid_sum(psi, vloc, parts):
    bands = psi.shape[1]
    local_g = psi.shape[3]
    x_table = plane_table()
    z_table = block_table(local_g, True)
    y_table = block_table(NGRID * NGRID, False)
    grid_potential = vloc[0].reshape(1, 1, NGRID, NGRID * NGRID)
    grouped_raw = psi[0].reshape(parts, bands // parts, 2, local_g)
    planes = lax.all_to_all(grouped_raw, "ga", split_axis=0, concat_axis=3, tiled=True)
    band_count = planes.shape[1]
    blocks_whole = planes.astype(jnp.float32).reshape(band_count, 2, NGRID**3 // local_g, local_g)
    along_z = jnp.einsum("mckp,cpdq->mdkq", blocks_whole, z_table, precision=highest) * (
        1.0 / NGRID
    )
    grid = along_z.reshape(band_count, 2, NGRID, NGRID * NGRID)
    grid = jnp.einsum("mcxr,cxdw->mdwr", grid, x_table, precision=highest) * (1.0 / NGRID)
    grid = jnp.einsum("mcxp,cpdq->mdxq", grid, y_table, precision=highest) * (1.0 / NGRID)
    grid = grid * grid_potential
    grid = jnp.einsum("mdxq,cpdq->mcxp", grid, y_table, precision=highest)
    grid = jnp.einsum("mdwr,cxdw->mcxr", grid, x_table, precision=highest)
    returning = grid.reshape(1, band_count, 2, NGRID**3)
    returned = lax.all_to_all(
        returning.astype(jnp.bfloat16), "ga", split_axis=3, concat_axis=0, tiled=True
    ).astype(returning.dtype)
    returned = returned.reshape(bands, 2, local_g)
    potential = jnp.einsum("bdq,cpdq->bcp", returned, z_table, precision=highest)
    return potential[:, 0], potential[:, 1]


def plane_rotation():
    small = np.arange(NGRID)
    angle = small[:, None] * small[None, :] % NGRID * (2.0 * np.pi / NGRID)
    side = NGRID * NGRID
    wave = np.kron(np.exp(1j * angle), np.exp(1j * angle))
    real, imag = np.real(wave), np.imag(wave)
    table = np.stack([np.stack([real, -imag], 1), np.stack([imag, real], 1)], 1)
    return jnp.asarray(table.reshape(2 * side, 2 * side).astype(np.float32), jnp.bfloat16)


def line_rotation(group):
    small = np.arange(NGRID)
    angle = small[:, None] * small[None, :] % NGRID * (2.0 * np.pi / NGRID)
    real, imag = np.cos(angle), np.sin(angle)
    form = np.stack([np.stack([real, -imag], 2), np.stack([imag, real], 2)], 1)
    same = np.eye(group)
    table = form[:, None, :, :, None, :] * same[None, :, None, None, :, None]
    size = 2 * NGRID * group
    return jnp.asarray(table.reshape(size, size).astype(np.float32), jnp.bfloat16)


def plane_out(psi, parts, plane_table, offset):
    bands = psi.shape[1]
    side = NGRID * NGRID
    planes = psi.shape[3] // side
    chunk = bands // CHUNKS
    pieces = []
    for first in range(0, bands, chunk):
        part = lax.dynamic_slice_in_dim(psi[0], first + offset, chunk, axis=0).reshape(chunk, 2, planes, side)
        part = part.transpose(2, 0, 1, 3).reshape(planes, chunk, 2 * side)
        pieces.append(
            jnp.stack(
                [
                    jnp.einsum(
                        "qk,bk->qb", plane_table, part[p], preferred_element_type=jnp.float32
                    )
                    .astype(jnp.bfloat16)
                    .reshape(parts, 2 * side // parts, chunk)
                    for p in range(planes)
                ],
                1,
            )
        )
    return pieces


def exchange(piece):
    return lax.all_to_all(piece, "ga", split_axis=0, concat_axis=0, tiled=True)


def line_action(vloc, parts):
    side = NGRID * NGRID
    points = side // parts
    group = min(8, points)
    groups = points // group
    line_table = line_rotation(group)
    start = lax.axis_index("ga") * points
    own = lax.dynamic_slice_in_dim(vloc[0].reshape(NGRID, side), start, points, axis=1)
    own = own.reshape(NGRID, groups, group).transpose(1, 0, 2) * (1.0 / (NGRID * side))
    own = jnp.broadcast_to(own[..., None], (groups, NGRID, group, 2)).reshape(groups, -1, 1)
    scaled = (own * line_table.astype(jnp.float32)).astype(jnp.bfloat16)
    return jnp.einsum(
        "ea,gec->gac", line_table, scaled, preferred_element_type=jnp.float32
    ).astype(jnp.bfloat16)


def line_step(action, lines):
    parts, planes, rows, chunk = lines.shape
    groups = action.shape[0]
    lines = lines.reshape(parts * planes, groups, rows // groups, chunk)
    lines = lines.transpose(1, 0, 2, 3).reshape(groups, -1, chunk)
    lines = jnp.einsum(
        "gac,gcb->gab", action, lines, preferred_element_type=jnp.float32
    ).astype(jnp.bfloat16)
    lines = lines.reshape(groups, parts * planes, rows // groups, chunk).transpose(1, 0, 2, 3)
    return lines.reshape(parts, planes, rows, chunk)


def plane_back(backs, plane_table):
    side = NGRID * NGRID
    reals, imags = [], []
    for back in backs:
        chunk = back.shape[3]
        whole = [
            jnp.einsum(
                "qb,qk->bk",
                back[:, p].reshape(2 * side, chunk),
                plane_table,
                preferred_element_type=jnp.float32,
            )
            for p in range(back.shape[1])
        ]
        reals.append(jnp.concatenate([w[:, :side] for w in whole], 1))
        imags.append(jnp.concatenate([w[:, side:] for w in whole], 1))
    return jnp.concatenate(reals, 0), jnp.concatenate(imags, 0)


def waves(oxygens, gvectors, profile):
    local_g = profile.shape[0]
    side = NGRID * NGRID
    if local_g % side:
        phases = jnp.einsum("ai,ag->ig", oxygens, gvectors, precision=highest)
        return profile * jnp.cos(phases), profile * jnp.sin(phases)
    spots = oxygens.T
    flat = spots[:, 1:2] * gvectors[1:2, :side] + spots[:, 2:3] * gvectors[2:3, :side]
    flat_cos, flat_sin = jnp.cos(flat), jnp.sin(flat)
    along = spots[:, 0:1] * gvectors[0:1, ::side]
    along_cos, along_sin = jnp.cos(along), jnp.sin(along)
    cosines, sines = [], []
    for p in range(local_g // side):
        c, s = along_cos[:, p : p + 1], along_sin[:, p : p + 1]
        cosines.append(c * flat_cos - s * flat_sin)
        sines.append(s * flat_cos + c * flat_sin)
    return profile * jnp.concatenate(cosines, 1), profile * jnp.concatenate(sines, 1)


def per_device(positions, weights, psi, vloc):
    near_forces = field_forces(positions)
    weight_float = weights.astype(jnp.float32)
    mixing = weight_float / jnp.sum(weight_float, axis=1, keepdims=True)
    centres = jnp.einsum("cj,jan->can", mixing, positions, precision=highest)
    parts = lax.axis_size("ga")
    near_oxygen = centres[0][:, 0::3]
    own_waters = near_oxygen.shape[1]
    everyone = lax.dynamic_update_slice(
        jnp.zeros((3, own_waters * parts), jnp.float32),
        near_oxygen,
        (0, lax.axis_index("ga") * own_waters),
    )
    oxygens = lax.psum(everyone, "ga")
    side = NGRID * NGRID
    whole_planes = psi.shape[3] % side == 0 and side % parts == 0
    if whole_planes:
        plane_table = plane_rotation()
        pieces = plane_out(psi, parts, plane_table, (oxygens[0, 0] * 0.0).astype(jnp.int32))
        lines = [exchange(piece) for piece in pieces]
        action = line_action(vloc, parts)
    bands = psi.shape[1]
    local_g = psi.shape[3]
    flat_index = lax.axis_index("ga") * local_g + jnp.arange(local_g, dtype=jnp.int32)
    gvectors = jnp.stack(
        [
            frequency(flat_index // (NGRID * NGRID), NGRID),
            frequency(flat_index // NGRID % NGRID, NGRID),
            frequency(flat_index % NGRID, NGRID),
        ]
    )
    square = jnp.sum(gvectors * gvectors, axis=0)
    profile = jnp.exp(-0.5 * width_square * square)
    kinetic = 0.5 * square
    wave_cos, wave_sin = waves(oxygens, gvectors, profile)
    table = jnp.concatenate(
        [jnp.concatenate([wave_cos, -wave_sin], 1), jnp.concatenate([wave_sin, wave_cos], 1)], 0
    ).astype(jnp.bfloat16)
    wavefunc = psi[0].reshape(bands, 2 * local_g)
    partial_proj = (inner(table, wavefunc) * (1.0 / GVECS)).reshape(2, WATERS, bands)
    share = lax.psum_scatter(partial_proj, "ga", scatter_dimension=1, tiled=True).astype(
        jnp.bfloat16
    )
    table_blocks = table.reshape(2 * WATERS, 2 * local_g)
    copies = jnp.broadcast_to(share[None], (parts,) + share.shape)
    if whole_planes:
        lines[-1], copies = lax.optimization_barrier((lines[-1], copies))
    all_proj = lax.all_to_all(copies, "ga", split_axis=0, concat_axis=0, tiled=True)
    if whole_planes:
        moved = [line_step(action, line) for line in lines]
        moved[0], all_proj = lax.optimization_barrier((moved[0], all_proj))
        backs = [exchange(piece) for piece in moved]
    all_proj = all_proj.transpose(1, 0, 2, 3).reshape(2 * WATERS, bands)
    nonlocal_term = jnp.einsum(
        "ib,ig->bg", all_proj, table_blocks, preferred_element_type=jnp.float32
    )
    crossed = jnp.dot(all_proj, wavefunc, preferred_element_type=jnp.float32)
    weighted_re = crossed[:WATERS, :local_g] + crossed[WATERS:, local_g:]
    weighted_im = crossed[:WATERS, local_g:] - crossed[WATERS:, :local_g]
    mixed_wave = wave_cos * weighted_im + wave_sin * weighted_re
    force_part = (
        2.0
        * occupation
        * nonlocal_strength
        / GVECS
        * jnp.einsum("ag,ig->ai", gvectors, mixed_wave, precision=highest)
    )
    force_rows = force_part.reshape(3, parts, own_waters).transpose(1, 0, 2)
    force_rows = force_rows.reshape(parts, 1, 3 * own_waters)
    force_rows = jnp.pad(force_rows, ((0, 0), (0, 0), (0, bands - 3 * own_waters)))
    wave_float = psi[0].astype(jnp.float32)
    if whole_planes:
        potential = plane_back(backs, plane_table)
    else:
        potential = grid_sum(psi, vloc, parts)
    hamil_re = (
        kinetic * wave_float[:, 0]
        + potential[0]
        + nonlocal_strength * nonlocal_term[:, :local_g]
    )
    hamil_im = (
        kinetic * wave_float[:, 1]
        + potential[1]
        + nonlocal_strength * nonlocal_term[:, local_g:]
    )
    trial_re = (wave_float[:, 0] - step_size * hamil_re).astype(jnp.bfloat16)
    trial_im = (wave_float[:, 1] - step_size * hamil_im).astype(jnp.bfloat16)
    row = lax.broadcasted_iota(jnp.int32, (bands, bands), 0)
    column = lax.broadcasted_iota(jnp.int32, (bands, bands), 1)
    even = inner(trial_re, trial_re) + inner(trial_im, trial_im)
    odd = inner(trial_im, trial_re) - inner(trial_re, trial_im)
    packed = jnp.where(row <= column, even, odd) * (1.0 / GVECS)
    shares = lax.all_to_all(
        jnp.concatenate([packed.reshape(parts, bands // parts, bands), force_rows], 1),
        "ga",
        split_axis=0,
        concat_axis=0,
        tiled=True,
    )
    sums = jnp.sum(shares, axis=0)
    oxygen_force = sums[-1, : 3 * own_waters].reshape(3, own_waters)
    hydrogen_zero = jnp.zeros_like(oxygen_force)
    dft_forces = [jnp.stack([oxygen_force, hydrogen_zero, hydrogen_zero], axis=2).reshape(3, -1)]
    own_rows = lax.broadcasted_iota(jnp.int32, (bands // parts, bands), 0) + lax.axis_index(
        "ga"
    ) * (bands // parts)
    own_columns = lax.broadcasted_iota(jnp.int32, (bands // parts, bands), 1)
    mixed_rows = jnp.where(own_rows == own_columns, 1.5, 0.0) - 0.5 * sums[:-1]
    mixed = lax.all_gather(mixed_rows.astype(jnp.bfloat16), "ga", axis=0, tiled=True)
    turned = mixed.T
    mix_re = jnp.where(row <= column, mixed, turned)
    mix_im = jnp.where(row > column, mixed, jnp.where(row < column, -turned, jnp.zeros_like(turned)))
    both = jnp.concatenate([trial_re, trial_im], 0)
    new_re = jnp.dot(
        jnp.concatenate([mix_re, -mix_im], 1), both, preferred_element_type=jnp.float32
    ).astype(jnp.bfloat16)
    new_im = jnp.dot(
        jnp.concatenate([mix_im, mix_re], 1), both, preferred_element_type=jnp.float32
    ).astype(jnp.bfloat16)
    new_waves = [jnp.stack([new_re, new_im], 1)]
    contracted_force = jnp.einsum("cj,can->jan", mixing, jnp.stack(dft_forces), precision=highest)
    bead_forces = near_forces + BEADS / CBEADS * contracted_force
    return (jnp.stack(new_waves), bead_forces)


def product(left_mat, right_mat):
    return jnp.dot(left_mat, right_mat, preferred_element_type=jnp.float32)


def trig_tables():
    small = np.arange(NGRID)
    angle = small[:, None] * small[None, :] % NGRID * (2.0 * np.pi / NGRID)
    cosines, sines = np.cos(angle), np.sin(angle)
    rows = [np.repeat(cosines, NGRID, 1), np.repeat(sines, NGRID, 1)]
    rows += [np.tile(cosines, (1, NGRID)), np.tile(sines, (1, NGRID))]
    return jnp.asarray(np.stack(rows), jnp.float32)


def cross_tables(parts, planes, share):
    spot = (np.arange(parts)[None, :] * planes + np.arange(planes)[:, None]).reshape(-1)
    angle = spot[:, None] * spot[None, :] % NGRID * (2.0 * np.pi / NGRID)
    same = np.eye(share)
    pair = np.stack([np.kron(np.cos(angle), same), np.kron(np.sin(angle), same)])
    return jnp.asarray(pair.astype(np.float32), jnp.bfloat16)


def step_kernel(
    sizes,
    psi_hbm,
    positions,
    weights,
    trig,
    cross,
    vloc,
    trial_hbm,
    mixed_out,
    force_out,
    raw,
    psi,
    own_waves,
    grid,
    near,
    all_waves,
    table_cos,
    table_sin,
    wave_cos,
    wave_sin,
    plane_cos,
    plane_sin,
    potential,
    got,
    whole,
    middle,
    giving,
    back,
    base,
    trial,
    partial,
    landing,
    gathered,
    turned,
    margin,
    landing_two,
    gathered_two,
    force_sum,
    force_land,
    grid_rows,
    local_sem,
    wave_sems,
    out_sems,
    back_sems,
    force_sems,
    sum_sems,
    share_sems,
):
    parts, bands, local_g = sizes
    side = NGRID * NGRID
    planes = local_g // side
    share = bands // (parts * CHUNKS)
    block = parts * share
    steps = parts.bit_length() - 1
    tile = 256
    me = lax.axis_index("ga")

    def other(turn):
        total = 0
        for bit in range(steps):
            size = 1 << bit
            total = total + (me // size + turn // size) % 2 * size
        return total

    def remote(source, target, sems, peer):
        return pltpu.make_async_remote_copy(
            src_ref=source,
            dst_ref=target,
            send_sem=sems[0],
            recv_sem=sems[1],
            device_id={"ga": peer},
            device_id_type=pl.DeviceIdType.MESH,
        )

    def each_peer(act):
        def body(turn, carry):
            act(turn)
            return carry

        lax.fori_loop(1, parts, body, 0)

    def pair(sems, *spot):
        return sems.at[(0,) + spot], sems.at[(1,) + spot]

    def wave_copy(turn):
        waters = own_waves.shape[0]
        spot = pl.ds(pl.multiple_of(me * waters, waters), waters)
        return remote(own_waves, all_waves.at[spot], pair(wave_sems, turn), other(turn))

    def out_copy(chunk, turn):
        peer = other(turn)
        source = pl.ds(pl.multiple_of(chunk * block + peer * share, share), share)
        target = pl.ds(pl.multiple_of(me * share, share), share)
        return remote(
            psi_hbm.at[source], got.at[chunk, target], pair(out_sems, chunk, turn), peer
        )

    def back_copy(chunk, turn):
        peer = other(turn)
        source = pl.ds(pl.multiple_of(peer * share, share), share)
        target = pl.ds(pl.multiple_of(chunk * block + me * share, share), share)
        return remote(
            giving.at[chunk, source], back.at[target], pair(back_sems, chunk, turn), peer
        )

    def force_copy(turn):
        peer = other(turn)
        waters = own_waves.shape[0]
        source = pl.ds(pl.multiple_of(peer * waters, waters), waters)
        return remote(
            force_sum.at[source], force_land.at[me], pair(force_sems, turn), peer
        )

    local_psi = pltpu.make_async_copy(psi_hbm, raw, local_sem.at[0])
    local_psi.start()
    barrier = pltpu.get_barrier_semaphore()

    def greet(turn):
        pl.semaphore_signal(
            barrier, inc=1, device_id={"ga": other(turn)}, device_id_type=pl.DeviceIdType.MESH
        )

    each_peer(greet)
    waters = own_waves.shape[0]
    atoms = positions.shape[2]
    beads = positions.shape[0]

    def exact(left_mat, right_mat, right_axis=0):
        return lax.dot_general(
            left_mat,
            right_mat,
            (((1,), (right_axis,)), ((), ())),
            precision=highest,
            preferred_element_type=jnp.float32,
        )

    def spots(shape):
        return lax.broadcasted_iota(jnp.int32, shape, 0), lax.broadcasted_iota(jnp.int32, shape, 1)

    weight_row = weights[...].astype(jnp.float32)
    mixing = weight_row / jnp.sum(weight_row, axis=1, keepdims=True)
    wave_row, wave_lane = spots(own_waves.shape)
    own_row, own_atom = spots((waters, atoms))
    oxygen_pick = jnp.where(own_atom == 3 * own_row, 1.0, 0.0)
    spokes = frequency(wave_lane % NGRID, NGRID)
    angles = jnp.zeros(own_waves.shape, jnp.float32)
    for axis in range(3):
        centre = exact(jnp.broadcast_to(mixing, (8, beads)), positions[:, axis, :])
        column = exact(oxygen_pick, centre, 1)[:, 0:1]
        angles += column * jnp.where(wave_lane // (2 * NGRID) == axis, spokes, 0.0)
    own_waves[...] = jnp.where(wave_lane // NGRID % 2 == 0, jnp.cos(angles), jnp.sin(angles))
    own_spot = pl.ds(pl.multiple_of(me * waters, waters), waters)
    all_waves[own_spot, :] = own_waves[...]
    pl.semaphore_wait(barrier, parts - 1)

    units = [(chunk, far) for chunk in range(CHUNKS) for far in range(parts // 2)]
    queue = list(units)

    def issue(count):
        for _ in range(count):
            if queue:
                chunk, far = queue.pop(0)
                out_copy(chunk, parts // 2 + far).start()
                if far > 0:
                    out_copy(chunk, far).start()

    each_peer(lambda turn: wave_copy(turn).start())
    issue(2)

    flat_index = me * local_g + lax.broadcasted_iota(jnp.int32, (1, local_g), 1)
    gvectors = [
        frequency(flat_index // side, NGRID),
        frequency(flat_index // NGRID % NGRID, NGRID),
        frequency(flat_index % NGRID, NGRID),
    ]
    square = gvectors[0] * gvectors[0] + gvectors[1] * gvectors[1] + gvectors[2] * gvectors[2]
    grid[0:1, :] = jnp.exp(-0.5 * width_square * square)
    grid[1:2, :] = 0.5 * square
    grid_rows[...] = jnp.zeros_like(grid_rows)
    for axis in range(3):
        grid_rows[axis : axis + 1, :] = gvectors[axis]

    def plane_rows(row, carry):
        spot = pl.ds(pl.multiple_of(row * NGRID, NGRID), NGRID)
        across_cos, across_sin = trig[0, pl.ds(row, 1), :], trig[1, pl.ds(row, 1), :]
        plane_cos[spot, :] = (across_cos * trig[2] - across_sin * trig[3]).astype(jnp.bfloat16)
        plane_sin[spot, :] = (across_sin * trig[2] + across_cos * trig[3]).astype(jnp.bfloat16)
        return carry

    lax.fori_loop(0, NGRID, plane_rows, 0)

    def potential_rows(spot, carry):
        plane = spot % planes * parts + spot // planes
        rows = pl.ds(pl.multiple_of(plane * share, share), share)
        value = vloc[:, pl.ds(pl.multiple_of(spot * side, side), side)] * (1.0 / NGRID**3)
        potential[rows, :] = jnp.broadcast_to(value, (share, side))
        return carry

    lax.fori_loop(0, NGRID, potential_rows, 0)

    strip = 16

    def unpack_rows(step, carry):
        rows = pl.ds(pl.multiple_of(step * strip, strip), strip)
        psi[rows, :local_g] = raw[rows, 0, :]
        psi[rows, local_g:] = raw[rows, 1, :]
        return carry

    local_psi.wait()
    lax.fori_loop(0, bands // strip, unpack_rows, 0)
    each_peer(lambda turn: wave_copy(turn).wait_recv())
    lane = lax.broadcasted_iota(jnp.int32, all_waves.shape, 1)
    line = lax.broadcasted_iota(jnp.int32, (all_waves.shape[1], tile), 0)
    place = lax.broadcasted_iota(jnp.int32, (all_waves.shape[1], tile), 1)

    def pick(first, spot):
        return jnp.where(line == first * NGRID + spot, 1.0, 0.0)

    def spread(first, spot):
        return lax.dot_general(
            all_waves[...],
            pick(first, spot),
            (((1,), (0,)), ((), ())),
            precision=highest,
            preferred_element_type=jnp.float32,
        )

    def table_tile(step, carry):
        first = step * tile
        flat = first + place
        rise, along = flat // NGRID, flat % NGRID
        rise_cos, rise_sin = spread(2, rise), spread(3, rise)
        long_cos, long_sin = spread(4, along), spread(5, along)
        flat_cos = rise_cos * long_cos - rise_sin * long_sin
        flat_sin = rise_sin * long_cos + rise_cos * long_sin
        for plane in range(planes):
            level = me * planes + plane
            c = jnp.sum(jnp.where(lane == level, all_waves[...], 0.0), axis=1, keepdims=True)
            s = jnp.sum(
                jnp.where(lane == level + NGRID, all_waves[...], 0.0), axis=1, keepdims=True
            )
            spot = pl.ds(pl.multiple_of(plane * side + first, tile), tile)
            profile = grid[0:1, spot]
            full_cos = profile * (c * flat_cos - s * flat_sin)
            full_sin = profile * (s * flat_cos + c * flat_sin)
            wave_cos[:, spot] = full_cos
            wave_sin[:, spot] = full_sin
            table_cos[:, spot] = full_cos.astype(jnp.bfloat16)
            table_sin[:, spot] = full_sin.astype(jnp.bfloat16)
        return carry

    lax.fori_loop(0, side // tile, table_tile, 0)
    partial[...] = jnp.zeros_like(partial)

    def project(step, carry):
        spot = pl.ds(pl.multiple_of(step * tile, tile), tile)
        far = pl.ds(pl.multiple_of(local_g + step * tile, tile), tile)
        real, imag = psi[:, spot], psi[:, far]
        cosines, sines = table_cos[:, spot], table_sin[:, spot]
        partial[:WATERS, :] += inner(cosines, real) - inner(sines, imag)
        partial[WATERS:, :] += inner(sines, real) + inner(cosines, imag)
        return carry

    lax.fori_loop(0, local_g // tile, project, 0)

    def own_start(upto, rows):
        start = 0
        for bit in range(upto):
            start = start + me // (1 << bit) % 2 * (rows >> (bit + 1))
        return start

    def sum_step(values, land, which, bit, between):
        rows = values.shape[0]
        half = rows >> (bit + 1)
        size = 1 << bit
        mine = me // size % 2
        start = own_start(bit, rows)
        away = pl.ds(pl.multiple_of(start + (1 - mine) * half, half), half)
        keep = pl.ds(pl.multiple_of(start + mine * half, half), half)
        spot = pl.ds(rows - 2 * half, half)
        copy = remote(
            values.at[away], land.at[spot], pair(sum_sems, which, bit), me + (1 - 2 * mine) * size
        )
        copy.start()
        between()
        copy.wait()
        values[keep, :] += land[spot, :]

    def share_step(values, which, bit, between):
        rows = values.shape[0]
        size = 1 << bit
        mine = me // size % 2
        count = rows >> (bit + 1)
        spot = pl.ds(pl.multiple_of(own_start(bit + 1, rows), count), count)
        copy = remote(
            values.at[spot],
            values.at[spot],
            pair(share_sems, which, bit),
            me + (1 - 2 * mine) * size,
        )
        copy.start()
        between()
        copy.wait()

    for bit in range(steps):
        sum_step(partial, landing, 0, bit, lambda: issue(1))
    own_rows = partial.shape[0] // parts
    own = pl.ds(pl.multiple_of(own_start(steps, partial.shape[0]), own_rows), own_rows)
    gathered[own, :] = (partial[own, :] * (1.0 / GVECS)).astype(jnp.bfloat16)
    for bit in reversed(range(steps)):
        share_step(gathered, 0, bit, lambda: issue(1))
    issue(len(units))

    for first in range(0, gathered.shape[0], tile):
        for second in range(0, bands, tile):
            part = gathered[first : first + tile, second : second + tile].astype(jnp.float32)
            turned[second : second + tile, first : first + tile] = part.T.astype(jnp.bfloat16)

    def transform(chunk):
        mine = pl.ds(pl.multiple_of(me * share, share), share)
        own_bands = pl.ds(pl.multiple_of(chunk * block + me * share, share), share)
        whole[mine, :] = psi[own_bands, :]

        def unpack_peer(turn):
            out_copy(chunk, turn).wait_recv()
            rows = pl.ds(pl.multiple_of(other(turn) * share, share), share)
            whole[rows, :local_g] = got[chunk, rows, 0, :]
            whole[rows, local_g:] = got[chunk, rows, 1, :]

        each_peer(unpack_peer)
        columns = side // tile

        def forward(step, carry):
            plane, column = step // columns, step % columns
            spot = pl.ds(pl.multiple_of(column * tile, tile), tile)
            rows = pl.ds(pl.multiple_of(plane * block, block), block)
            real = whole[:, pl.ds(pl.multiple_of(plane * side, side), side)]
            imag = whole[:, pl.ds(pl.multiple_of(local_g + plane * side, side), side)]
            cosines, sines = plane_cos[:, spot], plane_sin[:, spot]
            middle[0, rows, spot] = (product(real, cosines) - product(imag, sines)).astype(
                jnp.bfloat16
            )
            middle[1, rows, spot] = (product(real, sines) + product(imag, cosines)).astype(
                jnp.bfloat16
            )
            return carry

        lax.fori_loop(0, planes * columns, forward, 0)

        def lines(column, carry):
            spot = pl.ds(pl.multiple_of(column * tile, tile), tile)
            real, imag = middle[0, :, spot], middle[1, :, spot]
            value = potential[:, spot]
            cosines, sines = cross[0], cross[1]
            upper = (product(cosines, real) - product(sines, imag)) * value
            lower = (product(sines, real) + product(cosines, imag)) * value
            upper, lower = upper.astype(jnp.bfloat16), lower.astype(jnp.bfloat16)
            middle[0, :, spot] = (product(cosines, upper) + product(sines, lower)).astype(
                jnp.bfloat16
            )
            middle[1, :, spot] = (product(cosines, lower) - product(sines, upper)).astype(
                jnp.bfloat16
            )
            return carry

        lax.fori_loop(0, columns, lines, 0)

        def backward(step, carry):
            plane, column = step // columns, step % columns
            spot = pl.ds(pl.multiple_of(column * tile, tile), tile)
            rows = pl.ds(pl.multiple_of(plane * block, block), block)
            real, imag = middle[0, rows, :], middle[1, rows, :]
            cosines, sines = plane_cos[:, spot], plane_sin[:, spot]
            upper = pl.ds(pl.multiple_of(plane * side + column * tile, tile), tile)
            lower = pl.ds(pl.multiple_of(local_g + plane * side + column * tile, tile), tile)
            giving[chunk, :, upper] = (product(real, cosines) + product(imag, sines)).astype(
                jnp.bfloat16
            )
            giving[chunk, :, lower] = (product(imag, cosines) - product(real, sines)).astype(
                jnp.bfloat16
            )
            return carry

        lax.fori_loop(0, planes * columns, backward, 0)
        back[own_bands, :] = giving[chunk, mine, :]
        for far in range(parts // 2):
            back_copy(chunk, parts // 2 + far).start()
            if far > 0:
                back_copy(chunk, far).start()

    def near_forces():
        here, there = spots((atoms, atoms))
        same = jnp.where(here == there, 1.0, 0.0)
        offset_pick = same - jnp.where(here == there - there % 3, 1.0, 0.0)
        pull_pick = same - jnp.where(there == here - here % 3, 1.0, 0.0)
        bead, beside = spots((beads, beads))
        spring = 2.0 * jnp.where(bead == beside, 1.0, 0.0)
        spring -= jnp.where((bead + 1) % beads == beside, 1.0, 0.0)
        spring -= jnp.where((beside + 1) % beads == bead, 1.0, 0.0)
        offsets = [exact(positions[:, axis, :], offset_pick) for axis in range(3)]
        squares = offsets[0] * offsets[0] + offsets[1] * offsets[1] + offsets[2] * offsets[2]
        hydrogen = lax.broadcasted_iota(jnp.int32, squares.shape, 1) % 3 > 0
        length = jnp.sqrt(jnp.where(hydrogen, squares, 1.0))
        for axis in range(3):
            pull = -bond_stiff * (length - bond_rest) * offsets[axis] / length
            pull = jnp.where(hydrogen, pull, 0.0)
            near[axis] = exact(pull, pull_pick) - spring_stiff * exact(
                spring, positions[:, axis, :]
            )

    transform(0)

    force_sum[...] = jnp.zeros_like(force_sum)

    def local_part(step, carry):
        spot = pl.ds(pl.multiple_of(step * tile, tile), tile)
        far = pl.ds(pl.multiple_of(local_g + step * tile, tile), tile)
        kinetic = 1.0 - step_size * grid[1:2, spot]
        real, imag = psi[:, spot], psi[:, far]
        cosines, sines = table_cos[:, spot], table_sin[:, spot]
        turned_re, turned_im = turned[:, :WATERS], turned[:, WATERS:]
        strength = step_size * nonlocal_strength
        base[:, spot] = kinetic * real.astype(jnp.float32) - strength * (
            product(turned_re, cosines) + product(turned_im, sines)
        )
        base[:, far] = kinetic * imag.astype(jnp.float32) - strength * (
            product(turned_im, cosines) - product(turned_re, sines)
        )
        proj_re, proj_im = gathered[:WATERS, :], gathered[WATERS:, :]
        weighted_re = product(proj_re, real) + product(proj_im, imag)
        weighted_im = product(proj_re, imag) - product(proj_im, real)
        mixed = wave_cos[:, spot] * weighted_im + wave_sin[:, spot] * weighted_re
        force_sum[...] += lax.dot_general(
            mixed,
            grid_rows[:, spot],
            (((1,), (1,)), ((), ())),
            precision=highest,
            preferred_element_type=jnp.float32,
        )
        return carry

    lax.fori_loop(0, local_g // tile, local_part, 0)
    force_land[me] = force_sum[own_spot, :]
    each_peer(lambda turn: force_copy(turn).start())

    near_forces()
    transform(1)
    each_peer(lambda turn: force_copy(turn).wait_recv())

    def add_force(source, carry):
        return carry + force_land[source]

    strength = 2.0 * occupation * nonlocal_strength / GVECS
    total = strength * lax.fori_loop(
        0, parts, add_force, jnp.zeros(force_land.shape[1:], jnp.float32)
    )
    bead_row, bead_column = spots((beads, beads))
    mixing_column = jnp.sum(
        jnp.where(bead_row == bead_column, jnp.broadcast_to(mixing, (beads, beads)), 0.0),
        axis=1,
        keepdims=True,
    )
    for axis in range(3):
        placed = jnp.where(own_atom == 3 * own_row, total[:, axis : axis + 1], 0.0)
        placed = jnp.sum(placed, axis=0, keepdims=True)
        force_out[:, axis, :] = near[axis] + BEADS / CBEADS * (mixing_column * placed)

    def finish(chunk):
        def rows_of(turn, carry):
            @pl.when(turn > 0)
            def _():
                back_copy(chunk, turn).wait_recv()

            rows = pl.ds(
                pl.multiple_of(chunk * block + other(turn) * share, share), share
            )
            value = base[rows, :] - step_size * back[rows, :].astype(jnp.float32)
            value = value.astype(jnp.bfloat16)
            trial[0, rows, :] = value[:, :local_g]
            trial[1, rows, :] = value[:, local_g:]
            return carry

        lax.fori_loop(0, parts, rows_of, 0)

    corner_row = lax.broadcasted_iota(jnp.int32, (block, block), 0)
    corner_column = lax.broadcasted_iota(jnp.int32, (block, block), 1)

    def overlap(first, second):
        rows = pl.ds(first * block, block)
        columns = pl.ds(second * block, block)

        def even(spot):
            return inner(trial[0, rows, spot], trial[0, columns, spot]) + inner(
                trial[1, rows, spot], trial[1, columns, spot]
            )

        def odd(spot):
            return inner(trial[1, rows, spot], trial[0, columns, spot]) - inner(
                trial[0, rows, spot], trial[1, columns, spot]
            )

        margin[rows, columns] = jnp.zeros((block, block), jnp.float32)

        def add(step, carry):
            spot = pl.ds(pl.multiple_of(step * tile, tile), tile)
            if first < second:
                value = even(spot)
            elif first > second:
                value = odd(spot)
            else:
                value = jnp.where(corner_row <= corner_column, even(spot), odd(spot))
            margin[rows, columns] += value
            return carry

        lax.fori_loop(0, local_g // tile, add, 0)

    for chunk in range(CHUNKS):
        finish(chunk)
        trial_copy = pltpu.make_async_copy(
            trial.at[:, pl.ds(chunk * block, block)],
            trial_hbm.at[:, pl.ds(chunk * block, block)],
            local_sem.at[1 + chunk],
        )
        trial_copy.start()
        for first in range(chunk + 1):
            overlap(first, chunk)
            if first != chunk:
                overlap(chunk, first)

    for bit in range(steps):
        sum_step(margin, landing_two, 1, bit, lambda: None)
    start = own_start(steps, bands)
    own_rows = bands // parts
    own = pl.ds(pl.multiple_of(start, own_rows), own_rows)
    row = start + lax.broadcasted_iota(jnp.int32, (own_rows, bands), 0)
    column = lax.broadcasted_iota(jnp.int32, (own_rows, bands), 1)
    mixed_rows = jnp.where(row == column, 1.5, 0.0) - (0.5 / GVECS) * margin[own, :]
    gathered_two[own, :] = mixed_rows.astype(jnp.bfloat16)
    for bit in reversed(range(steps)):
        share_step(gathered_two, 1, bit, lambda: None)

    for first in range(0, bands, tile):
        for second in range(0, bands, tile):
            there = gathered_two[first : first + tile, second : second + tile]
            flipped = gathered_two[second : second + tile, first : first + tile]
            there = there.astype(jnp.float32)
            flipped = flipped.astype(jnp.float32).T
            row = first + lax.broadcasted_iota(jnp.int32, (tile, tile), 0)
            column = second + lax.broadcasted_iota(jnp.int32, (tile, tile), 1)
            mix_re = jnp.where(row <= column, there, flipped)
            mix_im = jnp.where(
                row > column, there, jnp.where(row < column, -flipped, jnp.zeros_like(there))
            )
            mixed_out[0, first : first + tile, second : second + tile] = mix_re.astype(
                jnp.bfloat16
            )
            mixed_out[1, first : first + tile, second : second + tile] = mix_im.astype(
                jnp.bfloat16
            )

    for chunk in range(CHUNKS):
        pltpu.make_async_copy(
            trial.at[:, pl.ds(chunk * block, block)],
            trial_hbm.at[:, pl.ds(chunk * block, block)],
            local_sem.at[1 + chunk],
        ).wait()
        each_peer(lambda turn: out_copy(chunk, turn).wait_send())
        each_peer(lambda turn: back_copy(chunk, turn).wait_send())
    each_peer(lambda turn: wave_copy(turn).wait_send())
    each_peer(lambda turn: force_copy(turn).wait_send())


def rotate_kernel(sizes, mixed, trial_hbm, out, trial, sem):
    rows, local_g = sizes
    tile = 256
    copy = pltpu.make_async_copy(trial_hbm, trial, sem.at[0])

    @pl.when(pl.program_id(0) == 0)
    def _():
        copy.start()
        copy.wait()

    mix_re, mix_im = mixed[0], mixed[1]

    def columns(step, carry):
        spot = pl.ds(pl.multiple_of(step * tile, tile), tile)
        real, imag = trial[0, :, spot], trial[1, :, spot]
        out[:, 0, spot] = (product(mix_re, real) - product(mix_im, imag)).astype(out.dtype)
        out[:, 1, spot] = (product(mix_im, real) + product(mix_re, imag)).astype(out.dtype)
        return carry

    lax.fori_loop(0, local_g // tile, columns, 0)


def rotate(mixed, trial):
    bands, local_g = trial.shape[1:]
    rows = 128
    return pl.pallas_call(
        functools.partial(rotate_kernel, (rows, local_g)),
        grid=(bands // rows,),
        out_shape=jax.ShapeDtypeStruct((bands, 2, local_g), jnp.bfloat16),
        in_specs=[
            pl.BlockSpec((2, rows, bands), lambda step: (0, step, 0)),
            pl.BlockSpec(memory_space=pl.ANY),
        ],
        out_specs=pl.BlockSpec((rows, 2, local_g), lambda step: (step, 0, 0)),
        scratch_shapes=[
            pltpu.VMEM(trial.shape, trial.dtype),
            pltpu.SemaphoreType.DMA((1,)),
        ],
        compiler_params=pltpu.CompilerParams(vmem_limit_bytes=32 * 2**20),
    )(mixed, trial)


def fused_device(positions, weights, psi, vloc):
    parts = lax.axis_size("ga")
    bands, local_g = psi.shape[1], psi.shape[3]
    side = NGRID * NGRID
    planes = local_g // side
    share = bands // (parts * CHUNKS)
    block = parts * share
    waters = positions.shape[2] // 3
    vmem = pl.BlockSpec(memory_space=pltpu.VMEM)
    anywhere = pl.BlockSpec(memory_space=pl.ANY)
    steps = parts.bit_length() - 1
    f32, bf16 = jnp.float32, jnp.bfloat16
    dma = pltpu.SemaphoreType.DMA
    trial, mixed, force = pl.pallas_call(
        functools.partial(step_kernel, (parts, bands, local_g)),
        out_shape=(
            jax.ShapeDtypeStruct((2, bands, local_g), bf16),
            jax.ShapeDtypeStruct((2, bands, bands), bf16),
            jax.ShapeDtypeStruct(positions.shape, f32),
        ),
        in_specs=[anywhere, vmem, vmem, vmem, vmem, vmem],
        out_specs=(anywhere, vmem, vmem),
        scratch_shapes=[
            pltpu.VMEM((bands, 2, local_g), bf16),
            pltpu.VMEM((bands, 2 * local_g), bf16),
            pltpu.VMEM((waters, 8 * NGRID), f32),
            pltpu.VMEM((8, local_g), f32),
            pltpu.VMEM((3,) + positions.shape[::2], f32),
            pltpu.VMEM((WATERS, 8 * NGRID), f32),
            pltpu.VMEM((WATERS, local_g), bf16),
            pltpu.VMEM((WATERS, local_g), bf16),
            pltpu.VMEM((WATERS, local_g), f32),
            pltpu.VMEM((WATERS, local_g), f32),
            pltpu.VMEM((side, side), bf16),
            pltpu.VMEM((side, side), bf16),
            pltpu.VMEM((planes * block, side), f32),
            pltpu.VMEM((CHUNKS, block, 2, local_g), bf16),
            pltpu.VMEM((block, 2 * local_g), bf16),
            pltpu.VMEM((2, planes * block, side), bf16),
            pltpu.VMEM((CHUNKS, block, 2 * local_g), bf16),
            pltpu.VMEM((bands, 2 * local_g), bf16),
            pltpu.VMEM((bands, 2 * local_g), f32),
            pltpu.VMEM((2, bands, local_g), bf16),
            pltpu.VMEM((2 * WATERS, bands), f32),
            pltpu.VMEM((2 * WATERS, bands), f32),
            pltpu.VMEM((2 * WATERS, bands), bf16),
            pltpu.VMEM((bands, 2 * WATERS), bf16),
            pltpu.VMEM((bands, bands), f32),
            pltpu.VMEM((bands, bands), f32),
            pltpu.VMEM((bands, bands), bf16),
            pltpu.VMEM((WATERS, 128), f32),
            pltpu.VMEM((parts, waters, 128), f32),
            pltpu.VMEM((128, local_g), f32),
            dma((1 + CHUNKS,)),
            dma((2, parts)),
            dma((2, CHUNKS, parts)),
            dma((2, CHUNKS, parts)),
            dma((2, parts)),
            dma((2, 2, steps)),
            dma((2, 2, steps)),
        ],
        compiler_params=pltpu.CompilerParams(
            collective_id=0, has_side_effects=True, vmem_limit_bytes=67043328
        ),
    )(
        psi[0],
        positions,
        weights,
        trig_tables(),
        cross_tables(parts, planes, share),
        vloc,
    )
    return (rotate(mixed, trial)[None], force)


def step_device(positions, weights, psi, vloc):
    parts = lax.axis_size("ga")
    bands, local_g = psi.shape[1], psi.shape[3]
    side = NGRID * NGRID
    fits = (
        local_g % side == 0
        and parts & (parts - 1) == 0
        and parts >= 4
        and bands % (parts * CHUNKS * 16) == 0
        and bands // CHUNKS % 256 == 0
        and bands * local_g <= 2**20
    )
    if fits:
        return fused_device(positions, weights, psi, vloc)
    return per_device(positions, weights, psi, vloc)


def solution(mesh):
    placed = (P("rep", None, "ga"), P(), P("rep", None, None, "ga"), P("rep", None))
    return jax.shard_map(
        step_device,
        mesh=mesh,
        in_specs=placed,
        out_specs=(P("rep", None, None, "ga"), P("rep", None, "ga")),
        check_vma=False,
    )
```

```python
import functools

import jax
import jax.numpy as jnp
import numpy as np
from jax import lax
from jax.experimental import pallas as pl
from jax.experimental.pallas import tpu as pltpu
from jax.sharding import PartitionSpec as P

BEADS = 32
CBEADS = 1
WATERS = 256
NGRID = 32
GVECS = 32768
CHUNKS = 2


box_length = 20.0
bond_stiff = 0.5
bond_rest = 1.8
spring_stiff = 2.0
width_square = 0.09
step_size = 0.02
nonlocal_strength = 250.0
occupation = 2.0
highest = lax.Precision.HIGHEST


def frequency(index, count):
    signed = jnp.where(index < count // 2, index, index - count)
    return signed.astype(jnp.float32) * (2.0 * jnp.pi / box_length)


def field_forces(positions):
    oxygen = positions[:, :, 0::3]
    toward_one = positions[:, :, 1::3] - oxygen
    toward_two = positions[:, :, 2::3] - oxygen

    def stretch(offset):
        length = jnp.sqrt(jnp.sum(offset * offset, axis=1, keepdims=True))
        return -bond_stiff * (length - bond_rest) * offset / length

    pull_one = stretch(toward_one)
    pull_two = stretch(toward_two)
    bonds = jnp.stack([-(pull_one + pull_two), pull_one, pull_two], axis=3).reshape(positions.shape)
    springs = 2.0 * positions - jnp.roll(positions, 1, axis=0) - jnp.roll(positions, -1, axis=0)
    return bonds - spring_stiff * springs


def inner(left_mat, right_mat):
    return lax.dot_general(
        left_mat, right_mat, (((1,), (1,)), ((), ())), preferred_element_type=jnp.float32
    )


def real_form(freq_index, group_index):
    product = freq_index[:, None] * freq_index[None, :] % NGRID
    angle = product.astype(jnp.float32) * (2.0 * jnp.pi / NGRID)
    same = (group_index[:, None] == group_index[None, :]).astype(jnp.float32)
    cosines = jnp.cos(angle) * same
    sines = jnp.sin(angle) * same
    return jnp.stack([jnp.stack([cosines, sines], 1), jnp.stack([-sines, cosines], 1)], 0)


def plane_table():
    index = jnp.arange(NGRID, dtype=jnp.int32)
    return real_form(index, jnp.zeros_like(index))


def block_table(length, within):
    index = jnp.arange(length, dtype=jnp.int32)
    if within:
        return real_form(index % NGRID, index // NGRID)
    return real_form(index // NGRID, index % NGRID)


def grid_sum(psi, vloc, parts):
    bands = psi.shape[1]
    local_g = psi.shape[3]
    x_table = plane_table()
    z_table = block_table(local_g, True)
    y_table = block_table(NGRID * NGRID, False)
    grid_potential = vloc[0].reshape(1, 1, NGRID, NGRID * NGRID)
    grouped_raw = psi[0].reshape(parts, bands // parts, 2, local_g)
    planes = lax.all_to_all(grouped_raw, "ga", split_axis=0, concat_axis=3, tiled=True)
    band_count = planes.shape[1]
    blocks_whole = planes.astype(jnp.float32).reshape(band_count, 2, NGRID**3 // local_g, local_g)
    along_z = jnp.einsum("mckp,cpdq->mdkq", blocks_whole, z_table, precision=highest) * (
        1.0 / NGRID
    )
    grid = along_z.reshape(band_count, 2, NGRID, NGRID * NGRID)
    grid = jnp.einsum("mcxr,cxdw->mdwr", grid, x_table, precision=highest) * (1.0 / NGRID)
    grid = jnp.einsum("mcxp,cpdq->mdxq", grid, y_table, precision=highest) * (1.0 / NGRID)
    grid = grid * grid_potential
    grid = jnp.einsum("mdxq,cpdq->mcxp", grid, y_table, precision=highest)
    grid = jnp.einsum("mdwr,cxdw->mcxr", grid, x_table, precision=highest)
    returning = grid.reshape(1, band_count, 2, NGRID**3)
    returned = lax.all_to_all(
        returning.astype(jnp.bfloat16), "ga", split_axis=3, concat_axis=0, tiled=True
    ).astype(returning.dtype)
    returned = returned.reshape(bands, 2, local_g)
    potential = jnp.einsum("bdq,cpdq->bcp", returned, z_table, precision=highest)
    return potential[:, 0], potential[:, 1]


def plane_rotation():
    small = np.arange(NGRID)
    angle = small[:, None] * small[None, :] % NGRID * (2.0 * np.pi / NGRID)
    side = NGRID * NGRID
    wave = np.kron(np.exp(1j * angle), np.exp(1j * angle))
    real, imag = np.real(wave), np.imag(wave)
    table = np.stack([np.stack([real, -imag], 1), np.stack([imag, real], 1)], 1)
    return jnp.asarray(table.reshape(2 * side, 2 * side).astype(np.float32), jnp.bfloat16)


def line_rotation(group):
    small = np.arange(NGRID)
    angle = small[:, None] * small[None, :] % NGRID * (2.0 * np.pi / NGRID)
    real, imag = np.cos(angle), np.sin(angle)
    form = np.stack([np.stack([real, -imag], 2), np.stack([imag, real], 2)], 1)
    same = np.eye(group)
    table = form[:, None, :, :, None, :] * same[None, :, None, None, :, None]
    size = 2 * NGRID * group
    return jnp.asarray(table.reshape(size, size).astype(np.float32), jnp.bfloat16)


def plane_out(psi, parts, plane_table, offset):
    bands = psi.shape[1]
    side = NGRID * NGRID
    planes = psi.shape[3] // side
    chunk = bands // CHUNKS
    pieces = []
    for first in range(0, bands, chunk):
        part = lax.dynamic_slice_in_dim(psi[0], first + offset, chunk, axis=0).reshape(chunk, 2, planes, side)
        part = part.transpose(2, 0, 1, 3).reshape(planes, chunk, 2 * side)
        pieces.append(
            jnp.stack(
                [
                    jnp.einsum(
                        "qk,bk->qb", plane_table, part[p], preferred_element_type=jnp.float32
                    )
                    .astype(jnp.bfloat16)
                    .reshape(parts, 2 * side // parts, chunk)
                    for p in range(planes)
                ],
                1,
            )
        )
    return pieces


def exchange(piece):
    return lax.all_to_all(piece, "ga", split_axis=0, concat_axis=0, tiled=True)


def line_action(vloc, parts):
    side = NGRID * NGRID
    points = side // parts
    group = min(8, points)
    groups = points // group
    line_table = line_rotation(group)
    start = lax.axis_index("ga") * points
    own = lax.dynamic_slice_in_dim(vloc[0].reshape(NGRID, side), start, points, axis=1)
    own = own.reshape(NGRID, groups, group).transpose(1, 0, 2) * (1.0 / (NGRID * side))
    own = jnp.broadcast_to(own[..., None], (groups, NGRID, group, 2)).reshape(groups, -1, 1)
    scaled = (own * line_table.astype(jnp.float32)).astype(jnp.bfloat16)
    return jnp.einsum(
        "ea,gec->gac", line_table, scaled, preferred_element_type=jnp.float32
    ).astype(jnp.bfloat16)


def line_step(action, lines):
    parts, planes, rows, chunk = lines.shape
    groups = action.shape[0]
    lines = lines.reshape(parts * planes, groups, rows // groups, chunk)
    lines = lines.transpose(1, 0, 2, 3).reshape(groups, -1, chunk)
    lines = jnp.einsum(
        "gac,gcb->gab", action, lines, preferred_element_type=jnp.float32
    ).astype(jnp.bfloat16)
    lines = lines.reshape(groups, parts * planes, rows // groups, chunk).transpose(1, 0, 2, 3)
    return lines.reshape(parts, planes, rows, chunk)


def plane_back(backs, plane_table):
    side = NGRID * NGRID
    reals, imags = [], []
    for back in backs:
        chunk = back.shape[3]
        whole = [
            jnp.einsum(
                "qb,qk->bk",
                back[:, p].reshape(2 * side, chunk),
                plane_table,
                preferred_element_type=jnp.float32,
            )
            for p in range(back.shape[1])
        ]
        reals.append(jnp.concatenate([w[:, :side] for w in whole], 1))
        imags.append(jnp.concatenate([w[:, side:] for w in whole], 1))
    return jnp.concatenate(reals, 0), jnp.concatenate(imags, 0)


def waves(oxygens, gvectors, profile):
    local_g = profile.shape[0]
    side = NGRID * NGRID
    if local_g % side:
        phases = jnp.einsum("ai,ag->ig", oxygens, gvectors, precision=highest)
        return profile * jnp.cos(phases), profile * jnp.sin(phases)
    spots = oxygens.T
    flat = spots[:, 1:2] * gvectors[1:2, :side] + spots[:, 2:3] * gvectors[2:3, :side]
    flat_cos, flat_sin = jnp.cos(flat), jnp.sin(flat)
    along = spots[:, 0:1] * gvectors[0:1, ::side]
    along_cos, along_sin = jnp.cos(along), jnp.sin(along)
    cosines, sines = [], []
    for p in range(local_g // side):
        c, s = along_cos[:, p : p + 1], along_sin[:, p : p + 1]
        cosines.append(c * flat_cos - s * flat_sin)
        sines.append(s * flat_cos + c * flat_sin)
    return profile * jnp.concatenate(cosines, 1), profile * jnp.concatenate(sines, 1)


def per_device(positions, weights, psi, vloc):
    near_forces = field_forces(positions)
    weight_float = weights.astype(jnp.float32)
    mixing = weight_float / jnp.sum(weight_float, axis=1, keepdims=True)
    centres = jnp.einsum("cj,jan->can", mixing, positions, precision=highest)
    parts = lax.axis_size("ga")
    near_oxygen = centres[0][:, 0::3]
    own_waters = near_oxygen.shape[1]
    everyone = lax.dynamic_update_slice(
        jnp.zeros((3, own_waters * parts), jnp.float32),
        near_oxygen,
        (0, lax.axis_index("ga") * own_waters),
    )
    oxygens = lax.psum(everyone, "ga")
    side = NGRID * NGRID
    whole_planes = psi.shape[3] % side == 0 and side % parts == 0
    if whole_planes:
        plane_table = plane_rotation()
        pieces = plane_out(psi, parts, plane_table, (oxygens[0, 0] * 0.0).astype(jnp.int32))
        lines = [exchange(piece) for piece in pieces]
        action = line_action(vloc, parts)
    bands = psi.shape[1]
    local_g = psi.shape[3]
    flat_index = lax.axis_index("ga") * local_g + jnp.arange(local_g, dtype=jnp.int32)
    gvectors = jnp.stack(
        [
            frequency(flat_index // (NGRID * NGRID), NGRID),
            frequency(flat_index // NGRID % NGRID, NGRID),
            frequency(flat_index % NGRID, NGRID),
        ]
    )
    square = jnp.sum(gvectors * gvectors, axis=0)
    profile = jnp.exp(-0.5 * width_square * square)
    kinetic = 0.5 * square
    wave_cos, wave_sin = waves(oxygens, gvectors, profile)
    table = jnp.concatenate(
        [jnp.concatenate([wave_cos, -wave_sin], 1), jnp.concatenate([wave_sin, wave_cos], 1)], 0
    ).astype(jnp.bfloat16)
    wavefunc = psi[0].reshape(bands, 2 * local_g)
    partial_proj = (inner(table, wavefunc) * (1.0 / GVECS)).reshape(2, WATERS, bands)
    share = lax.psum_scatter(partial_proj, "ga", scatter_dimension=1, tiled=True).astype(
        jnp.bfloat16
    )
    table_blocks = table.reshape(2 * WATERS, 2 * local_g)
    copies = jnp.broadcast_to(share[None], (parts,) + share.shape)
    if whole_planes:
        lines[-1], copies = lax.optimization_barrier((lines[-1], copies))
    all_proj = lax.all_to_all(copies, "ga", split_axis=0, concat_axis=0, tiled=True)
    if whole_planes:
        moved = [line_step(action, line) for line in lines]
        moved[0], all_proj = lax.optimization_barrier((moved[0], all_proj))
        backs = [exchange(piece) for piece in moved]
    all_proj = all_proj.transpose(1, 0, 2, 3).reshape(2 * WATERS, bands)
    nonlocal_term = jnp.einsum(
        "ib,ig->bg", all_proj, table_blocks, preferred_element_type=jnp.float32
    )
    crossed = jnp.dot(all_proj, wavefunc, preferred_element_type=jnp.float32)
    weighted_re = crossed[:WATERS, :local_g] + crossed[WATERS:, local_g:]
    weighted_im = crossed[:WATERS, local_g:] - crossed[WATERS:, :local_g]
    mixed_wave = wave_cos * weighted_im + wave_sin * weighted_re
    force_part = (
        2.0
        * occupation
        * nonlocal_strength
        / GVECS
        * jnp.einsum("ag,ig->ai", gvectors, mixed_wave, precision=highest)
    )
    force_rows = force_part.reshape(3, parts, own_waters).transpose(1, 0, 2)
    force_rows = force_rows.reshape(parts, 1, 3 * own_waters)
    force_rows = jnp.pad(force_rows, ((0, 0), (0, 0), (0, bands - 3 * own_waters)))
    wave_float = psi[0].astype(jnp.float32)
    if whole_planes:
        potential = plane_back(backs, plane_table)
    else:
        potential = grid_sum(psi, vloc, parts)
    hamil_re = (
        kinetic * wave_float[:, 0]
        + potential[0]
        + nonlocal_strength * nonlocal_term[:, :local_g]
    )
    hamil_im = (
        kinetic * wave_float[:, 1]
        + potential[1]
        + nonlocal_strength * nonlocal_term[:, local_g:]
    )
    trial_re = (wave_float[:, 0] - step_size * hamil_re).astype(jnp.bfloat16)
    trial_im = (wave_float[:, 1] - step_size * hamil_im).astype(jnp.bfloat16)
    row = lax.broadcasted_iota(jnp.int32, (bands, bands), 0)
    column = lax.broadcasted_iota(jnp.int32, (bands, bands), 1)
    even = inner(trial_re, trial_re) + inner(trial_im, trial_im)
    odd = inner(trial_im, trial_re) - inner(trial_re, trial_im)
    packed = jnp.where(row <= column, even, odd) * (1.0 / GVECS)
    shares = lax.all_to_all(
        jnp.concatenate([packed.reshape(parts, bands // parts, bands), force_rows], 1),
        "ga",
        split_axis=0,
        concat_axis=0,
        tiled=True,
    )
    sums = jnp.sum(shares, axis=0)
    oxygen_force = sums[-1, : 3 * own_waters].reshape(3, own_waters)
    hydrogen_zero = jnp.zeros_like(oxygen_force)
    dft_forces = [jnp.stack([oxygen_force, hydrogen_zero, hydrogen_zero], axis=2).reshape(3, -1)]
    own_rows = lax.broadcasted_iota(jnp.int32, (bands // parts, bands), 0) + lax.axis_index(
        "ga"
    ) * (bands // parts)
    own_columns = lax.broadcasted_iota(jnp.int32, (bands // parts, bands), 1)
    mixed_rows = jnp.where(own_rows == own_columns, 1.5, 0.0) - 0.5 * sums[:-1]
    mixed = lax.all_gather(mixed_rows.astype(jnp.bfloat16), "ga", axis=0, tiled=True)
    turned = mixed.T
    mix_re = jnp.where(row <= column, mixed, turned)
    mix_im = jnp.where(row > column, mixed, jnp.where(row < column, -turned, jnp.zeros_like(turned)))
    both = jnp.concatenate([trial_re, trial_im], 0)
    new_re = jnp.dot(
        jnp.concatenate([mix_re, -mix_im], 1), both, preferred_element_type=jnp.float32
    ).astype(jnp.bfloat16)
    new_im = jnp.dot(
        jnp.concatenate([mix_im, mix_re], 1), both, preferred_element_type=jnp.float32
    ).astype(jnp.bfloat16)
    new_waves = [jnp.stack([new_re, new_im], 1)]
    contracted_force = jnp.einsum("cj,can->jan", mixing, jnp.stack(dft_forces), precision=highest)
    bead_forces = near_forces + BEADS / CBEADS * contracted_force
    return (jnp.stack(new_waves), bead_forces)


def product(left_mat, right_mat):
    return jnp.dot(left_mat, right_mat, preferred_element_type=jnp.float32)


def trig_tables():
    small = np.arange(NGRID)
    angle = small[:, None] * small[None, :] % NGRID * (2.0 * np.pi / NGRID)
    cosines, sines = np.cos(angle), np.sin(angle)
    rows = [np.repeat(cosines, NGRID, 1), np.repeat(sines, NGRID, 1)]
    rows += [np.tile(cosines, (1, NGRID)), np.tile(sines, (1, NGRID))]
    return jnp.asarray(np.stack(rows), jnp.float32)


def cross_tables(parts, planes, share):
    spot = (np.arange(parts)[None, :] * planes + np.arange(planes)[:, None]).reshape(-1)
    angle = spot[:, None] * spot[None, :] % NGRID * (2.0 * np.pi / NGRID)
    same = np.eye(share)
    pair = np.stack([np.kron(np.cos(angle), same), np.kron(np.sin(angle), same)])
    return jnp.asarray(pair.astype(np.float32), jnp.bfloat16)


def step_kernel(
    sizes,
    psi_hbm,
    positions,
    weights,
    trig,
    cross,
    vloc,
    psi_out,
    force_out,
    raw,
    psi,
    own_waves,
    grid,
    near,
    all_waves,
    table_cos,
    table_sin,
    wave_cos,
    wave_sin,
    plane_cos,
    plane_sin,
    potential,
    got,
    whole,
    middle,
    giving,
    back,
    base,
    trial,
    partial,
    landing,
    gathered,
    turned,
    margin,
    landing_two,
    gathered_two,
    mixed,
    force_sum,
    force_land,
    grid_rows,
    local_sem,
    wave_sems,
    out_sems,
    back_sems,
    force_sems,
    sum_sems,
    share_sems,
):
    parts, bands, local_g = sizes
    side = NGRID * NGRID
    planes = local_g // side
    share = bands // (parts * CHUNKS)
    block = parts * share
    steps = parts.bit_length() - 1
    tile = 256
    me = lax.axis_index("ga")

    def other(turn):
        total = 0
        for bit in range(steps):
            size = 1 << bit
            total = total + (me // size + turn // size) % 2 * size
        return total

    def remote(source, target, sems, peer):
        return pltpu.make_async_remote_copy(
            src_ref=source,
            dst_ref=target,
            send_sem=sems[0],
            recv_sem=sems[1],
            device_id={"ga": peer},
            device_id_type=pl.DeviceIdType.MESH,
        )

    def each_peer(act):
        def body(turn, carry):
            act(turn)
            return carry

        lax.fori_loop(1, parts, body, 0)

    def pair(sems, *spot):
        return sems.at[(0,) + spot], sems.at[(1,) + spot]

    def wave_copy(turn):
        waters = own_waves.shape[0]
        spot = pl.ds(pl.multiple_of(me * waters, waters), waters)
        return remote(own_waves, all_waves.at[spot], pair(wave_sems, turn), other(turn))

    def out_copy(chunk, turn):
        peer = other(turn)
        source = pl.ds(pl.multiple_of(chunk * block + peer * share, share), share)
        target = pl.ds(pl.multiple_of(me * share, share), share)
        return remote(
            psi_hbm.at[source], got.at[chunk, target], pair(out_sems, chunk, turn), peer
        )

    def back_copy(chunk, turn):
        peer = other(turn)
        source = pl.ds(pl.multiple_of(peer * share, share), share)
        target = pl.ds(pl.multiple_of(chunk * block + me * share, share), share)
        return remote(
            giving.at[chunk, source], back.at[target], pair(back_sems, chunk, turn), peer
        )

    def force_copy(turn):
        peer = other(turn)
        waters = own_waves.shape[0]
        source = pl.ds(pl.multiple_of(peer * waters, waters), waters)
        return remote(
            force_sum.at[source], force_land.at[me], pair(force_sems, turn), peer
        )

    local_psi = pltpu.make_async_copy(psi_hbm, raw, local_sem.at[0])
    local_psi.start()
    barrier = pltpu.get_barrier_semaphore()

    def greet(turn):
        pl.semaphore_signal(
            barrier, inc=1, device_id={"ga": other(turn)}, device_id_type=pl.DeviceIdType.MESH
        )

    each_peer(greet)
    waters = own_waves.shape[0]
    atoms = positions.shape[2]
    beads = positions.shape[0]

    def exact(left_mat, right_mat, right_axis=0):
        return lax.dot_general(
            left_mat,
            right_mat,
            (((1,), (right_axis,)), ((), ())),
            precision=highest,
            preferred_element_type=jnp.float32,
        )

    def spots(shape):
        return lax.broadcasted_iota(jnp.int32, shape, 0), lax.broadcasted_iota(jnp.int32, shape, 1)

    weight_row = weights[...].astype(jnp.float32)
    mixing = weight_row / jnp.sum(weight_row, axis=1, keepdims=True)
    wave_row, wave_lane = spots(own_waves.shape)
    own_row, own_atom = spots((waters, atoms))
    oxygen_pick = jnp.where(own_atom == 3 * own_row, 1.0, 0.0)
    spokes = frequency(wave_lane % NGRID, NGRID)
    angles = jnp.zeros(own_waves.shape, jnp.float32)
    for axis in range(3):
        centre = exact(jnp.broadcast_to(mixing, (8, beads)), positions[:, axis, :])
        column = exact(oxygen_pick, centre, 1)[:, 0:1]
        angles += column * jnp.where(wave_lane // (2 * NGRID) == axis, spokes, 0.0)
    own_waves[...] = jnp.where(wave_lane // NGRID % 2 == 0, jnp.cos(angles), jnp.sin(angles))
    own_spot = pl.ds(pl.multiple_of(me * waters, waters), waters)
    all_waves[own_spot, :] = own_waves[...]
    pl.semaphore_wait(barrier, parts - 1)

    units = [(chunk, far) for chunk in range(CHUNKS) for far in range(parts // 2)]
    queue = list(units)

    def issue(count):
        for _ in range(count):
            if queue:
                chunk, far = queue.pop(0)
                out_copy(chunk, parts // 2 + far).start()
                if far > 0:
                    out_copy(chunk, far).start()

    each_peer(lambda turn: wave_copy(turn).start())
    issue(2)

    flat_index = me * local_g + lax.broadcasted_iota(jnp.int32, (1, local_g), 1)
    gvectors = [
        frequency(flat_index // side, NGRID),
        frequency(flat_index // NGRID % NGRID, NGRID),
        frequency(flat_index % NGRID, NGRID),
    ]
    square = gvectors[0] * gvectors[0] + gvectors[1] * gvectors[1] + gvectors[2] * gvectors[2]
    grid[0:1, :] = jnp.exp(-0.5 * width_square * square)
    grid[1:2, :] = 0.5 * square
    grid_rows[...] = jnp.zeros_like(grid_rows)
    for axis in range(3):
        grid_rows[axis : axis + 1, :] = gvectors[axis]

    def plane_rows(row, carry):
        spot = pl.ds(pl.multiple_of(row * NGRID, NGRID), NGRID)
        across_cos, across_sin = trig[0, pl.ds(row, 1), :], trig[1, pl.ds(row, 1), :]
        plane_cos[spot, :] = (across_cos * trig[2] - across_sin * trig[3]).astype(jnp.bfloat16)
        plane_sin[spot, :] = (across_sin * trig[2] + across_cos * trig[3]).astype(jnp.bfloat16)
        return carry

    lax.fori_loop(0, NGRID, plane_rows, 0)

    def potential_rows(spot, carry):
        plane = spot % planes * parts + spot // planes
        rows = pl.ds(pl.multiple_of(plane * share, share), share)
        value = vloc[:, pl.ds(pl.multiple_of(spot * side, side), side)] * (1.0 / NGRID**3)
        potential[rows, :] = jnp.broadcast_to(value, (share, side))
        return carry

    lax.fori_loop(0, NGRID, potential_rows, 0)

    strip = 16

    def unpack_rows(step, carry):
        rows = pl.ds(pl.multiple_of(step * strip, strip), strip)
        psi[rows, :local_g] = raw[rows, 0, :]
        psi[rows, local_g:] = raw[rows, 1, :]
        return carry

    local_psi.wait()
    lax.fori_loop(0, bands // strip, unpack_rows, 0)
    each_peer(lambda turn: wave_copy(turn).wait_recv())
    lane = lax.broadcasted_iota(jnp.int32, all_waves.shape, 1)
    line = lax.broadcasted_iota(jnp.int32, (all_waves.shape[1], tile), 0)
    place = lax.broadcasted_iota(jnp.int32, (all_waves.shape[1], tile), 1)

    def pick(first, spot):
        return jnp.where(line == first * NGRID + spot, 1.0, 0.0)

    def spread(first, spot):
        return lax.dot_general(
            all_waves[...],
            pick(first, spot),
            (((1,), (0,)), ((), ())),
            precision=highest,
            preferred_element_type=jnp.float32,
        )

    def table_tile(step, carry):
        first = step * tile
        flat = first + place
        rise, along = flat // NGRID, flat % NGRID
        rise_cos, rise_sin = spread(2, rise), spread(3, rise)
        long_cos, long_sin = spread(4, along), spread(5, along)
        flat_cos = rise_cos * long_cos - rise_sin * long_sin
        flat_sin = rise_sin * long_cos + rise_cos * long_sin
        for plane in range(planes):
            level = me * planes + plane
            c = jnp.sum(jnp.where(lane == level, all_waves[...], 0.0), axis=1, keepdims=True)
            s = jnp.sum(
                jnp.where(lane == level + NGRID, all_waves[...], 0.0), axis=1, keepdims=True
            )
            spot = pl.ds(pl.multiple_of(plane * side + first, tile), tile)
            profile = grid[0:1, spot]
            full_cos = profile * (c * flat_cos - s * flat_sin)
            full_sin = profile * (s * flat_cos + c * flat_sin)
            wave_cos[:, spot] = full_cos
            wave_sin[:, spot] = full_sin
            table_cos[:, spot] = full_cos.astype(jnp.bfloat16)
            table_sin[:, spot] = full_sin.astype(jnp.bfloat16)
        return carry

    lax.fori_loop(0, side // tile, table_tile, 0)
    partial[...] = jnp.zeros_like(partial)

    def project(step, carry):
        spot = pl.ds(pl.multiple_of(step * tile, tile), tile)
        far = pl.ds(pl.multiple_of(local_g + step * tile, tile), tile)
        real, imag = psi[:, spot], psi[:, far]
        cosines, sines = table_cos[:, spot], table_sin[:, spot]
        partial[:WATERS, :] += inner(cosines, real) - inner(sines, imag)
        partial[WATERS:, :] += inner(sines, real) + inner(cosines, imag)
        return carry

    lax.fori_loop(0, local_g // tile, project, 0)

    straight = list(range(steps))
    crossed = [0] + straight[2:] + [1]
    narrow = bands // 2
    single = [(0, straight, pl.ds(0, bands))]
    double = [(1, straight, pl.ds(0, narrow)), (2, crossed, pl.ds(narrow, narrow))]

    def own_start(order, upto, rows):
        start = 0
        for place, bit in enumerate(order[:upto]):
            start = start + me // (1 << bit) % 2 * (rows >> (place + 1))
        return start

    def partner(bit):
        size = 1 << bit
        mine = me // size % 2
        return mine, me + (1 - 2 * mine) * size

    def sum_step(values, land, halves, place, between):
        rows = values.shape[0]
        half = rows >> (place + 1)
        spot = pl.ds(rows - 2 * half, half)
        pending = []
        for which, order, columns in halves:
            mine, peer = partner(order[place])
            start = own_start(order, place, rows)
            away = pl.ds(pl.multiple_of(start + (1 - mine) * half, half), half)
            keep = pl.ds(pl.multiple_of(start + mine * half, half), half)
            copy = remote(
                values.at[away, columns],
                land.at[spot, columns],
                pair(sum_sems, which, place),
                peer,
            )
            copy.start()
            pending.append((copy, keep, columns))
        between()
        for copy, keep, columns in pending:
            copy.wait()
            values[keep, columns] += land[spot, columns]

    def share_step(values, halves, place, between):
        rows = values.shape[0]
        count = rows >> (place + 1)
        pending = []
        for which, order, columns in halves:
            _, peer = partner(order[place])
            spot = pl.ds(pl.multiple_of(own_start(order, place + 1, rows), count), count)
            copy = remote(
                values.at[spot, columns],
                values.at[spot, columns],
                pair(share_sems, which, place),
                peer,
            )
            copy.start()
            pending.append(copy)
        between()
        for copy in pending:
            copy.wait()

    for bit in range(steps):
        sum_step(partial, landing, single, bit, lambda: issue(1))
    own_rows = partial.shape[0] // parts
    own = pl.ds(pl.multiple_of(own_start(straight, steps, partial.shape[0]), own_rows), own_rows)
    gathered[own, :] = (partial[own, :] * (1.0 / GVECS)).astype(jnp.bfloat16)
    for bit in reversed(range(steps)):
        share_step(gathered, single, bit, lambda: issue(1))
    issue(len(units))

    for first in range(0, gathered.shape[0], tile):
        for second in range(0, bands, tile):
            part = gathered[first : first + tile, second : second + tile].astype(jnp.float32)
            turned[second : second + tile, first : first + tile] = part.T.astype(jnp.bfloat16)

    def transform(chunk):
        mine = pl.ds(pl.multiple_of(me * share, share), share)
        own_bands = pl.ds(pl.multiple_of(chunk * block + me * share, share), share)
        whole[mine, :] = psi[own_bands, :]

        def unpack_peer(turn):
            out_copy(chunk, turn).wait_recv()
            rows = pl.ds(pl.multiple_of(other(turn) * share, share), share)
            whole[rows, :local_g] = got[chunk, rows, 0, :]
            whole[rows, local_g:] = got[chunk, rows, 1, :]

        each_peer(unpack_peer)
        columns = side // tile

        def forward(step, carry):
            plane, column = step // columns, step % columns
            spot = pl.ds(pl.multiple_of(column * tile, tile), tile)
            rows = pl.ds(pl.multiple_of(plane * block, block), block)
            real = whole[:, pl.ds(pl.multiple_of(plane * side, side), side)]
            imag = whole[:, pl.ds(pl.multiple_of(local_g + plane * side, side), side)]
            cosines, sines = plane_cos[:, spot], plane_sin[:, spot]
            middle[0, rows, spot] = (product(real, cosines) - product(imag, sines)).astype(
                jnp.bfloat16
            )
            middle[1, rows, spot] = (product(real, sines) + product(imag, cosines)).astype(
                jnp.bfloat16
            )
            return carry

        lax.fori_loop(0, planes * columns, forward, 0)

        def lines(column, carry):
            spot = pl.ds(pl.multiple_of(column * tile, tile), tile)
            real, imag = middle[0, :, spot], middle[1, :, spot]
            value = potential[:, spot]
            cosines, sines = cross[0], cross[1]
            upper = (product(cosines, real) - product(sines, imag)) * value
            lower = (product(sines, real) + product(cosines, imag)) * value
            upper, lower = upper.astype(jnp.bfloat16), lower.astype(jnp.bfloat16)
            middle[0, :, spot] = (product(cosines, upper) + product(sines, lower)).astype(
                jnp.bfloat16
            )
            middle[1, :, spot] = (product(cosines, lower) - product(sines, upper)).astype(
                jnp.bfloat16
            )
            return carry

        lax.fori_loop(0, columns, lines, 0)

        def backward(step, carry):
            plane, column = step // columns, step % columns
            spot = pl.ds(pl.multiple_of(column * tile, tile), tile)
            rows = pl.ds(pl.multiple_of(plane * block, block), block)
            real, imag = middle[0, rows, :], middle[1, rows, :]
            cosines, sines = plane_cos[:, spot], plane_sin[:, spot]
            upper = pl.ds(pl.multiple_of(plane * side + column * tile, tile), tile)
            lower = pl.ds(pl.multiple_of(local_g + plane * side + column * tile, tile), tile)
            giving[chunk, :, upper] = (product(real, cosines) + product(imag, sines)).astype(
                jnp.bfloat16
            )
            giving[chunk, :, lower] = (product(imag, cosines) - product(real, sines)).astype(
                jnp.bfloat16
            )
            return carry

        lax.fori_loop(0, planes * columns, backward, 0)
        back[own_bands, :] = giving[chunk, mine, :]
        for far in range(parts // 2):
            back_copy(chunk, parts // 2 + far).start()
            if far > 0:
                back_copy(chunk, far).start()

    def near_forces():
        here, there = spots((atoms, atoms))
        same = jnp.where(here == there, 1.0, 0.0)
        offset_pick = same - jnp.where(here == there - there % 3, 1.0, 0.0)
        pull_pick = same - jnp.where(there == here - here % 3, 1.0, 0.0)
        bead, beside = spots((beads, beads))
        spring = 2.0 * jnp.where(bead == beside, 1.0, 0.0)
        spring -= jnp.where((bead + 1) % beads == beside, 1.0, 0.0)
        spring -= jnp.where((beside + 1) % beads == bead, 1.0, 0.0)
        offsets = [exact(positions[:, axis, :], offset_pick) for axis in range(3)]
        squares = offsets[0] * offsets[0] + offsets[1] * offsets[1] + offsets[2] * offsets[2]
        hydrogen = lax.broadcasted_iota(jnp.int32, squares.shape, 1) % 3 > 0
        length = jnp.sqrt(jnp.where(hydrogen, squares, 1.0))
        for axis in range(3):
            pull = -bond_stiff * (length - bond_rest) * offsets[axis] / length
            pull = jnp.where(hydrogen, pull, 0.0)
            near[axis] = exact(pull, pull_pick) - spring_stiff * exact(
                spring, positions[:, axis, :]
            )

    transform(0)

    force_sum[...] = jnp.zeros_like(force_sum)

    def local_part(step, carry):
        spot = pl.ds(pl.multiple_of(step * tile, tile), tile)
        far = pl.ds(pl.multiple_of(local_g + step * tile, tile), tile)
        kinetic = 1.0 - step_size * grid[1:2, spot]
        real, imag = psi[:, spot], psi[:, far]
        cosines, sines = table_cos[:, spot], table_sin[:, spot]
        turned_re, turned_im = turned[:, :WATERS], turned[:, WATERS:]
        strength = step_size * nonlocal_strength
        base[:, spot] = kinetic * real.astype(jnp.float32) - strength * (
            product(turned_re, cosines) + product(turned_im, sines)
        )
        base[:, far] = kinetic * imag.astype(jnp.float32) - strength * (
            product(turned_im, cosines) - product(turned_re, sines)
        )
        proj_re, proj_im = gathered[:WATERS, :], gathered[WATERS:, :]
        weighted_re = product(proj_re, real) + product(proj_im, imag)
        weighted_im = product(proj_re, imag) - product(proj_im, real)
        mixed = wave_cos[:, spot] * weighted_im + wave_sin[:, spot] * weighted_re
        force_sum[...] += lax.dot_general(
            mixed,
            grid_rows[:, spot],
            (((1,), (1,)), ((), ())),
            precision=highest,
            preferred_element_type=jnp.float32,
        )
        return carry

    lax.fori_loop(0, local_g // tile, local_part, 0)
    force_land[me] = force_sum[own_spot, :]
    each_peer(lambda turn: force_copy(turn).start())

    near_forces()
    transform(1)
    each_peer(lambda turn: force_copy(turn).wait_recv())

    def add_force(source, carry):
        return carry + force_land[source]

    strength = 2.0 * occupation * nonlocal_strength / GVECS
    total = strength * lax.fori_loop(
        0, parts, add_force, jnp.zeros(force_land.shape[1:], jnp.float32)
    )
    bead_row, bead_column = spots((beads, beads))
    mixing_column = jnp.sum(
        jnp.where(bead_row == bead_column, jnp.broadcast_to(mixing, (beads, beads)), 0.0),
        axis=1,
        keepdims=True,
    )
    for axis in range(3):
        placed = jnp.where(own_atom == 3 * own_row, total[:, axis : axis + 1], 0.0)
        placed = jnp.sum(placed, axis=0, keepdims=True)
        force_out[:, axis, :] = near[axis] + BEADS / CBEADS * (mixing_column * placed)

    def finish(chunk):
        def rows_of(turn, carry):
            @pl.when(turn > 0)
            def _():
                back_copy(chunk, turn).wait_recv()

            rows = pl.ds(
                pl.multiple_of(chunk * block + other(turn) * share, share), share
            )
            value = base[rows, :] - step_size * back[rows, :].astype(jnp.float32)
            value = value.astype(jnp.bfloat16)
            trial[0, rows, :] = value[:, :local_g]
            trial[1, rows, :] = value[:, local_g:]
            return carry

        lax.fori_loop(0, parts, rows_of, 0)

    corner_row = lax.broadcasted_iota(jnp.int32, (block, block), 0)
    corner_column = lax.broadcasted_iota(jnp.int32, (block, block), 1)

    def overlap(later, earlier):
        wide = 2 * tile
        rows = pl.ds(later * block, block)
        columns = pl.ds(earlier * block, block)
        margin[rows, columns] = jnp.zeros((block, block), jnp.float32)
        margin[columns, rows] = jnp.zeros((block, block), jnp.float32)

        def add(step, carry):
            spot = pl.ds(pl.multiple_of(step * wide, wide), wide)
            stacked = trial[:, rows, spot].reshape(2 * block, wide)
            on_real = inner(stacked, trial[0, columns, spot])
            on_imag = inner(stacked, trial[1, columns, spot])
            even = on_real[:block] + on_imag[block:]
            odd = on_real[block:] - on_imag[:block]
            if later == earlier:
                margin[rows, columns] += jnp.where(corner_row <= corner_column, even, odd)
            else:
                margin[columns, rows] += even
                margin[rows, columns] += odd
            return carry

        lax.fori_loop(0, local_g // wide, add, 0)

    for chunk in range(CHUNKS):
        finish(chunk)
        for earlier in range(chunk + 1):
            overlap(chunk, earlier)

    for place in range(steps):
        sum_step(margin, landing_two, double, place, lambda: None)
    own_rows = bands // parts
    for _, order, columns in double:
        start = own_start(order, steps, bands)
        own = pl.ds(pl.multiple_of(start, own_rows), own_rows)
        row, column = spots((own_rows, narrow))
        same = start + row == columns.start + column
        mixed_rows = jnp.where(same, 1.5, 0.0) - (0.5 / GVECS) * margin[own, columns]
        gathered_two[own, columns] = mixed_rows.astype(jnp.bfloat16)
    for place in reversed(range(steps)):
        share_step(gathered_two, double, place, lambda: None)

    for chunk in range(CHUNKS):
        rows = pl.ds(chunk * block, block)
        there = gathered_two[rows, rows].astype(jnp.float32)
        flipped = there.T
        mix_re = jnp.where(corner_row <= corner_column, there, flipped)
        mix_im = jnp.where(
            corner_row > corner_column,
            there,
            jnp.where(corner_row < corner_column, -flipped, jnp.zeros_like(there)),
        )
        mixed[chunk, :block, rows] = mix_re.astype(jnp.bfloat16)
        mixed[chunk, block:, rows] = mix_im.astype(jnp.bfloat16)
        for earlier in range(chunk):
            columns = pl.ds(earlier * block, block)
            even, odd = gathered_two[columns, rows], gathered_two[rows, columns]
            mixed[chunk, :block, columns] = even
            mixed[chunk, block:, columns] = odd
            mixed[earlier, :block, rows] = even.astype(jnp.float32).T.astype(jnp.bfloat16)
            mixed[earlier, block:, rows] = (-odd.astype(jnp.float32).T).astype(jnp.bfloat16)

    def result_copy(chunk):
        return pltpu.make_async_copy(
            got.at[chunk], psi_out.at[pl.ds(chunk * block, block)], local_sem.at[1 + chunk]
        )

    for chunk in range(CHUNKS):

        def turn_columns(step, carry):
            spot = pl.ds(pl.multiple_of(step * tile, tile), tile)
            on_real = product(mixed[chunk], trial[0, :, spot])
            on_imag = product(mixed[chunk], trial[1, :, spot])
            real = on_real[:block] - on_imag[block:]
            imag = on_real[block:] + on_imag[:block]
            got[chunk, :, 0, spot] = real.astype(jnp.bfloat16)
            got[chunk, :, 1, spot] = imag.astype(jnp.bfloat16)
            return carry

        lax.fori_loop(0, local_g // tile, turn_columns, 0)
        result_copy(chunk).start()

    for chunk in range(CHUNKS):
        result_copy(chunk).wait()
        each_peer(lambda turn: out_copy(chunk, turn).wait_send())
        each_peer(lambda turn: back_copy(chunk, turn).wait_send())
    each_peer(lambda turn: wave_copy(turn).wait_send())
    each_peer(lambda turn: force_copy(turn).wait_send())


def fused_device(positions, weights, psi, vloc):
    parts = lax.axis_size("ga")
    bands, local_g = psi.shape[1], psi.shape[3]
    side = NGRID * NGRID
    planes = local_g // side
    share = bands // (parts * CHUNKS)
    block = parts * share
    waters = positions.shape[2] // 3
    vmem = pl.BlockSpec(memory_space=pltpu.VMEM)
    anywhere = pl.BlockSpec(memory_space=pl.ANY)
    steps = parts.bit_length() - 1
    f32, bf16 = jnp.float32, jnp.bfloat16
    dma = pltpu.SemaphoreType.DMA
    psi_new, force = pl.pallas_call(
        functools.partial(step_kernel, (parts, bands, local_g)),
        out_shape=(
            jax.ShapeDtypeStruct((bands, 2, local_g), bf16),
            jax.ShapeDtypeStruct(positions.shape, f32),
        ),
        in_specs=[anywhere, vmem, vmem, vmem, vmem, vmem],
        out_specs=(anywhere, vmem),
        scratch_shapes=[
            pltpu.VMEM((bands, 2, local_g), bf16),
            pltpu.VMEM((bands, 2 * local_g), bf16),
            pltpu.VMEM((waters, 8 * NGRID), f32),
            pltpu.VMEM((8, local_g), f32),
            pltpu.VMEM((3,) + positions.shape[::2], f32),
            pltpu.VMEM((WATERS, 8 * NGRID), f32),
            pltpu.VMEM((WATERS, local_g), bf16),
            pltpu.VMEM((WATERS, local_g), bf16),
            pltpu.VMEM((WATERS, local_g), f32),
            pltpu.VMEM((WATERS, local_g), f32),
            pltpu.VMEM((side, side), bf16),
            pltpu.VMEM((side, side), bf16),
            pltpu.VMEM((planes * block, side), f32),
            pltpu.VMEM((CHUNKS, block, 2, local_g), bf16),
            pltpu.VMEM((block, 2 * local_g), bf16),
            pltpu.VMEM((2, planes * block, side), bf16),
            pltpu.VMEM((CHUNKS, block, 2 * local_g), bf16),
            pltpu.VMEM((bands, 2 * local_g), bf16),
            pltpu.VMEM((bands, 2 * local_g), f32),
            pltpu.VMEM((2, bands, local_g), bf16),
            pltpu.VMEM((2 * WATERS, bands), f32),
            pltpu.VMEM((2 * WATERS, bands), f32),
            pltpu.VMEM((2 * WATERS, bands), bf16),
            pltpu.VMEM((bands, 2 * WATERS), bf16),
            pltpu.VMEM((bands, bands), f32),
            pltpu.VMEM((bands, bands), f32),
            pltpu.VMEM((bands, bands), bf16),
            pltpu.VMEM((CHUNKS, 2 * block, bands), bf16),
            pltpu.VMEM((WATERS, 128), f32),
            pltpu.VMEM((parts, waters, 128), f32),
            pltpu.VMEM((128, local_g), f32),
            dma((1 + CHUNKS,)),
            dma((2, parts)),
            dma((2, CHUNKS, parts)),
            dma((2, CHUNKS, parts)),
            dma((2, parts)),
            dma((2, 3, steps)),
            dma((2, 3, steps)),
        ],
        compiler_params=pltpu.CompilerParams(
            collective_id=0, has_side_effects=True, vmem_limit_bytes=67043328
        ),
    )(
        psi[0],
        positions,
        weights,
        trig_tables(),
        cross_tables(parts, planes, share),
        vloc,
    )
    return (psi_new[None], force)


def step_device(positions, weights, psi, vloc):
    parts = lax.axis_size("ga")
    bands, local_g = psi.shape[1], psi.shape[3]
    side = NGRID * NGRID
    fits = (
        local_g % side == 0
        and parts & (parts - 1) == 0
        and parts >= 4
        and bands % (parts * CHUNKS * 16) == 0
        and bands // CHUNKS % 256 == 0
        and bands * local_g <= 2**20
    )
    if fits:
        return fused_device(positions, weights, psi, vloc)
    return per_device(positions, weights, psi, vloc)


def solution(mesh):
    placed = (P("rep", None, "ga"), P(), P("rep", None, None, "ga"), P("rep", None))
    return jax.shard_map(
        step_device,
        mesh=mesh,
        in_specs=placed,
        out_specs=(P("rep", None, None, "ga"), P("rep", None, "ga")),
        check_vma=False,
    )
```

```python
import functools

import jax
import jax.numpy as jnp
import numpy as np
from jax import lax
from jax.experimental import pallas as pl
from jax.experimental.pallas import tpu as pltpu
from jax.sharding import PartitionSpec as P

BEADS = 32
CBEADS = 1
WATERS = 256
NGRID = 32
GVECS = 32768
CHUNKS = 2


box_length = 20.0
bond_stiff = 0.5
bond_rest = 1.8
spring_stiff = 2.0
width_square = 0.09
step_size = 0.02
nonlocal_strength = 250.0
occupation = 2.0
highest = lax.Precision.HIGHEST


def frequency(index, count):
    signed = jnp.where(index < count // 2, index, index - count)
    return signed.astype(jnp.float32) * (2.0 * jnp.pi / box_length)


def field_forces(positions):
    oxygen = positions[:, :, 0::3]
    toward_one = positions[:, :, 1::3] - oxygen
    toward_two = positions[:, :, 2::3] - oxygen

    def stretch(offset):
        length = jnp.sqrt(jnp.sum(offset * offset, axis=1, keepdims=True))
        return -bond_stiff * (length - bond_rest) * offset / length

    pull_one = stretch(toward_one)
    pull_two = stretch(toward_two)
    bonds = jnp.stack([-(pull_one + pull_two), pull_one, pull_two], axis=3).reshape(positions.shape)
    springs = 2.0 * positions - jnp.roll(positions, 1, axis=0) - jnp.roll(positions, -1, axis=0)
    return bonds - spring_stiff * springs


def inner(left_mat, right_mat):
    return lax.dot_general(
        left_mat, right_mat, (((1,), (1,)), ((), ())), preferred_element_type=jnp.float32
    )


def real_form(freq_index, group_index):
    product = freq_index[:, None] * freq_index[None, :] % NGRID
    angle = product.astype(jnp.float32) * (2.0 * jnp.pi / NGRID)
    same = (group_index[:, None] == group_index[None, :]).astype(jnp.float32)
    cosines = jnp.cos(angle) * same
    sines = jnp.sin(angle) * same
    return jnp.stack([jnp.stack([cosines, sines], 1), jnp.stack([-sines, cosines], 1)], 0)


def plane_table():
    index = jnp.arange(NGRID, dtype=jnp.int32)
    return real_form(index, jnp.zeros_like(index))


def block_table(length, within):
    index = jnp.arange(length, dtype=jnp.int32)
    if within:
        return real_form(index % NGRID, index // NGRID)
    return real_form(index // NGRID, index % NGRID)


def grid_sum(psi, vloc, parts):
    bands = psi.shape[1]
    local_g = psi.shape[3]
    x_table = plane_table()
    z_table = block_table(local_g, True)
    y_table = block_table(NGRID * NGRID, False)
    grid_potential = vloc[0].reshape(1, 1, NGRID, NGRID * NGRID)
    grouped_raw = psi[0].reshape(parts, bands // parts, 2, local_g)
    planes = lax.all_to_all(grouped_raw, "ga", split_axis=0, concat_axis=3, tiled=True)
    band_count = planes.shape[1]
    blocks_whole = planes.astype(jnp.float32).reshape(band_count, 2, NGRID**3 // local_g, local_g)
    along_z = jnp.einsum("mckp,cpdq->mdkq", blocks_whole, z_table, precision=highest) * (
        1.0 / NGRID
    )
    grid = along_z.reshape(band_count, 2, NGRID, NGRID * NGRID)
    grid = jnp.einsum("mcxr,cxdw->mdwr", grid, x_table, precision=highest) * (1.0 / NGRID)
    grid = jnp.einsum("mcxp,cpdq->mdxq", grid, y_table, precision=highest) * (1.0 / NGRID)
    grid = grid * grid_potential
    grid = jnp.einsum("mdxq,cpdq->mcxp", grid, y_table, precision=highest)
    grid = jnp.einsum("mdwr,cxdw->mcxr", grid, x_table, precision=highest)
    returning = grid.reshape(1, band_count, 2, NGRID**3)
    returned = lax.all_to_all(
        returning.astype(jnp.bfloat16), "ga", split_axis=3, concat_axis=0, tiled=True
    ).astype(returning.dtype)
    returned = returned.reshape(bands, 2, local_g)
    potential = jnp.einsum("bdq,cpdq->bcp", returned, z_table, precision=highest)
    return potential[:, 0], potential[:, 1]


def plane_rotation():
    small = np.arange(NGRID)
    angle = small[:, None] * small[None, :] % NGRID * (2.0 * np.pi / NGRID)
    side = NGRID * NGRID
    wave = np.kron(np.exp(1j * angle), np.exp(1j * angle))
    real, imag = np.real(wave), np.imag(wave)
    table = np.stack([np.stack([real, -imag], 1), np.stack([imag, real], 1)], 1)
    return jnp.asarray(table.reshape(2 * side, 2 * side).astype(np.float32), jnp.bfloat16)


def line_rotation(group):
    small = np.arange(NGRID)
    angle = small[:, None] * small[None, :] % NGRID * (2.0 * np.pi / NGRID)
    real, imag = np.cos(angle), np.sin(angle)
    form = np.stack([np.stack([real, -imag], 2), np.stack([imag, real], 2)], 1)
    same = np.eye(group)
    table = form[:, None, :, :, None, :] * same[None, :, None, None, :, None]
    size = 2 * NGRID * group
    return jnp.asarray(table.reshape(size, size).astype(np.float32), jnp.bfloat16)


def plane_out(psi, parts, plane_table, offset):
    bands = psi.shape[1]
    side = NGRID * NGRID
    planes = psi.shape[3] // side
    chunk = bands // CHUNKS
    pieces = []
    for first in range(0, bands, chunk):
        part = lax.dynamic_slice_in_dim(psi[0], first + offset, chunk, axis=0).reshape(chunk, 2, planes, side)
        part = part.transpose(2, 0, 1, 3).reshape(planes, chunk, 2 * side)
        pieces.append(
            jnp.stack(
                [
                    jnp.einsum(
                        "qk,bk->qb", plane_table, part[p], preferred_element_type=jnp.float32
                    )
                    .astype(jnp.bfloat16)
                    .reshape(parts, 2 * side // parts, chunk)
                    for p in range(planes)
                ],
                1,
            )
        )
    return pieces


def exchange(piece):
    return lax.all_to_all(piece, "ga", split_axis=0, concat_axis=0, tiled=True)


def line_action(vloc, parts):
    side = NGRID * NGRID
    points = side // parts
    group = min(8, points)
    groups = points // group
    line_table = line_rotation(group)
    start = lax.axis_index("ga") * points
    own = lax.dynamic_slice_in_dim(vloc[0].reshape(NGRID, side), start, points, axis=1)
    own = own.reshape(NGRID, groups, group).transpose(1, 0, 2) * (1.0 / (NGRID * side))
    own = jnp.broadcast_to(own[..., None], (groups, NGRID, group, 2)).reshape(groups, -1, 1)
    scaled = (own * line_table.astype(jnp.float32)).astype(jnp.bfloat16)
    return jnp.einsum(
        "ea,gec->gac", line_table, scaled, preferred_element_type=jnp.float32
    ).astype(jnp.bfloat16)


def line_step(action, lines):
    parts, planes, rows, chunk = lines.shape
    groups = action.shape[0]
    lines = lines.reshape(parts * planes, groups, rows // groups, chunk)
    lines = lines.transpose(1, 0, 2, 3).reshape(groups, -1, chunk)
    lines = jnp.einsum(
        "gac,gcb->gab", action, lines, preferred_element_type=jnp.float32
    ).astype(jnp.bfloat16)
    lines = lines.reshape(groups, parts * planes, rows // groups, chunk).transpose(1, 0, 2, 3)
    return lines.reshape(parts, planes, rows, chunk)


def plane_back(backs, plane_table):
    side = NGRID * NGRID
    reals, imags = [], []
    for back in backs:
        chunk = back.shape[3]
        whole = [
            jnp.einsum(
                "qb,qk->bk",
                back[:, p].reshape(2 * side, chunk),
                plane_table,
                preferred_element_type=jnp.float32,
            )
            for p in range(back.shape[1])
        ]
        reals.append(jnp.concatenate([w[:, :side] for w in whole], 1))
        imags.append(jnp.concatenate([w[:, side:] for w in whole], 1))
    return jnp.concatenate(reals, 0), jnp.concatenate(imags, 0)


def waves(oxygens, gvectors, profile):
    local_g = profile.shape[0]
    side = NGRID * NGRID
    if local_g % side:
        phases = jnp.einsum("ai,ag->ig", oxygens, gvectors, precision=highest)
        return profile * jnp.cos(phases), profile * jnp.sin(phases)
    spots = oxygens.T
    flat = spots[:, 1:2] * gvectors[1:2, :side] + spots[:, 2:3] * gvectors[2:3, :side]
    flat_cos, flat_sin = jnp.cos(flat), jnp.sin(flat)
    along = spots[:, 0:1] * gvectors[0:1, ::side]
    along_cos, along_sin = jnp.cos(along), jnp.sin(along)
    cosines, sines = [], []
    for p in range(local_g // side):
        c, s = along_cos[:, p : p + 1], along_sin[:, p : p + 1]
        cosines.append(c * flat_cos - s * flat_sin)
        sines.append(s * flat_cos + c * flat_sin)
    return profile * jnp.concatenate(cosines, 1), profile * jnp.concatenate(sines, 1)


def per_device(positions, weights, psi, vloc):
    near_forces = field_forces(positions)
    weight_float = weights.astype(jnp.float32)
    mixing = weight_float / jnp.sum(weight_float, axis=1, keepdims=True)
    centres = jnp.einsum("cj,jan->can", mixing, positions, precision=highest)
    parts = lax.axis_size("ga")
    near_oxygen = centres[0][:, 0::3]
    own_waters = near_oxygen.shape[1]
    everyone = lax.dynamic_update_slice(
        jnp.zeros((3, own_waters * parts), jnp.float32),
        near_oxygen,
        (0, lax.axis_index("ga") * own_waters),
    )
    oxygens = lax.psum(everyone, "ga")
    side = NGRID * NGRID
    whole_planes = psi.shape[3] % side == 0 and side % parts == 0
    if whole_planes:
        plane_table = plane_rotation()
        pieces = plane_out(psi, parts, plane_table, (oxygens[0, 0] * 0.0).astype(jnp.int32))
        lines = [exchange(piece) for piece in pieces]
        action = line_action(vloc, parts)
    bands = psi.shape[1]
    local_g = psi.shape[3]
    flat_index = lax.axis_index("ga") * local_g + jnp.arange(local_g, dtype=jnp.int32)
    gvectors = jnp.stack(
        [
            frequency(flat_index // (NGRID * NGRID), NGRID),
            frequency(flat_index // NGRID % NGRID, NGRID),
            frequency(flat_index % NGRID, NGRID),
        ]
    )
    square = jnp.sum(gvectors * gvectors, axis=0)
    profile = jnp.exp(-0.5 * width_square * square)
    kinetic = 0.5 * square
    wave_cos, wave_sin = waves(oxygens, gvectors, profile)
    table = jnp.concatenate(
        [jnp.concatenate([wave_cos, -wave_sin], 1), jnp.concatenate([wave_sin, wave_cos], 1)], 0
    ).astype(jnp.bfloat16)
    wavefunc = psi[0].reshape(bands, 2 * local_g)
    partial_proj = (inner(table, wavefunc) * (1.0 / GVECS)).reshape(2, WATERS, bands)
    share = lax.psum_scatter(partial_proj, "ga", scatter_dimension=1, tiled=True).astype(
        jnp.bfloat16
    )
    table_blocks = table.reshape(2 * WATERS, 2 * local_g)
    copies = jnp.broadcast_to(share[None], (parts,) + share.shape)
    if whole_planes:
        lines[-1], copies = lax.optimization_barrier((lines[-1], copies))
    all_proj = lax.all_to_all(copies, "ga", split_axis=0, concat_axis=0, tiled=True)
    if whole_planes:
        moved = [line_step(action, line) for line in lines]
        moved[0], all_proj = lax.optimization_barrier((moved[0], all_proj))
        backs = [exchange(piece) for piece in moved]
    all_proj = all_proj.transpose(1, 0, 2, 3).reshape(2 * WATERS, bands)
    nonlocal_term = jnp.einsum(
        "ib,ig->bg", all_proj, table_blocks, preferred_element_type=jnp.float32
    )
    crossed = jnp.dot(all_proj, wavefunc, preferred_element_type=jnp.float32)
    weighted_re = crossed[:WATERS, :local_g] + crossed[WATERS:, local_g:]
    weighted_im = crossed[:WATERS, local_g:] - crossed[WATERS:, :local_g]
    mixed_wave = wave_cos * weighted_im + wave_sin * weighted_re
    force_part = (
        2.0
        * occupation
        * nonlocal_strength
        / GVECS
        * jnp.einsum("ag,ig->ai", gvectors, mixed_wave, precision=highest)
    )
    force_rows = force_part.reshape(3, parts, own_waters).transpose(1, 0, 2)
    force_rows = force_rows.reshape(parts, 1, 3 * own_waters)
    force_rows = jnp.pad(force_rows, ((0, 0), (0, 0), (0, bands - 3 * own_waters)))
    wave_float = psi[0].astype(jnp.float32)
    if whole_planes:
        potential = plane_back(backs, plane_table)
    else:
        potential = grid_sum(psi, vloc, parts)
    hamil_re = (
        kinetic * wave_float[:, 0]
        + potential[0]
        + nonlocal_strength * nonlocal_term[:, :local_g]
    )
    hamil_im = (
        kinetic * wave_float[:, 1]
        + potential[1]
        + nonlocal_strength * nonlocal_term[:, local_g:]
    )
    trial_re = (wave_float[:, 0] - step_size * hamil_re).astype(jnp.bfloat16)
    trial_im = (wave_float[:, 1] - step_size * hamil_im).astype(jnp.bfloat16)
    row = lax.broadcasted_iota(jnp.int32, (bands, bands), 0)
    column = lax.broadcasted_iota(jnp.int32, (bands, bands), 1)
    even = inner(trial_re, trial_re) + inner(trial_im, trial_im)
    odd = inner(trial_im, trial_re) - inner(trial_re, trial_im)
    packed = jnp.where(row <= column, even, odd) * (1.0 / GVECS)
    shares = lax.all_to_all(
        jnp.concatenate([packed.reshape(parts, bands // parts, bands), force_rows], 1),
        "ga",
        split_axis=0,
        concat_axis=0,
        tiled=True,
    )
    sums = jnp.sum(shares, axis=0)
    oxygen_force = sums[-1, : 3 * own_waters].reshape(3, own_waters)
    hydrogen_zero = jnp.zeros_like(oxygen_force)
    dft_forces = [jnp.stack([oxygen_force, hydrogen_zero, hydrogen_zero], axis=2).reshape(3, -1)]
    own_rows = lax.broadcasted_iota(jnp.int32, (bands // parts, bands), 0) + lax.axis_index(
        "ga"
    ) * (bands // parts)
    own_columns = lax.broadcasted_iota(jnp.int32, (bands // parts, bands), 1)
    mixed_rows = jnp.where(own_rows == own_columns, 1.5, 0.0) - 0.5 * sums[:-1]
    mixed = lax.all_gather(mixed_rows.astype(jnp.bfloat16), "ga", axis=0, tiled=True)
    turned = mixed.T
    mix_re = jnp.where(row <= column, mixed, turned)
    mix_im = jnp.where(row > column, mixed, jnp.where(row < column, -turned, jnp.zeros_like(turned)))
    both = jnp.concatenate([trial_re, trial_im], 0)
    new_re = jnp.dot(
        jnp.concatenate([mix_re, -mix_im], 1), both, preferred_element_type=jnp.float32
    ).astype(jnp.bfloat16)
    new_im = jnp.dot(
        jnp.concatenate([mix_im, mix_re], 1), both, preferred_element_type=jnp.float32
    ).astype(jnp.bfloat16)
    new_waves = [jnp.stack([new_re, new_im], 1)]
    contracted_force = jnp.einsum("cj,can->jan", mixing, jnp.stack(dft_forces), precision=highest)
    bead_forces = near_forces + BEADS / CBEADS * contracted_force
    return (jnp.stack(new_waves), bead_forces)


def product(left_mat, right_mat):
    return jnp.dot(left_mat, right_mat, preferred_element_type=jnp.float32)


def trig_tables():
    small = np.arange(NGRID)
    angle = small[:, None] * small[None, :] % NGRID * (2.0 * np.pi / NGRID)
    cosines, sines = np.cos(angle), np.sin(angle)
    rows = [np.repeat(cosines, NGRID, 1), np.repeat(sines, NGRID, 1)]
    rows += [np.tile(cosines, (1, NGRID)), np.tile(sines, (1, NGRID))]
    return jnp.asarray(np.stack(rows), jnp.float32)


def cross_tables(parts, planes, share):
    spot = (np.arange(parts)[None, :] * planes + np.arange(planes)[:, None]).reshape(-1)
    angle = spot[:, None] * spot[None, :] % NGRID * (2.0 * np.pi / NGRID)
    same = np.eye(share)
    pair = np.stack([np.kron(np.cos(angle), same), np.kron(np.sin(angle), same)])
    return jnp.asarray(pair.astype(np.float32), jnp.bfloat16)


def step_kernel(
    sizes,
    psi_hbm,
    positions,
    weights,
    trig,
    cross,
    vloc,
    trial_hbm,
    mixed,
    force_out,
    raw,
    psi,
    own_centres,
    all_centres,
    grid,
    near,
    all_waves,
    table_cos,
    table_sin,
    wave_cos,
    wave_sin,
    plane_cos,
    plane_sin,
    potential,
    got,
    whole,
    middle,
    giving,
    back,
    base,
    trial,
    partial,
    landing,
    gathered,
    turned,
    margin,
    landing_two,
    gathered_two,
    force_sum,
    force_land,
    grid_rows,
    local_sem,
    wave_sems,
    out_sems,
    back_sems,
    force_sems,
    sum_sems,
    share_sems,
):
    parts, bands, local_g = sizes
    side = NGRID * NGRID
    planes = local_g // side
    share = bands // (parts * CHUNKS)
    block = parts * share
    steps = parts.bit_length() - 1
    tile = 256
    atoms = positions.shape[2]
    waters = atoms // 3
    me = lax.axis_index("ga")

    def other(turn):
        total = 0
        for bit in range(steps):
            size = 1 << bit
            total = total + (me // size + turn // size) % 2 * size
        return total

    def remote(source, target, sems, peer):
        return pltpu.make_async_remote_copy(
            src_ref=source,
            dst_ref=target,
            send_sem=sems[0],
            recv_sem=sems[1],
            device_id={"ga": peer},
            device_id_type=pl.DeviceIdType.MESH,
        )

    def each_peer(act):
        def body(turn, carry):
            act(turn)
            return carry

        lax.fori_loop(1, parts, body, 0)

    def pair(sems, *spot):
        return sems.at[(0,) + spot], sems.at[(1,) + spot]

    def wave_copy(turn):
        rows = own_centres.shape[0]
        spot = pl.ds(pl.multiple_of(me * rows, rows), rows)
        return remote(own_centres, all_centres.at[spot], pair(wave_sems, turn), other(turn))

    def out_copy(chunk, turn):
        peer = other(turn)
        source = pl.ds(pl.multiple_of(chunk * block + peer * share, share), share)
        target = pl.ds(pl.multiple_of(me * share, share), share)
        return remote(
            psi_hbm.at[source], got.at[chunk, target], pair(out_sems, chunk, turn), peer
        )

    def back_copy(chunk, turn):
        peer = other(turn)
        source = pl.ds(pl.multiple_of(peer * share, share), share)
        target = pl.ds(pl.multiple_of(chunk * block + me * share, share), share)
        return remote(
            giving.at[chunk, source], back.at[target], pair(back_sems, chunk, turn), peer
        )

    def force_copy(turn):
        peer = other(turn)
        source = pl.ds(pl.multiple_of(peer * waters, waters), waters)
        return remote(
            force_sum.at[source], force_land.at[me], pair(force_sems, turn), peer
        )

    local_psi = pltpu.make_async_copy(psi_hbm, raw, local_sem.at[0])
    local_psi.start()
    barrier = pltpu.get_barrier_semaphore()

    def greet(turn):
        pl.semaphore_signal(
            barrier, inc=1, device_id={"ga": other(turn)}, device_id_type=pl.DeviceIdType.MESH
        )

    each_peer(greet)
    beads = positions.shape[0]

    def exact(left_mat, right_mat, right_axis=0):
        return lax.dot_general(
            left_mat,
            right_mat,
            (((1,), (right_axis,)), ((), ())),
            precision=highest,
            preferred_element_type=jnp.float32,
        )

    def spots(shape):
        return lax.broadcasted_iota(jnp.int32, shape, 0), lax.broadcasted_iota(jnp.int32, shape, 1)

    weight_row = weights[...].astype(jnp.float32)
    mixing = weight_row / jnp.sum(weight_row, axis=1, keepdims=True)
    own_row, own_atom = spots((waters, atoms))
    pick_row, pick_atom = spots((own_centres.shape[1], atoms))
    oxygen_pick = jnp.where(pick_atom == 3 * pick_row, 1.0, 0.0)
    centre_row = lax.broadcasted_iota(jnp.int32, own_centres.shape, 0)
    near_centres = jnp.zeros(own_centres.shape, jnp.float32)
    for axis in range(3):
        centre = exact(jnp.broadcast_to(mixing, (8, beads)), positions[:, axis, :])
        near_centres += jnp.where(centre_row == axis, exact(centre, oxygen_pick, 1), 0.0)
    own_centres[...] = near_centres
    all_centres[pl.ds(pl.multiple_of(me * 8, 8), 8), :] = near_centres
    own_spot = pl.ds(pl.multiple_of(me * waters, waters), waters)
    pl.semaphore_wait(barrier, parts - 1)

    units = [(chunk, far) for chunk in range(CHUNKS) for far in range(parts // 2)]
    queue = list(units)

    def issue(count):
        for _ in range(count):
            if queue:
                chunk, far = queue.pop(0)
                out_copy(chunk, parts // 2 + far).start()
                if far > 0:
                    out_copy(chunk, far).start()

    each_peer(lambda turn: wave_copy(turn).start())
    issue(2)

    flat_index = me * local_g + lax.broadcasted_iota(jnp.int32, (1, local_g), 1)
    gvectors = [
        frequency(flat_index // side, NGRID),
        frequency(flat_index // NGRID % NGRID, NGRID),
        frequency(flat_index % NGRID, NGRID),
    ]
    square = gvectors[0] * gvectors[0] + gvectors[1] * gvectors[1] + gvectors[2] * gvectors[2]
    grid[0:1, :] = jnp.exp(-0.5 * width_square * square)
    grid[1:2, :] = 0.5 * square
    grid_rows[...] = jnp.zeros_like(grid_rows)
    for axis in range(3):
        grid_rows[axis : axis + 1, :] = gvectors[axis]

    def plane_rows(row, carry):
        spot = pl.ds(pl.multiple_of(row * NGRID, NGRID), NGRID)
        across_cos, across_sin = trig[0, pl.ds(row, 1), :], trig[1, pl.ds(row, 1), :]
        plane_cos[spot, :] = (across_cos * trig[2] - across_sin * trig[3]).astype(jnp.bfloat16)
        plane_sin[spot, :] = (across_sin * trig[2] + across_cos * trig[3]).astype(jnp.bfloat16)
        return carry

    lax.fori_loop(0, NGRID, plane_rows, 0)

    def potential_rows(spot, carry):
        plane = spot % planes * parts + spot // planes
        rows = pl.ds(pl.multiple_of(plane * share, share), share)
        value = vloc[:, pl.ds(pl.multiple_of(spot * side, side), side)] * (1.0 / NGRID**3)
        potential[rows, :] = jnp.broadcast_to(value, (share, side))
        return carry

    lax.fori_loop(0, NGRID, potential_rows, 0)

    strip = 16

    def unpack_rows(step, carry):
        rows = pl.ds(pl.multiple_of(step * strip, strip), strip)
        psi[rows, :local_g] = raw[rows, 0, :]
        psi[rows, local_g:] = raw[rows, 1, :]
        return carry

    local_psi.wait()
    lax.fori_loop(0, bands // strip, unpack_rows, 0)
    each_peer(lambda turn: wave_copy(turn).wait_recv())
    lined = all_centres[...].T
    _, wave_lane = spots((waters, all_waves.shape[1]))
    spokes = frequency(wave_lane % NGRID, NGRID)
    for source in range(parts):
        angles = jnp.zeros(spokes.shape, jnp.float32)
        for axis in range(3):
            column = lined[:waters, 8 * source + axis : 8 * source + axis + 1]
            angles += column * jnp.where(wave_lane // (2 * NGRID) == axis, spokes, 0.0)
        all_waves[source * waters : (source + 1) * waters, :] = angles

    def wave_rows(source, carry):
        rows = pl.ds(pl.multiple_of(source * waters, waters), waters)
        angles = all_waves[rows, :]
        all_waves[rows, :] = jnp.where(
            wave_lane // NGRID % 2 == 0, jnp.cos(angles), jnp.sin(angles)
        )
        return carry

    lax.fori_loop(0, parts, wave_rows, 0)
    lane = lax.broadcasted_iota(jnp.int32, all_waves.shape, 1)
    line = lax.broadcasted_iota(jnp.int32, (all_waves.shape[1], tile), 0)
    place = lax.broadcasted_iota(jnp.int32, (all_waves.shape[1], tile), 1)

    def pick(first, spot):
        return jnp.where(line == first * NGRID + spot, 1.0, 0.0)

    def spread(first, spot):
        return lax.dot_general(
            all_waves[...],
            pick(first, spot),
            (((1,), (0,)), ((), ())),
            precision=highest,
            preferred_element_type=jnp.float32,
        )

    def table_tile(step, carry):
        first = step * tile
        flat = first + place
        rise, along = flat // NGRID, flat % NGRID
        rise_cos, rise_sin = spread(2, rise), spread(3, rise)
        long_cos, long_sin = spread(4, along), spread(5, along)
        flat_cos = rise_cos * long_cos - rise_sin * long_sin
        flat_sin = rise_sin * long_cos + rise_cos * long_sin
        for plane in range(planes):
            level = me * planes + plane
            c = jnp.sum(jnp.where(lane == level, all_waves[...], 0.0), axis=1, keepdims=True)
            s = jnp.sum(
                jnp.where(lane == level + NGRID, all_waves[...], 0.0), axis=1, keepdims=True
            )
            spot = pl.ds(pl.multiple_of(plane * side + first, tile), tile)
            profile = grid[0:1, spot]
            full_cos = profile * (c * flat_cos - s * flat_sin)
            full_sin = profile * (s * flat_cos + c * flat_sin)
            wave_cos[:, spot] = full_cos
            wave_sin[:, spot] = full_sin
            table_cos[:, spot] = full_cos.astype(jnp.bfloat16)
            table_sin[:, spot] = full_sin.astype(jnp.bfloat16)
        return carry

    lax.fori_loop(0, side // tile, table_tile, 0)
    partial[...] = jnp.zeros_like(partial)

    def project(step, carry):
        spot = pl.ds(pl.multiple_of(step * tile, tile), tile)
        far = pl.ds(pl.multiple_of(local_g + step * tile, tile), tile)
        real, imag = psi[:, spot], psi[:, far]
        cosines, sines = table_cos[:, spot], table_sin[:, spot]
        partial[:WATERS, :] += inner(cosines, real) - inner(sines, imag)
        partial[WATERS:, :] += inner(sines, real) + inner(cosines, imag)
        return carry

    lax.fori_loop(0, local_g // tile, project, 0)

    straight = list(range(steps))
    crossed = [0] + straight[2:] + [1]
    narrow = bands // 2
    single = [(0, straight, pl.ds(0, bands))]
    double = [(1, straight, pl.ds(0, narrow)), (2, crossed, pl.ds(narrow, narrow))]

    def own_start(order, upto, rows):
        start = 0
        for place, bit in enumerate(order[:upto]):
            start = start + me // (1 << bit) % 2 * (rows >> (place + 1))
        return start

    def partner(bit):
        size = 1 << bit
        mine = me // size % 2
        return mine, me + (1 - 2 * mine) * size

    def sum_step(values, land, halves, place, between):
        rows = values.shape[0]
        half = rows >> (place + 1)
        spot = pl.ds(rows - 2 * half, half)
        pending = []
        for which, order, columns in halves:
            mine, peer = partner(order[place])
            start = own_start(order, place, rows)
            away = pl.ds(pl.multiple_of(start + (1 - mine) * half, half), half)
            keep = pl.ds(pl.multiple_of(start + mine * half, half), half)
            copy = remote(
                values.at[away, columns],
                land.at[spot, columns],
                pair(sum_sems, which, place),
                peer,
            )
            copy.start()
            pending.append((copy, keep, columns))
        between()
        for copy, keep, columns in pending:
            copy.wait()
            values[keep, columns] += land[spot, columns]

    def share_step(values, halves, place, between):
        rows = values.shape[0]
        count = rows >> (place + 1)
        pending = []
        for which, order, columns in halves:
            _, peer = partner(order[place])
            spot = pl.ds(pl.multiple_of(own_start(order, place + 1, rows), count), count)
            copy = remote(
                values.at[spot, columns],
                values.at[spot, columns],
                pair(share_sems, which, place),
                peer,
            )
            copy.start()
            pending.append(copy)
        between()
        for copy in pending:
            copy.wait()

    for bit in range(steps):
        sum_step(partial, landing, single, bit, lambda: issue(1))
    own_rows = partial.shape[0] // parts
    own = pl.ds(pl.multiple_of(own_start(straight, steps, partial.shape[0]), own_rows), own_rows)
    gathered[own, :] = (partial[own, :] * (1.0 / GVECS)).astype(jnp.bfloat16)
    for bit in reversed(range(steps)):
        share_step(gathered, single, bit, lambda: issue(1))
    issue(len(units))

    for first in range(0, gathered.shape[0], tile):
        for second in range(0, bands, tile):
            part = gathered[first : first + tile, second : second + tile].astype(jnp.float32)
            turned[second : second + tile, first : first + tile] = part.T.astype(jnp.bfloat16)

    def transform(chunk):
        mine = pl.ds(pl.multiple_of(me * share, share), share)
        own_bands = pl.ds(pl.multiple_of(chunk * block + me * share, share), share)
        whole[mine, :] = psi[own_bands, :]

        def unpack_peer(turn):
            out_copy(chunk, turn).wait_recv()
            rows = pl.ds(pl.multiple_of(other(turn) * share, share), share)
            whole[rows, :local_g] = got[chunk, rows, 0, :]
            whole[rows, local_g:] = got[chunk, rows, 1, :]

        each_peer(unpack_peer)
        columns = side // tile

        def forward(step, carry):
            plane, column = step // columns, step % columns
            spot = pl.ds(pl.multiple_of(column * tile, tile), tile)
            rows = pl.ds(pl.multiple_of(plane * block, block), block)
            real = whole[:, pl.ds(pl.multiple_of(plane * side, side), side)]
            imag = whole[:, pl.ds(pl.multiple_of(local_g + plane * side, side), side)]
            cosines, sines = plane_cos[:, spot], plane_sin[:, spot]
            middle[0, rows, spot] = (product(real, cosines) - product(imag, sines)).astype(
                jnp.bfloat16
            )
            middle[1, rows, spot] = (product(real, sines) + product(imag, cosines)).astype(
                jnp.bfloat16
            )
            return carry

        lax.fori_loop(0, planes * columns, forward, 0)

        def lines(column, carry):
            spot = pl.ds(pl.multiple_of(column * tile, tile), tile)
            real, imag = middle[0, :, spot], middle[1, :, spot]
            value = potential[:, spot]
            cosines, sines = cross[0], cross[1]
            upper = (product(cosines, real) - product(sines, imag)) * value
            lower = (product(sines, real) + product(cosines, imag)) * value
            upper, lower = upper.astype(jnp.bfloat16), lower.astype(jnp.bfloat16)
            middle[0, :, spot] = (product(cosines, upper) + product(sines, lower)).astype(
                jnp.bfloat16
            )
            middle[1, :, spot] = (product(cosines, lower) - product(sines, upper)).astype(
                jnp.bfloat16
            )
            return carry

        lax.fori_loop(0, columns, lines, 0)

        def backward(step, carry):
            plane, column = step // columns, step % columns
            spot = pl.ds(pl.multiple_of(column * tile, tile), tile)
            rows = pl.ds(pl.multiple_of(plane * block, block), block)
            real, imag = middle[0, rows, :], middle[1, rows, :]
            cosines, sines = plane_cos[:, spot], plane_sin[:, spot]
            upper = pl.ds(pl.multiple_of(plane * side + column * tile, tile), tile)
            lower = pl.ds(pl.multiple_of(local_g + plane * side + column * tile, tile), tile)
            giving[chunk, :, upper] = (product(real, cosines) + product(imag, sines)).astype(
                jnp.bfloat16
            )
            giving[chunk, :, lower] = (product(imag, cosines) - product(real, sines)).astype(
                jnp.bfloat16
            )
            return carry

        lax.fori_loop(0, planes * columns, backward, 0)
        back[own_bands, :] = giving[chunk, mine, :]
        for far in range(parts // 2):
            back_copy(chunk, parts // 2 + far).start()
            if far > 0:
                back_copy(chunk, far).start()

    def near_forces():
        here, there = spots((atoms, atoms))
        same = jnp.where(here == there, 1.0, 0.0)
        offset_pick = same - jnp.where(here == there - there % 3, 1.0, 0.0)
        pull_pick = same - jnp.where(there == here - here % 3, 1.0, 0.0)
        bead, beside = spots((beads, beads))
        spring = 2.0 * jnp.where(bead == beside, 1.0, 0.0)
        spring -= jnp.where((bead + 1) % beads == beside, 1.0, 0.0)
        spring -= jnp.where((beside + 1) % beads == bead, 1.0, 0.0)
        offsets = [exact(positions[:, axis, :], offset_pick) for axis in range(3)]
        squares = offsets[0] * offsets[0] + offsets[1] * offsets[1] + offsets[2] * offsets[2]
        hydrogen = lax.broadcasted_iota(jnp.int32, squares.shape, 1) % 3 > 0
        length = jnp.sqrt(jnp.where(hydrogen, squares, 1.0))
        for axis in range(3):
            pull = -bond_stiff * (length - bond_rest) * offsets[axis] / length
            pull = jnp.where(hydrogen, pull, 0.0)
            near[axis] = exact(pull, pull_pick) - spring_stiff * exact(
                spring, positions[:, axis, :]
            )

    transform(0)

    force_sum[...] = jnp.zeros_like(force_sum)

    def local_part(step, carry):
        spot = pl.ds(pl.multiple_of(step * tile, tile), tile)
        far = pl.ds(pl.multiple_of(local_g + step * tile, tile), tile)
        kinetic = 1.0 - step_size * grid[1:2, spot]
        real, imag = psi[:, spot], psi[:, far]
        cosines, sines = table_cos[:, spot], table_sin[:, spot]
        turned_re, turned_im = turned[:, :WATERS], turned[:, WATERS:]
        strength = step_size * nonlocal_strength
        base[:, spot] = kinetic * real.astype(jnp.float32) - strength * (
            product(turned_re, cosines) + product(turned_im, sines)
        )
        base[:, far] = kinetic * imag.astype(jnp.float32) - strength * (
            product(turned_im, cosines) - product(turned_re, sines)
        )
        proj_re, proj_im = gathered[:WATERS, :], gathered[WATERS:, :]
        weighted_re = product(proj_re, real) + product(proj_im, imag)
        weighted_im = product(proj_re, imag) - product(proj_im, real)
        mixed = wave_cos[:, spot] * weighted_im + wave_sin[:, spot] * weighted_re
        force_sum[...] += lax.dot_general(
            mixed,
            grid_rows[:, spot],
            (((1,), (1,)), ((), ())),
            precision=highest,
            preferred_element_type=jnp.float32,
        )
        return carry

    lax.fori_loop(0, local_g // tile, local_part, 0)
    force_land[me] = force_sum[own_spot, :]
    each_peer(lambda turn: force_copy(turn).start())

    near_forces()
    transform(1)
    each_peer(lambda turn: force_copy(turn).wait_recv())

    def add_force(source, carry):
        return carry + force_land[source]

    strength = 2.0 * occupation * nonlocal_strength / GVECS
    total = strength * lax.fori_loop(
        0, parts, add_force, jnp.zeros(force_land.shape[1:], jnp.float32)
    )
    bead_row, bead_column = spots((beads, beads))
    mixing_column = jnp.sum(
        jnp.where(bead_row == bead_column, jnp.broadcast_to(mixing, (beads, beads)), 0.0),
        axis=1,
        keepdims=True,
    )
    for axis in range(3):
        placed = jnp.where(own_atom == 3 * own_row, total[:, axis : axis + 1], 0.0)
        placed = jnp.sum(placed, axis=0, keepdims=True)
        force_out[:, axis, :] = near[axis] + BEADS / CBEADS * (mixing_column * placed)

    def finish(chunk):
        def rows_of(turn, carry):
            @pl.when(turn > 0)
            def _():
                back_copy(chunk, turn).wait_recv()

            rows = pl.ds(
                pl.multiple_of(chunk * block + other(turn) * share, share), share
            )
            value = base[rows, :] - step_size * back[rows, :].astype(jnp.float32)
            value = value.astype(jnp.bfloat16)
            trial[0, rows, :] = value[:, :local_g]
            trial[1, rows, :] = value[:, local_g:]
            return carry

        lax.fori_loop(0, parts, rows_of, 0)

    corner_row = lax.broadcasted_iota(jnp.int32, (block, block), 0)
    corner_column = lax.broadcasted_iota(jnp.int32, (block, block), 1)

    def overlap(later, earlier):
        wide = 2 * tile
        rows = pl.ds(later * block, block)
        columns = pl.ds(earlier * block, block)
        margin[rows, columns] = jnp.zeros((block, block), jnp.float32)
        margin[columns, rows] = jnp.zeros((block, block), jnp.float32)

        def add(step, carry):
            spot = pl.ds(pl.multiple_of(step * wide, wide), wide)
            stacked = trial[:, rows, spot].reshape(2 * block, wide)
            on_real = inner(stacked, trial[0, columns, spot])
            on_imag = inner(stacked, trial[1, columns, spot])
            even = on_real[:block] + on_imag[block:]
            odd = on_real[block:] - on_imag[:block]
            if later == earlier:
                margin[rows, columns] += jnp.where(corner_row <= corner_column, even, odd)
            else:
                margin[columns, rows] += even
                margin[rows, columns] += odd
            return carry

        lax.fori_loop(0, local_g // wide, add, 0)

    def trial_copy(chunk):
        rows = pl.ds(chunk * block, block)
        return pltpu.make_async_copy(
            trial.at[:, rows], trial_hbm.at[:, rows], local_sem.at[1 + chunk]
        )

    for chunk in range(CHUNKS):
        finish(chunk)
        trial_copy(chunk).start()
        for earlier in range(chunk + 1):
            overlap(chunk, earlier)

    for place in range(steps):
        sum_step(margin, landing_two, double, place, lambda: None)
    own_rows = bands // parts
    for _, order, columns in double:
        start = own_start(order, steps, bands)
        own = pl.ds(pl.multiple_of(start, own_rows), own_rows)
        row, column = spots((own_rows, narrow))
        same = start + row == columns.start + column
        mixed_rows = jnp.where(same, 1.5, 0.0) - (0.5 / GVECS) * margin[own, columns]
        gathered_two[own, columns] = mixed_rows.astype(jnp.bfloat16)
    for place in reversed(range(steps)):
        share_step(gathered_two, double, place, lambda: None)

    for chunk in range(CHUNKS):
        rows = pl.ds(chunk * block, block)
        there = gathered_two[rows, rows].astype(jnp.float32)
        flipped = there.T
        mix_re = jnp.where(corner_row <= corner_column, there, flipped)
        mix_im = jnp.where(
            corner_row > corner_column,
            there,
            jnp.where(corner_row < corner_column, -flipped, jnp.zeros_like(there)),
        )
        mixed[chunk, :block, rows] = mix_re.astype(jnp.bfloat16)
        mixed[chunk, block:, rows] = mix_im.astype(jnp.bfloat16)
        for earlier in range(chunk):
            columns = pl.ds(earlier * block, block)
            even, odd = gathered_two[columns, rows], gathered_two[rows, columns]
            mixed[chunk, :block, columns] = even
            mixed[chunk, block:, columns] = odd
            mixed[earlier, :block, rows] = even.astype(jnp.float32).T.astype(jnp.bfloat16)
            mixed[earlier, block:, rows] = (-odd.astype(jnp.float32).T).astype(jnp.bfloat16)

    for chunk in range(CHUNKS):
        trial_copy(chunk).wait()
        each_peer(lambda turn: out_copy(chunk, turn).wait_send())
        each_peer(lambda turn: back_copy(chunk, turn).wait_send())
    each_peer(lambda turn: wave_copy(turn).wait_send())
    each_peer(lambda turn: force_copy(turn).wait_send())


def rotate_kernel(mixed_hbm, trial_hbm, out_hbm, mixed, trial, out, sems):
    block = mixed.shape[1] // 2
    tiles, tile = trial.shape[0], trial.shape[3]
    mixed_copy = pltpu.make_async_copy(mixed_hbm, mixed, sems.at[tiles])

    def trial_copy(step):
        spot = pl.ds(pl.multiple_of(step * tile, tile), tile)
        return pltpu.make_async_copy(trial_hbm.at[:, :, spot], trial.at[step], sems.at[step])

    def out_copy(chunk):
        rows = pl.ds(chunk * block, block)
        return pltpu.make_async_copy(
            out.at[rows], out_hbm.at[rows], sems.at[tiles + 1 + chunk]
        )

    trial_copy(0).start()
    mixed_copy.start()
    for step in range(1, tiles):
        trial_copy(step).start()
    mixed_copy.wait()
    for chunk in range(CHUNKS):
        rows = pl.ds(chunk * block, block)

        def turn_columns(step, carry):
            if chunk == 0:
                trial_copy(step).wait()
            spot = pl.ds(pl.multiple_of(step * tile, tile), tile)
            on_real = product(mixed[chunk], trial[step, 0])
            on_imag = product(mixed[chunk], trial[step, 1])
            real = on_real[:block] - on_imag[block:]
            imag = on_real[block:] + on_imag[:block]
            out[rows, 0, spot] = real.astype(jnp.bfloat16)
            out[rows, 1, spot] = imag.astype(jnp.bfloat16)
            return carry

        lax.fori_loop(0, tiles, turn_columns, 0)
        out_copy(chunk).start()
    for chunk in range(CHUNKS):
        out_copy(chunk).wait()


def rotate(mixed, trial):
    bands, local_g = trial.shape[1:]
    tile = 256
    tiles = local_g // tile
    anywhere = pl.BlockSpec(memory_space=pl.ANY)
    return pl.pallas_call(
        rotate_kernel,
        out_shape=jax.ShapeDtypeStruct((bands, 2, local_g), jnp.bfloat16),
        in_specs=[anywhere, anywhere],
        out_specs=anywhere,
        scratch_shapes=[
            pltpu.VMEM(mixed.shape, mixed.dtype),
            pltpu.VMEM((tiles, 2, bands, tile), trial.dtype),
            pltpu.VMEM((bands, 2, local_g), trial.dtype),
            pltpu.SemaphoreType.DMA((tiles + 1 + CHUNKS,)),
        ],
        compiler_params=pltpu.CompilerParams(vmem_limit_bytes=67043328),
    )(mixed, trial)


def fused_device(positions, weights, psi, vloc):
    parts = lax.axis_size("ga")
    bands, local_g = psi.shape[1], psi.shape[3]
    side = NGRID * NGRID
    planes = local_g // side
    share = bands // (parts * CHUNKS)
    block = parts * share
    waters = positions.shape[2] // 3
    vmem = pl.BlockSpec(memory_space=pltpu.VMEM)
    anywhere = pl.BlockSpec(memory_space=pl.ANY)
    steps = parts.bit_length() - 1
    f32, bf16 = jnp.float32, jnp.bfloat16
    dma = pltpu.SemaphoreType.DMA
    trial, mixed, force = pl.pallas_call(
        functools.partial(step_kernel, (parts, bands, local_g)),
        out_shape=(
            jax.ShapeDtypeStruct((2, bands, local_g), bf16),
            jax.ShapeDtypeStruct((CHUNKS, 2 * block, bands), bf16),
            jax.ShapeDtypeStruct(positions.shape, f32),
        ),
        in_specs=[anywhere, vmem, vmem, vmem, vmem, vmem],
        out_specs=(anywhere, vmem, vmem),
        scratch_shapes=[
            pltpu.VMEM((bands, 2, local_g), bf16),
            pltpu.VMEM((bands, 2 * local_g), bf16),
            pltpu.VMEM((8, 128), f32),
            pltpu.VMEM((parts * 8, 128), f32),
            pltpu.VMEM((8, local_g), f32),
            pltpu.VMEM((3,) + positions.shape[::2], f32),
            pltpu.VMEM((WATERS, 8 * NGRID), f32),
            pltpu.VMEM((WATERS, local_g), bf16),
            pltpu.VMEM((WATERS, local_g), bf16),
            pltpu.VMEM((WATERS, local_g), f32),
            pltpu.VMEM((WATERS, local_g), f32),
            pltpu.VMEM((side, side), bf16),
            pltpu.VMEM((side, side), bf16),
            pltpu.VMEM((planes * block, side), f32),
            pltpu.VMEM((CHUNKS, block, 2, local_g), bf16),
            pltpu.VMEM((block, 2 * local_g), bf16),
            pltpu.VMEM((2, planes * block, side), bf16),
            pltpu.VMEM((CHUNKS, block, 2 * local_g), bf16),
            pltpu.VMEM((bands, 2 * local_g), bf16),
            pltpu.VMEM((bands, 2 * local_g), f32),
            pltpu.VMEM((2, bands, local_g), bf16),
            pltpu.VMEM((2 * WATERS, bands), f32),
            pltpu.VMEM((2 * WATERS, bands), f32),
            pltpu.VMEM((2 * WATERS, bands), bf16),
            pltpu.VMEM((bands, 2 * WATERS), bf16),
            pltpu.VMEM((bands, bands), f32),
            pltpu.VMEM((bands, bands), f32),
            pltpu.VMEM((bands, bands), bf16),
            pltpu.VMEM((WATERS, 128), f32),
            pltpu.VMEM((parts, waters, 128), f32),
            pltpu.VMEM((128, local_g), f32),
            dma((1 + CHUNKS,)),
            dma((2, parts)),
            dma((2, CHUNKS, parts)),
            dma((2, CHUNKS, parts)),
            dma((2, parts)),
            dma((2, 3, steps)),
            dma((2, 3, steps)),
        ],
        compiler_params=pltpu.CompilerParams(
            collective_id=0, has_side_effects=True, vmem_limit_bytes=67043328
        ),
    )(
        psi[0],
        positions,
        weights,
        trig_tables(),
        cross_tables(parts, planes, share),
        vloc,
    )
    return (rotate(mixed, trial)[None], force)


def step_device(positions, weights, psi, vloc):
    parts = lax.axis_size("ga")
    bands, local_g = psi.shape[1], psi.shape[3]
    side = NGRID * NGRID
    fits = (
        local_g % side == 0
        and parts & (parts - 1) == 0
        and parts >= 4
        and bands % (parts * CHUNKS * 16) == 0
        and bands // CHUNKS % 256 == 0
        and bands * local_g <= 2**20
    )
    if fits:
        return fused_device(positions, weights, psi, vloc)
    return per_device(positions, weights, psi, vloc)


def solution(mesh):
    placed = (P("rep", None, "ga"), P(), P("rep", None, None, "ga"), P("rep", None))
    return jax.shard_map(
        step_device,
        mesh=mesh,
        in_specs=placed,
        out_specs=(P("rep", None, None, "ga"), P("rep", None, "ga")),
        check_vma=False,
    )
```

```python
import functools

import jax
import jax.numpy as jnp
import numpy as np
from jax import lax
from jax.experimental import pallas as pl
from jax.experimental.pallas import tpu as pltpu
from jax.sharding import PartitionSpec as P

BEADS = 32
CBEADS = 1
WATERS = 256
NGRID = 32
GVECS = 32768
CHUNKS = 2


box_length = 20.0
bond_stiff = 0.5
bond_rest = 1.8
spring_stiff = 2.0
width_square = 0.09
step_size = 0.02
nonlocal_strength = 250.0
occupation = 2.0
highest = lax.Precision.HIGHEST


def frequency(index, count):
    signed = jnp.where(index < count // 2, index, index - count)
    return signed.astype(jnp.float32) * (2.0 * jnp.pi / box_length)


def field_forces(positions):
    oxygen = positions[:, :, 0::3]
    toward_one = positions[:, :, 1::3] - oxygen
    toward_two = positions[:, :, 2::3] - oxygen

    def stretch(offset):
        length = jnp.sqrt(jnp.sum(offset * offset, axis=1, keepdims=True))
        return -bond_stiff * (length - bond_rest) * offset / length

    pull_one = stretch(toward_one)
    pull_two = stretch(toward_two)
    bonds = jnp.stack([-(pull_one + pull_two), pull_one, pull_two], axis=3).reshape(positions.shape)
    springs = 2.0 * positions - jnp.roll(positions, 1, axis=0) - jnp.roll(positions, -1, axis=0)
    return bonds - spring_stiff * springs


def inner(left_mat, right_mat):
    return lax.dot_general(
        left_mat, right_mat, (((1,), (1,)), ((), ())), preferred_element_type=jnp.float32
    )


def real_form(freq_index, group_index):
    product = freq_index[:, None] * freq_index[None, :] % NGRID
    angle = product.astype(jnp.float32) * (2.0 * jnp.pi / NGRID)
    same = (group_index[:, None] == group_index[None, :]).astype(jnp.float32)
    cosines = jnp.cos(angle) * same
    sines = jnp.sin(angle) * same
    return jnp.stack([jnp.stack([cosines, sines], 1), jnp.stack([-sines, cosines], 1)], 0)


def plane_table():
    index = jnp.arange(NGRID, dtype=jnp.int32)
    return real_form(index, jnp.zeros_like(index))


def block_table(length, within):
    index = jnp.arange(length, dtype=jnp.int32)
    if within:
        return real_form(index % NGRID, index // NGRID)
    return real_form(index // NGRID, index % NGRID)


def grid_sum(psi, vloc, parts):
    bands = psi.shape[1]
    local_g = psi.shape[3]
    x_table = plane_table()
    z_table = block_table(local_g, True)
    y_table = block_table(NGRID * NGRID, False)
    grid_potential = vloc[0].reshape(1, 1, NGRID, NGRID * NGRID)
    grouped_raw = psi[0].reshape(parts, bands // parts, 2, local_g)
    planes = lax.all_to_all(grouped_raw, "ga", split_axis=0, concat_axis=3, tiled=True)
    band_count = planes.shape[1]
    blocks_whole = planes.astype(jnp.float32).reshape(band_count, 2, NGRID**3 // local_g, local_g)
    along_z = jnp.einsum("mckp,cpdq->mdkq", blocks_whole, z_table, precision=highest) * (
        1.0 / NGRID
    )
    grid = along_z.reshape(band_count, 2, NGRID, NGRID * NGRID)
    grid = jnp.einsum("mcxr,cxdw->mdwr", grid, x_table, precision=highest) * (1.0 / NGRID)
    grid = jnp.einsum("mcxp,cpdq->mdxq", grid, y_table, precision=highest) * (1.0 / NGRID)
    grid = grid * grid_potential
    grid = jnp.einsum("mdxq,cpdq->mcxp", grid, y_table, precision=highest)
    grid = jnp.einsum("mdwr,cxdw->mcxr", grid, x_table, precision=highest)
    returning = grid.reshape(1, band_count, 2, NGRID**3)
    returned = lax.all_to_all(
        returning.astype(jnp.bfloat16), "ga", split_axis=3, concat_axis=0, tiled=True
    ).astype(returning.dtype)
    returned = returned.reshape(bands, 2, local_g)
    potential = jnp.einsum("bdq,cpdq->bcp", returned, z_table, precision=highest)
    return potential[:, 0], potential[:, 1]


def plane_rotation():
    small = np.arange(NGRID)
    angle = small[:, None] * small[None, :] % NGRID * (2.0 * np.pi / NGRID)
    side = NGRID * NGRID
    wave = np.kron(np.exp(1j * angle), np.exp(1j * angle))
    real, imag = np.real(wave), np.imag(wave)
    table = np.stack([np.stack([real, -imag], 1), np.stack([imag, real], 1)], 1)
    return jnp.asarray(table.reshape(2 * side, 2 * side).astype(np.float32), jnp.bfloat16)


def line_rotation(group):
    small = np.arange(NGRID)
    angle = small[:, None] * small[None, :] % NGRID * (2.0 * np.pi / NGRID)
    real, imag = np.cos(angle), np.sin(angle)
    form = np.stack([np.stack([real, -imag], 2), np.stack([imag, real], 2)], 1)
    same = np.eye(group)
    table = form[:, None, :, :, None, :] * same[None, :, None, None, :, None]
    size = 2 * NGRID * group
    return jnp.asarray(table.reshape(size, size).astype(np.float32), jnp.bfloat16)


def plane_out(psi, parts, plane_table, offset):
    bands = psi.shape[1]
    side = NGRID * NGRID
    planes = psi.shape[3] // side
    chunk = bands // CHUNKS
    pieces = []
    for first in range(0, bands, chunk):
        part = lax.dynamic_slice_in_dim(psi[0], first + offset, chunk, axis=0).reshape(chunk, 2, planes, side)
        part = part.transpose(2, 0, 1, 3).reshape(planes, chunk, 2 * side)
        pieces.append(
            jnp.stack(
                [
                    jnp.einsum(
                        "qk,bk->qb", plane_table, part[p], preferred_element_type=jnp.float32
                    )
                    .astype(jnp.bfloat16)
                    .reshape(parts, 2 * side // parts, chunk)
                    for p in range(planes)
                ],
                1,
            )
        )
    return pieces


def exchange(piece):
    return lax.all_to_all(piece, "ga", split_axis=0, concat_axis=0, tiled=True)


def line_action(vloc, parts):
    side = NGRID * NGRID
    points = side // parts
    group = min(8, points)
    groups = points // group
    line_table = line_rotation(group)
    start = lax.axis_index("ga") * points
    own = lax.dynamic_slice_in_dim(vloc[0].reshape(NGRID, side), start, points, axis=1)
    own = own.reshape(NGRID, groups, group).transpose(1, 0, 2) * (1.0 / (NGRID * side))
    own = jnp.broadcast_to(own[..., None], (groups, NGRID, group, 2)).reshape(groups, -1, 1)
    scaled = (own * line_table.astype(jnp.float32)).astype(jnp.bfloat16)
    return jnp.einsum(
        "ea,gec->gac", line_table, scaled, preferred_element_type=jnp.float32
    ).astype(jnp.bfloat16)


def line_step(action, lines):
    parts, planes, rows, chunk = lines.shape
    groups = action.shape[0]
    lines = lines.reshape(parts * planes, groups, rows // groups, chunk)
    lines = lines.transpose(1, 0, 2, 3).reshape(groups, -1, chunk)
    lines = jnp.einsum(
        "gac,gcb->gab", action, lines, preferred_element_type=jnp.float32
    ).astype(jnp.bfloat16)
    lines = lines.reshape(groups, parts * planes, rows // groups, chunk).transpose(1, 0, 2, 3)
    return lines.reshape(parts, planes, rows, chunk)


def plane_back(backs, plane_table):
    side = NGRID * NGRID
    reals, imags = [], []
    for back in backs:
        chunk = back.shape[3]
        whole = [
            jnp.einsum(
                "qb,qk->bk",
                back[:, p].reshape(2 * side, chunk),
                plane_table,
                preferred_element_type=jnp.float32,
            )
            for p in range(back.shape[1])
        ]
        reals.append(jnp.concatenate([w[:, :side] for w in whole], 1))
        imags.append(jnp.concatenate([w[:, side:] for w in whole], 1))
    return jnp.concatenate(reals, 0), jnp.concatenate(imags, 0)


def waves(oxygens, gvectors, profile):
    local_g = profile.shape[0]
    side = NGRID * NGRID
    if local_g % side:
        phases = jnp.einsum("ai,ag->ig", oxygens, gvectors, precision=highest)
        return profile * jnp.cos(phases), profile * jnp.sin(phases)
    spots = oxygens.T
    flat = spots[:, 1:2] * gvectors[1:2, :side] + spots[:, 2:3] * gvectors[2:3, :side]
    flat_cos, flat_sin = jnp.cos(flat), jnp.sin(flat)
    along = spots[:, 0:1] * gvectors[0:1, ::side]
    along_cos, along_sin = jnp.cos(along), jnp.sin(along)
    cosines, sines = [], []
    for p in range(local_g // side):
        c, s = along_cos[:, p : p + 1], along_sin[:, p : p + 1]
        cosines.append(c * flat_cos - s * flat_sin)
        sines.append(s * flat_cos + c * flat_sin)
    return profile * jnp.concatenate(cosines, 1), profile * jnp.concatenate(sines, 1)


def per_device(positions, weights, psi, vloc):
    near_forces = field_forces(positions)
    weight_float = weights.astype(jnp.float32)
    mixing = weight_float / jnp.sum(weight_float, axis=1, keepdims=True)
    centres = jnp.einsum("cj,jan->can", mixing, positions, precision=highest)
    parts = lax.axis_size("ga")
    near_oxygen = centres[0][:, 0::3]
    own_waters = near_oxygen.shape[1]
    everyone = lax.dynamic_update_slice(
        jnp.zeros((3, own_waters * parts), jnp.float32),
        near_oxygen,
        (0, lax.axis_index("ga") * own_waters),
    )
    oxygens = lax.psum(everyone, "ga")
    side = NGRID * NGRID
    whole_planes = psi.shape[3] % side == 0 and side % parts == 0
    if whole_planes:
        plane_table = plane_rotation()
        pieces = plane_out(psi, parts, plane_table, (oxygens[0, 0] * 0.0).astype(jnp.int32))
        lines = [exchange(piece) for piece in pieces]
        action = line_action(vloc, parts)
    bands = psi.shape[1]
    local_g = psi.shape[3]
    flat_index = lax.axis_index("ga") * local_g + jnp.arange(local_g, dtype=jnp.int32)
    gvectors = jnp.stack(
        [
            frequency(flat_index // (NGRID * NGRID), NGRID),
            frequency(flat_index // NGRID % NGRID, NGRID),
            frequency(flat_index % NGRID, NGRID),
        ]
    )
    square = jnp.sum(gvectors * gvectors, axis=0)
    profile = jnp.exp(-0.5 * width_square * square)
    kinetic = 0.5 * square
    wave_cos, wave_sin = waves(oxygens, gvectors, profile)
    table = jnp.concatenate(
        [jnp.concatenate([wave_cos, -wave_sin], 1), jnp.concatenate([wave_sin, wave_cos], 1)], 0
    ).astype(jnp.bfloat16)
    wavefunc = psi[0].reshape(bands, 2 * local_g)
    partial_proj = (inner(table, wavefunc) * (1.0 / GVECS)).reshape(2, WATERS, bands)
    share = lax.psum_scatter(partial_proj, "ga", scatter_dimension=1, tiled=True).astype(
        jnp.bfloat16
    )
    table_blocks = table.reshape(2 * WATERS, 2 * local_g)
    copies = jnp.broadcast_to(share[None], (parts,) + share.shape)
    if whole_planes:
        lines[-1], copies = lax.optimization_barrier((lines[-1], copies))
    all_proj = lax.all_to_all(copies, "ga", split_axis=0, concat_axis=0, tiled=True)
    if whole_planes:
        moved = [line_step(action, line) for line in lines]
        moved[0], all_proj = lax.optimization_barrier((moved[0], all_proj))
        backs = [exchange(piece) for piece in moved]
    all_proj = all_proj.transpose(1, 0, 2, 3).reshape(2 * WATERS, bands)
    nonlocal_term = jnp.einsum(
        "ib,ig->bg", all_proj, table_blocks, preferred_element_type=jnp.float32
    )
    crossed = jnp.dot(all_proj, wavefunc, preferred_element_type=jnp.float32)
    weighted_re = crossed[:WATERS, :local_g] + crossed[WATERS:, local_g:]
    weighted_im = crossed[:WATERS, local_g:] - crossed[WATERS:, :local_g]
    mixed_wave = wave_cos * weighted_im + wave_sin * weighted_re
    force_part = (
        2.0
        * occupation
        * nonlocal_strength
        / GVECS
        * jnp.einsum("ag,ig->ai", gvectors, mixed_wave, precision=highest)
    )
    force_rows = force_part.reshape(3, parts, own_waters).transpose(1, 0, 2)
    force_rows = force_rows.reshape(parts, 1, 3 * own_waters)
    force_rows = jnp.pad(force_rows, ((0, 0), (0, 0), (0, bands - 3 * own_waters)))
    wave_float = psi[0].astype(jnp.float32)
    if whole_planes:
        potential = plane_back(backs, plane_table)
    else:
        potential = grid_sum(psi, vloc, parts)
    hamil_re = (
        kinetic * wave_float[:, 0]
        + potential[0]
        + nonlocal_strength * nonlocal_term[:, :local_g]
    )
    hamil_im = (
        kinetic * wave_float[:, 1]
        + potential[1]
        + nonlocal_strength * nonlocal_term[:, local_g:]
    )
    trial_re = (wave_float[:, 0] - step_size * hamil_re).astype(jnp.bfloat16)
    trial_im = (wave_float[:, 1] - step_size * hamil_im).astype(jnp.bfloat16)
    row = lax.broadcasted_iota(jnp.int32, (bands, bands), 0)
    column = lax.broadcasted_iota(jnp.int32, (bands, bands), 1)
    even = inner(trial_re, trial_re) + inner(trial_im, trial_im)
    odd = inner(trial_im, trial_re) - inner(trial_re, trial_im)
    packed = jnp.where(row <= column, even, odd) * (1.0 / GVECS)
    shares = lax.all_to_all(
        jnp.concatenate([packed.reshape(parts, bands // parts, bands), force_rows], 1),
        "ga",
        split_axis=0,
        concat_axis=0,
        tiled=True,
    )
    sums = jnp.sum(shares, axis=0)
    oxygen_force = sums[-1, : 3 * own_waters].reshape(3, own_waters)
    hydrogen_zero = jnp.zeros_like(oxygen_force)
    dft_forces = [jnp.stack([oxygen_force, hydrogen_zero, hydrogen_zero], axis=2).reshape(3, -1)]
    own_rows = lax.broadcasted_iota(jnp.int32, (bands // parts, bands), 0) + lax.axis_index(
        "ga"
    ) * (bands // parts)
    own_columns = lax.broadcasted_iota(jnp.int32, (bands // parts, bands), 1)
    mixed_rows = jnp.where(own_rows == own_columns, 1.5, 0.0) - 0.5 * sums[:-1]
    mixed = lax.all_gather(mixed_rows.astype(jnp.bfloat16), "ga", axis=0, tiled=True)
    turned = mixed.T
    mix_re = jnp.where(row <= column, mixed, turned)
    mix_im = jnp.where(row > column, mixed, jnp.where(row < column, -turned, jnp.zeros_like(turned)))
    both = jnp.concatenate([trial_re, trial_im], 0)
    new_re = jnp.dot(
        jnp.concatenate([mix_re, -mix_im], 1), both, preferred_element_type=jnp.float32
    ).astype(jnp.bfloat16)
    new_im = jnp.dot(
        jnp.concatenate([mix_im, mix_re], 1), both, preferred_element_type=jnp.float32
    ).astype(jnp.bfloat16)
    new_waves = [jnp.stack([new_re, new_im], 1)]
    contracted_force = jnp.einsum("cj,can->jan", mixing, jnp.stack(dft_forces), precision=highest)
    bead_forces = near_forces + BEADS / CBEADS * contracted_force
    return (jnp.stack(new_waves), bead_forces)


def product(left_mat, right_mat):
    return jnp.dot(left_mat, right_mat, preferred_element_type=jnp.float32)


def trig_tables():
    small = np.arange(NGRID)
    angle = small[:, None] * small[None, :] % NGRID * (2.0 * np.pi / NGRID)
    cosines, sines = np.cos(angle), np.sin(angle)
    rows = [np.repeat(cosines, NGRID, 1), np.repeat(sines, NGRID, 1)]
    rows += [np.tile(cosines, (1, NGRID)), np.tile(sines, (1, NGRID))]
    return jnp.asarray(np.stack(rows), jnp.float32)


def cross_tables(parts, planes, share):
    spot = (np.arange(parts)[None, :] * planes + np.arange(planes)[:, None]).reshape(-1)
    angle = spot[:, None] * spot[None, :] % NGRID * (2.0 * np.pi / NGRID)
    same = np.eye(share)
    pair = np.stack([np.kron(np.cos(angle), same), np.kron(np.sin(angle), same)])
    return jnp.asarray(pair.astype(np.float32), jnp.bfloat16)


def step_kernel(
    sizes,
    psi_hbm,
    positions,
    weights,
    trig,
    cross,
    vloc,
    trial_hbm,
    mixed,
    force_out,
    raw,
    psi,
    own_centres,
    all_centres,
    grid,
    near,
    all_waves,
    table_cos,
    table_sin,
    wave_cos,
    wave_sin,
    plane_cos,
    plane_sin,
    potential,
    got,
    whole,
    middle,
    giving,
    back,
    base,
    trial,
    partial,
    landing,
    gathered,
    turned,
    margin,
    landing_two,
    gathered_two,
    force_sum,
    force_land,
    grid_rows,
    local_sem,
    wave_sems,
    out_sems,
    back_sems,
    force_sems,
    sum_sems,
    share_sems,
):
    parts, bands, local_g = sizes
    side = NGRID * NGRID
    planes = local_g // side
    share = bands // (parts * CHUNKS)
    block = parts * share
    steps = parts.bit_length() - 1
    tile = 256
    atoms = positions.shape[2]
    waters = atoms // 3
    me = lax.axis_index("ga")

    def other(turn):
        total = 0
        for bit in range(steps):
            size = 1 << bit
            total = total + (me // size + turn // size) % 2 * size
        return total

    def remote(source, target, sems, peer):
        return pltpu.make_async_remote_copy(
            src_ref=source,
            dst_ref=target,
            send_sem=sems[0],
            recv_sem=sems[1],
            device_id={"ga": peer},
            device_id_type=pl.DeviceIdType.MESH,
        )

    def each_peer(act):
        def body(turn, carry):
            act(turn)
            return carry

        lax.fori_loop(1, parts, body, 0)

    def pair(sems, *spot):
        return sems.at[(0,) + spot], sems.at[(1,) + spot]

    def wave_copy(turn):
        rows = own_centres.shape[0]
        spot = pl.ds(pl.multiple_of(me * rows, rows), rows)
        return remote(own_centres, all_centres.at[spot], pair(wave_sems, turn), other(turn))

    def out_copy(chunk, turn):
        peer = other(turn)
        source = pl.ds(pl.multiple_of(chunk * block + peer * share, share), share)
        target = pl.ds(pl.multiple_of(me * share, share), share)
        return remote(
            psi_hbm.at[source], got.at[chunk, target], pair(out_sems, chunk, turn), peer
        )

    def back_copy(chunk, turn):
        peer = other(turn)
        source = pl.ds(pl.multiple_of(peer * share, share), share)
        target = pl.ds(pl.multiple_of(chunk * block + me * share, share), share)
        return remote(
            giving.at[chunk, source], back.at[target], pair(back_sems, chunk, turn), peer
        )

    def force_copy(turn):
        peer = other(turn)
        source = pl.ds(pl.multiple_of(peer * waters, waters), waters)
        return remote(
            force_sum.at[source], force_land.at[me], pair(force_sems, turn), peer
        )

    local_psi = pltpu.make_async_copy(psi_hbm, raw, local_sem.at[0])
    local_psi.start()
    barrier = pltpu.get_barrier_semaphore()

    def greet(turn):
        pl.semaphore_signal(
            barrier, inc=1, device_id={"ga": other(turn)}, device_id_type=pl.DeviceIdType.MESH
        )

    each_peer(greet)
    beads = positions.shape[0]

    def exact(left_mat, right_mat, right_axis=0):
        return lax.dot_general(
            left_mat,
            right_mat,
            (((1,), (right_axis,)), ((), ())),
            precision=highest,
            preferred_element_type=jnp.float32,
        )

    def spots(shape):
        return lax.broadcasted_iota(jnp.int32, shape, 0), lax.broadcasted_iota(jnp.int32, shape, 1)

    weight_row = weights[...].astype(jnp.float32)
    mixing = weight_row / jnp.sum(weight_row, axis=1, keepdims=True)
    own_row, own_atom = spots((waters, atoms))
    pick_row, pick_atom = spots((own_centres.shape[1], atoms))
    oxygen_pick = jnp.where(pick_atom == 3 * pick_row, 1.0, 0.0)
    centre_row = lax.broadcasted_iota(jnp.int32, own_centres.shape, 0)
    near_centres = jnp.zeros(own_centres.shape, jnp.float32)
    for axis in range(3):
        centre = exact(jnp.broadcast_to(mixing, (8, beads)), positions[:, axis, :])
        near_centres += jnp.where(centre_row == axis, exact(centre, oxygen_pick, 1), 0.0)
    own_centres[...] = near_centres
    all_centres[pl.ds(pl.multiple_of(me * 8, 8), 8), :] = near_centres
    own_spot = pl.ds(pl.multiple_of(me * waters, waters), waters)
    pl.semaphore_wait(barrier, parts - 1)

    units = [(chunk, far) for chunk in range(CHUNKS) for far in range(parts // 2)]
    queue = list(units)

    def issue(count):
        for _ in range(count):
            if queue:
                chunk, far = queue.pop(0)
                out_copy(chunk, parts // 2 + far).start()
                if far > 0:
                    out_copy(chunk, far).start()

    each_peer(lambda turn: wave_copy(turn).start())
    issue(5)

    flat_index = me * local_g + lax.broadcasted_iota(jnp.int32, (1, local_g), 1)
    gvectors = [
        frequency(flat_index // side, NGRID),
        frequency(flat_index // NGRID % NGRID, NGRID),
        frequency(flat_index % NGRID, NGRID),
    ]
    square = gvectors[0] * gvectors[0] + gvectors[1] * gvectors[1] + gvectors[2] * gvectors[2]
    grid[0:1, :] = jnp.exp(-0.5 * width_square * square)
    grid[1:2, :] = 0.5 * square
    grid_rows[...] = jnp.zeros_like(grid_rows)
    for axis in range(3):
        grid_rows[axis : axis + 1, :] = gvectors[axis]

    def plane_rows(row, carry):
        spot = pl.ds(pl.multiple_of(row * NGRID, NGRID), NGRID)
        across_cos, across_sin = trig[0, pl.ds(row, 1), :], trig[1, pl.ds(row, 1), :]
        plane_cos[spot, :] = (across_cos * trig[2] - across_sin * trig[3]).astype(jnp.bfloat16)
        plane_sin[spot, :] = (across_sin * trig[2] + across_cos * trig[3]).astype(jnp.bfloat16)
        return carry

    lax.fori_loop(0, NGRID, plane_rows, 0)

    def potential_rows(spot, carry):
        plane = spot % planes * parts + spot // planes
        rows = pl.ds(pl.multiple_of(plane * share, share), share)
        value = vloc[:, pl.ds(pl.multiple_of(spot * side, side), side)] * (1.0 / NGRID**3)
        potential[rows, :] = jnp.broadcast_to(value, (share, side))
        return carry

    lax.fori_loop(0, NGRID, potential_rows, 0)

    strip = 16

    def unpack_rows(step, carry):
        rows = pl.ds(pl.multiple_of(step * strip, strip), strip)
        psi[rows, :local_g] = raw[rows, 0, :]
        psi[rows, local_g:] = raw[rows, 1, :]
        return carry

    local_psi.wait()
    lax.fori_loop(0, bands // strip, unpack_rows, 0)
    each_peer(lambda turn: wave_copy(turn).wait_recv())
    lined = all_centres[...].T
    _, wave_lane = spots((waters, all_waves.shape[1]))
    spokes = frequency(wave_lane % NGRID, NGRID)
    for source in range(parts):
        angles = jnp.zeros(spokes.shape, jnp.float32)
        for axis in range(3):
            column = lined[:waters, 8 * source + axis : 8 * source + axis + 1]
            angles += column * jnp.where(wave_lane // (2 * NGRID) == axis, spokes, 0.0)
        all_waves[source * waters : (source + 1) * waters, :] = angles

    def wave_rows(source, carry):
        rows = pl.ds(pl.multiple_of(source * waters, waters), waters)
        angles = all_waves[rows, :]
        all_waves[rows, :] = jnp.where(
            wave_lane // NGRID % 2 == 0, jnp.cos(angles), jnp.sin(angles)
        )
        return carry

    lax.fori_loop(0, parts, wave_rows, 0)
    lane = lax.broadcasted_iota(jnp.int32, all_waves.shape, 1)
    line = lax.broadcasted_iota(jnp.int32, (all_waves.shape[1], tile), 0)
    place = lax.broadcasted_iota(jnp.int32, (all_waves.shape[1], tile), 1)

    def pick(first, spot):
        return jnp.where(line == first * NGRID + spot, 1.0, 0.0)

    def spread(first, spot):
        return lax.dot_general(
            all_waves[...],
            pick(first, spot),
            (((1,), (0,)), ((), ())),
            precision=highest,
            preferred_element_type=jnp.float32,
        )

    def table_tile(step, carry):
        first = step * tile
        flat = first + place
        rise, along = flat // NGRID, flat % NGRID
        rise_cos, rise_sin = spread(2, rise), spread(3, rise)
        long_cos, long_sin = spread(4, along), spread(5, along)
        flat_cos = rise_cos * long_cos - rise_sin * long_sin
        flat_sin = rise_sin * long_cos + rise_cos * long_sin
        for plane in range(planes):
            level = me * planes + plane
            c = jnp.sum(jnp.where(lane == level, all_waves[...], 0.0), axis=1, keepdims=True)
            s = jnp.sum(
                jnp.where(lane == level + NGRID, all_waves[...], 0.0), axis=1, keepdims=True
            )
            spot = pl.ds(pl.multiple_of(plane * side + first, tile), tile)
            profile = grid[0:1, spot]
            full_cos = profile * (c * flat_cos - s * flat_sin)
            full_sin = profile * (s * flat_cos + c * flat_sin)
            wave_cos[:, spot] = full_cos
            wave_sin[:, spot] = full_sin
            table_cos[:, spot] = full_cos.astype(jnp.bfloat16)
            table_sin[:, spot] = full_sin.astype(jnp.bfloat16)
        return carry

    lax.fori_loop(0, side // tile, table_tile, 0)
    partial[...] = jnp.zeros_like(partial)

    def project(step, carry):
        spot = pl.ds(pl.multiple_of(step * tile, tile), tile)
        far = pl.ds(pl.multiple_of(local_g + step * tile, tile), tile)
        real, imag = psi[:, spot], psi[:, far]
        cosines, sines = table_cos[:, spot], table_sin[:, spot]
        partial[:WATERS, :] += inner(cosines, real) - inner(sines, imag)
        partial[WATERS:, :] += inner(sines, real) + inner(cosines, imag)
        return carry

    lax.fori_loop(0, local_g // tile, project, 0)

    straight = list(range(steps))
    crossed = [0] + straight[2:] + [1]
    narrow = bands // 2
    single = [(0, straight, pl.ds(0, bands))]
    double = [(1, straight, pl.ds(0, narrow)), (2, crossed, pl.ds(narrow, narrow))]

    def own_start(order, upto, rows):
        start = 0
        for place, bit in enumerate(order[:upto]):
            start = start + me // (1 << bit) % 2 * (rows >> (place + 1))
        return start

    def partner(bit):
        size = 1 << bit
        mine = me // size % 2
        return mine, me + (1 - 2 * mine) * size

    def sum_step(values, land, halves, place, between):
        rows = values.shape[0]
        half = rows >> (place + 1)
        spot = pl.ds(rows - 2 * half, half)
        pending = []
        for which, order, columns in halves:
            mine, peer = partner(order[place])
            start = own_start(order, place, rows)
            away = pl.ds(pl.multiple_of(start + (1 - mine) * half, half), half)
            keep = pl.ds(pl.multiple_of(start + mine * half, half), half)
            copy = remote(
                values.at[away, columns],
                land.at[spot, columns],
                pair(sum_sems, which, place),
                peer,
            )
            copy.start()
            pending.append((copy, keep, columns))
        between()
        for copy, keep, columns in pending:
            copy.wait()
            values[keep, columns] += land[spot, columns]

    def share_step(values, halves, place, between):
        rows = values.shape[0]
        count = rows >> (place + 1)
        pending = []
        for which, order, columns in halves:
            _, peer = partner(order[place])
            spot = pl.ds(pl.multiple_of(own_start(order, place + 1, rows), count), count)
            copy = remote(
                values.at[spot, columns],
                values.at[spot, columns],
                pair(share_sems, which, place),
                peer,
            )
            copy.start()
            pending.append(copy)
        between()
        for copy in pending:
            copy.wait()

    for bit in range(steps):
        sum_step(partial, landing, single, bit, lambda: issue(1))
    own_rows = partial.shape[0] // parts
    own = pl.ds(pl.multiple_of(own_start(straight, steps, partial.shape[0]), own_rows), own_rows)
    gathered[own, :] = (partial[own, :] * (1.0 / GVECS)).astype(jnp.bfloat16)
    for bit in reversed(range(steps)):
        share_step(gathered, single, bit, lambda: issue(1))
    issue(len(units))

    for first in range(0, gathered.shape[0], tile):
        for second in range(0, bands, tile):
            part = gathered[first : first + tile, second : second + tile].astype(jnp.float32)
            turned[second : second + tile, first : first + tile] = part.T.astype(jnp.bfloat16)

    def transform(chunk):
        mine = pl.ds(pl.multiple_of(me * share, share), share)
        own_bands = pl.ds(pl.multiple_of(chunk * block + me * share, share), share)
        whole[mine, :] = psi[own_bands, :]

        def unpack_peer(turn):
            out_copy(chunk, turn).wait_recv()
            rows = pl.ds(pl.multiple_of(other(turn) * share, share), share)
            whole[rows, :local_g] = got[chunk, rows, 0, :]
            whole[rows, local_g:] = got[chunk, rows, 1, :]

        each_peer(unpack_peer)
        columns = side // tile

        def forward(step, carry):
            plane, column = step // columns, step % columns
            spot = pl.ds(pl.multiple_of(column * tile, tile), tile)
            rows = pl.ds(pl.multiple_of(plane * block, block), block)
            real = whole[:, pl.ds(pl.multiple_of(plane * side, side), side)]
            imag = whole[:, pl.ds(pl.multiple_of(local_g + plane * side, side), side)]
            cosines, sines = plane_cos[:, spot], plane_sin[:, spot]
            middle[0, rows, spot] = (product(real, cosines) - product(imag, sines)).astype(
                jnp.bfloat16
            )
            middle[1, rows, spot] = (product(real, sines) + product(imag, cosines)).astype(
                jnp.bfloat16
            )
            return carry

        lax.fori_loop(0, planes * columns, forward, 0)

        def lines(column, carry):
            spot = pl.ds(pl.multiple_of(column * tile, tile), tile)
            real, imag = middle[0, :, spot], middle[1, :, spot]
            value = potential[:, spot]
            cosines, sines = cross[0], cross[1]
            upper = (product(cosines, real) - product(sines, imag)) * value
            lower = (product(sines, real) + product(cosines, imag)) * value
            upper, lower = upper.astype(jnp.bfloat16), lower.astype(jnp.bfloat16)
            middle[0, :, spot] = (product(cosines, upper) + product(sines, lower)).astype(
                jnp.bfloat16
            )
            middle[1, :, spot] = (product(cosines, lower) - product(sines, upper)).astype(
                jnp.bfloat16
            )
            return carry

        lax.fori_loop(0, columns, lines, 0)

        def backward(step, carry):
            plane, column = step // columns, step % columns
            spot = pl.ds(pl.multiple_of(column * tile, tile), tile)
            rows = pl.ds(pl.multiple_of(plane * block, block), block)
            real, imag = middle[0, rows, :], middle[1, rows, :]
            cosines, sines = plane_cos[:, spot], plane_sin[:, spot]
            upper = pl.ds(pl.multiple_of(plane * side + column * tile, tile), tile)
            lower = pl.ds(pl.multiple_of(local_g + plane * side + column * tile, tile), tile)
            giving[chunk, :, upper] = (product(real, cosines) + product(imag, sines)).astype(
                jnp.bfloat16
            )
            giving[chunk, :, lower] = (product(imag, cosines) - product(real, sines)).astype(
                jnp.bfloat16
            )
            return carry

        lax.fori_loop(0, planes * columns, backward, 0)
        back[own_bands, :] = giving[chunk, mine, :]
        for far in range(parts // 2):
            back_copy(chunk, parts // 2 + far).start()
            if far > 0:
                back_copy(chunk, far).start()

    def near_forces():
        here, there = spots((atoms, atoms))
        same = jnp.where(here == there, 1.0, 0.0)
        offset_pick = same - jnp.where(here == there - there % 3, 1.0, 0.0)
        pull_pick = same - jnp.where(there == here - here % 3, 1.0, 0.0)
        bead, beside = spots((beads, beads))
        spring = 2.0 * jnp.where(bead == beside, 1.0, 0.0)
        spring -= jnp.where((bead + 1) % beads == beside, 1.0, 0.0)
        spring -= jnp.where((beside + 1) % beads == bead, 1.0, 0.0)
        offsets = [exact(positions[:, axis, :], offset_pick) for axis in range(3)]
        squares = offsets[0] * offsets[0] + offsets[1] * offsets[1] + offsets[2] * offsets[2]
        hydrogen = lax.broadcasted_iota(jnp.int32, squares.shape, 1) % 3 > 0
        length = jnp.sqrt(jnp.where(hydrogen, squares, 1.0))
        for axis in range(3):
            pull = -bond_stiff * (length - bond_rest) * offsets[axis] / length
            pull = jnp.where(hydrogen, pull, 0.0)
            near[axis] = exact(pull, pull_pick) - spring_stiff * exact(
                spring, positions[:, axis, :]
            )

    transform(0)

    force_sum[...] = jnp.zeros_like(force_sum)

    def local_part(step, carry):
        spot = pl.ds(pl.multiple_of(step * tile, tile), tile)
        far = pl.ds(pl.multiple_of(local_g + step * tile, tile), tile)
        kinetic = 1.0 - step_size * grid[1:2, spot]
        real, imag = psi[:, spot], psi[:, far]
        cosines, sines = table_cos[:, spot], table_sin[:, spot]
        turned_re, turned_im = turned[:, :WATERS], turned[:, WATERS:]
        strength = step_size * nonlocal_strength
        base[:, spot] = kinetic * real.astype(jnp.float32) - strength * (
            product(turned_re, cosines) + product(turned_im, sines)
        )
        base[:, far] = kinetic * imag.astype(jnp.float32) - strength * (
            product(turned_im, cosines) - product(turned_re, sines)
        )
        proj_re, proj_im = gathered[:WATERS, :], gathered[WATERS:, :]
        weighted_re = product(proj_re, real) + product(proj_im, imag)
        weighted_im = product(proj_re, imag) - product(proj_im, real)
        mixed = wave_cos[:, spot] * weighted_im + wave_sin[:, spot] * weighted_re
        force_sum[...] += lax.dot_general(
            mixed,
            grid_rows[:, spot],
            (((1,), (1,)), ((), ())),
            precision=highest,
            preferred_element_type=jnp.float32,
        )
        return carry

    lax.fori_loop(0, local_g // tile, local_part, 0)
    force_land[me] = force_sum[own_spot, :]
    each_peer(lambda turn: force_copy(turn).start())

    near_forces()
    transform(1)
    each_peer(lambda turn: force_copy(turn).wait_recv())

    def add_force(source, carry):
        return carry + force_land[source]

    strength = 2.0 * occupation * nonlocal_strength / GVECS
    total = strength * lax.fori_loop(
        0, parts, add_force, jnp.zeros(force_land.shape[1:], jnp.float32)
    )
    bead_row, bead_column = spots((beads, beads))
    mixing_column = jnp.sum(
        jnp.where(bead_row == bead_column, jnp.broadcast_to(mixing, (beads, beads)), 0.0),
        axis=1,
        keepdims=True,
    )
    for axis in range(3):
        placed = jnp.where(own_atom == 3 * own_row, total[:, axis : axis + 1], 0.0)
        placed = jnp.sum(placed, axis=0, keepdims=True)
        force_out[:, axis, :] = near[axis] + BEADS / CBEADS * (mixing_column * placed)

    def finish(chunk):
        def rows_of(turn, carry):
            @pl.when(turn > 0)
            def _():
                back_copy(chunk, turn).wait_recv()

            rows = pl.ds(
                pl.multiple_of(chunk * block + other(turn) * share, share), share
            )
            value = base[rows, :] - step_size * back[rows, :].astype(jnp.float32)
            value = value.astype(jnp.bfloat16)
            trial[0, rows, :] = value[:, :local_g]
            trial[1, rows, :] = value[:, local_g:]
            return carry

        lax.fori_loop(0, parts, rows_of, 0)

    corner_row = lax.broadcasted_iota(jnp.int32, (block, block), 0)
    corner_column = lax.broadcasted_iota(jnp.int32, (block, block), 1)

    def overlap(later, earlier):
        wide = 2 * tile
        rows = pl.ds(later * block, block)
        columns = pl.ds(earlier * block, block)
        margin[rows, columns] = jnp.zeros((block, block), jnp.float32)
        margin[columns, rows] = jnp.zeros((block, block), jnp.float32)

        def add(step, carry):
            spot = pl.ds(pl.multiple_of(step * wide, wide), wide)
            stacked = trial[:, rows, spot].reshape(2 * block, wide)
            on_real = inner(stacked, trial[0, columns, spot])
            on_imag = inner(stacked, trial[1, columns, spot])
            even = on_real[:block] + on_imag[block:]
            odd = on_real[block:] - on_imag[:block]
            if later == earlier:
                margin[rows, columns] += jnp.where(corner_row <= corner_column, even, odd)
            else:
                margin[columns, rows] += even
                margin[rows, columns] += odd
            return carry

        lax.fori_loop(0, local_g // wide, add, 0)

    def trial_copy(chunk):
        rows = pl.ds(chunk * block, block)
        return pltpu.make_async_copy(
            trial.at[:, rows], trial_hbm.at[:, rows], local_sem.at[1 + chunk]
        )

    for chunk in range(CHUNKS):
        finish(chunk)
        trial_copy(chunk).start()
        for earlier in range(chunk + 1):
            overlap(chunk, earlier)

    for place in range(steps):
        sum_step(margin, landing_two, double, place, lambda: None)
    own_rows = bands // parts
    for _, order, columns in double:
        start = own_start(order, steps, bands)
        own = pl.ds(pl.multiple_of(start, own_rows), own_rows)
        row, column = spots((own_rows, narrow))
        same = start + row == columns.start + column
        mixed_rows = jnp.where(same, 1.5, 0.0) - (0.5 / GVECS) * margin[own, columns]
        gathered_two[own, columns] = mixed_rows.astype(jnp.bfloat16)
    for place in reversed(range(steps)):
        share_step(gathered_two, double, place, lambda: None)

    for chunk in range(CHUNKS):
        rows = pl.ds(chunk * block, block)
        there = gathered_two[rows, rows].astype(jnp.float32)
        flipped = there.T
        mix_re = jnp.where(corner_row <= corner_column, there, flipped)
        mix_im = jnp.where(
            corner_row > corner_column,
            there,
            jnp.where(corner_row < corner_column, -flipped, jnp.zeros_like(there)),
        )
        mixed[chunk, :block, rows] = mix_re.astype(jnp.bfloat16)
        mixed[chunk, block:, rows] = mix_im.astype(jnp.bfloat16)
        for earlier in range(chunk):
            columns = pl.ds(earlier * block, block)
            even, odd = gathered_two[columns, rows], gathered_two[rows, columns]
            mixed[chunk, :block, columns] = even
            mixed[chunk, block:, columns] = odd
            mixed[earlier, :block, rows] = even.astype(jnp.float32).T.astype(jnp.bfloat16)
            mixed[earlier, block:, rows] = (-odd.astype(jnp.float32).T).astype(jnp.bfloat16)

    for chunk in range(CHUNKS):
        trial_copy(chunk).wait()
        each_peer(lambda turn: out_copy(chunk, turn).wait_send())
        each_peer(lambda turn: back_copy(chunk, turn).wait_send())
    each_peer(lambda turn: wave_copy(turn).wait_send())
    each_peer(lambda turn: force_copy(turn).wait_send())


def rotate_kernel(mixed_hbm, trial_hbm, out_hbm, mixed, trial, out, sems):
    block = mixed.shape[1] // 2
    tiles, tile = trial.shape[0], trial.shape[3]
    mixed_copy = pltpu.make_async_copy(mixed_hbm, mixed, sems.at[tiles])

    def trial_copy(step):
        spot = pl.ds(pl.multiple_of(step * tile, tile), tile)
        return pltpu.make_async_copy(trial_hbm.at[:, :, spot], trial.at[step], sems.at[step])

    def out_copy(chunk):
        rows = pl.ds(chunk * block, block)
        return pltpu.make_async_copy(
            out.at[rows], out_hbm.at[rows], sems.at[tiles + 1 + chunk]
        )

    trial_copy(0).start()
    mixed_copy.start()
    for step in range(1, tiles):
        trial_copy(step).start()
    mixed_copy.wait()
    for chunk in range(CHUNKS):
        rows = pl.ds(chunk * block, block)

        def turn_columns(step, carry):
            if chunk == 0:
                trial_copy(step).wait()
            spot = pl.ds(pl.multiple_of(step * tile, tile), tile)
            on_real = product(mixed[chunk], trial[step, 0])
            on_imag = product(mixed[chunk], trial[step, 1])
            real = on_real[:block] - on_imag[block:]
            imag = on_real[block:] + on_imag[:block]
            out[rows, 0, spot] = real.astype(jnp.bfloat16)
            out[rows, 1, spot] = imag.astype(jnp.bfloat16)
            return carry

        lax.fori_loop(0, tiles, turn_columns, 0)
        out_copy(chunk).start()
    for chunk in range(CHUNKS):
        out_copy(chunk).wait()


def rotate(mixed, trial):
    bands, local_g = trial.shape[1:]
    tile = 256
    tiles = local_g // tile
    anywhere = pl.BlockSpec(memory_space=pl.ANY)
    return pl.pallas_call(
        rotate_kernel,
        out_shape=jax.ShapeDtypeStruct((bands, 2, local_g), jnp.bfloat16),
        in_specs=[anywhere, anywhere],
        out_specs=anywhere,
        scratch_shapes=[
            pltpu.VMEM(mixed.shape, mixed.dtype),
            pltpu.VMEM((tiles, 2, bands, tile), trial.dtype),
            pltpu.VMEM((bands, 2, local_g), trial.dtype),
            pltpu.SemaphoreType.DMA((tiles + 1 + CHUNKS,)),
        ],
        compiler_params=pltpu.CompilerParams(vmem_limit_bytes=67043328),
    )(mixed, trial)


def fused_device(positions, weights, psi, vloc):
    parts = lax.axis_size("ga")
    bands, local_g = psi.shape[1], psi.shape[3]
    side = NGRID * NGRID
    planes = local_g // side
    share = bands // (parts * CHUNKS)
    block = parts * share
    waters = positions.shape[2] // 3
    vmem = pl.BlockSpec(memory_space=pltpu.VMEM)
    anywhere = pl.BlockSpec(memory_space=pl.ANY)
    steps = parts.bit_length() - 1
    f32, bf16 = jnp.float32, jnp.bfloat16
    dma = pltpu.SemaphoreType.DMA
    trial, mixed, force = pl.pallas_call(
        functools.partial(step_kernel, (parts, bands, local_g)),
        out_shape=(
            jax.ShapeDtypeStruct((2, bands, local_g), bf16),
            jax.ShapeDtypeStruct((CHUNKS, 2 * block, bands), bf16),
            jax.ShapeDtypeStruct(positions.shape, f32),
        ),
        in_specs=[anywhere, vmem, vmem, vmem, vmem, vmem],
        out_specs=(anywhere, vmem, vmem),
        scratch_shapes=[
            pltpu.VMEM((bands, 2, local_g), bf16),
            pltpu.VMEM((bands, 2 * local_g), bf16),
            pltpu.VMEM((8, 128), f32),
            pltpu.VMEM((parts * 8, 128), f32),
            pltpu.VMEM((8, local_g), f32),
            pltpu.VMEM((3,) + positions.shape[::2], f32),
            pltpu.VMEM((WATERS, 8 * NGRID), f32),
            pltpu.VMEM((WATERS, local_g), bf16),
            pltpu.VMEM((WATERS, local_g), bf16),
            pltpu.VMEM((WATERS, local_g), f32),
            pltpu.VMEM((WATERS, local_g), f32),
            pltpu.VMEM((side, side), bf16),
            pltpu.VMEM((side, side), bf16),
            pltpu.VMEM((planes * block, side), f32),
            pltpu.VMEM((CHUNKS, block, 2, local_g), bf16),
            pltpu.VMEM((block, 2 * local_g), bf16),
            pltpu.VMEM((2, planes * block, side), bf16),
            pltpu.VMEM((CHUNKS, block, 2 * local_g), bf16),
            pltpu.VMEM((bands, 2 * local_g), bf16),
            pltpu.VMEM((bands, 2 * local_g), f32),
            pltpu.VMEM((2, bands, local_g), bf16),
            pltpu.VMEM((2 * WATERS, bands), f32),
            pltpu.VMEM((2 * WATERS, bands), f32),
            pltpu.VMEM((2 * WATERS, bands), bf16),
            pltpu.VMEM((bands, 2 * WATERS), bf16),
            pltpu.VMEM((bands, bands), f32),
            pltpu.VMEM((bands, bands), f32),
            pltpu.VMEM((bands, bands), bf16),
            pltpu.VMEM((WATERS, 128), f32),
            pltpu.VMEM((parts, waters, 128), f32),
            pltpu.VMEM((128, local_g), f32),
            dma((1 + CHUNKS,)),
            dma((2, parts)),
            dma((2, CHUNKS, parts)),
            dma((2, CHUNKS, parts)),
            dma((2, parts)),
            dma((2, 3, steps)),
            dma((2, 3, steps)),
        ],
        compiler_params=pltpu.CompilerParams(
            collective_id=0, has_side_effects=True, vmem_limit_bytes=67043328
        ),
    )(
        psi[0],
        positions,
        weights,
        trig_tables(),
        cross_tables(parts, planes, share),
        vloc,
    )
    return (rotate(mixed, trial)[None], force)


def step_device(positions, weights, psi, vloc):
    parts = lax.axis_size("ga")
    bands, local_g = psi.shape[1], psi.shape[3]
    side = NGRID * NGRID
    fits = (
        local_g % side == 0
        and parts & (parts - 1) == 0
        and parts >= 4
        and bands % (parts * CHUNKS * 16) == 0
        and bands // CHUNKS % 256 == 0
        and bands * local_g <= 2**20
    )
    if fits:
        return fused_device(positions, weights, psi, vloc)
    return per_device(positions, weights, psi, vloc)


def solution(mesh):
    placed = (P("rep", None, "ga"), P(), P("rep", None, None, "ga"), P("rep", None))
    return jax.shard_map(
        step_device,
        mesh=mesh,
        in_specs=placed,
        out_specs=(P("rep", None, None, "ga"), P("rep", None, "ga")),
        check_vma=False,
    )
```
